128 devices in a mesh: section: 8 (over z_hi, y), dp: 16 (over z_lo, x, core).
Axes of the slice: x: 4, y: 4, z: 4 (z_hi: 2, z_lo: 2; z = z_hi * 2 + z_lo), core: 2. Of those that a mesh axis runs over, the one named last changes fastest.
Arguments:
- queries: bfloat16 [8, 32, 128, 4096], P('section', 'dp'), may hold values from -240 to 240, as said below
- image_tokens: bfloat16 [32, 192, 8192], P('dp', 'section'), may hold values from -6 to 6
- key_weight: bfloat16 [8, 8192, 512], P('section'), may hold values from -0.0625 to 0.0625
- value_weight: bfloat16 [8, 8192, 512], P('section'), may hold values from -0.0625 to 0.0625
- cotangent: bfloat16 [8, 32, 128, 4096], P('section', 'dp'), may hold values from -6 to 6
- tile_counts: int32 [32], P('dp'), may hold values from 1 to 4
- text_lengths: int32 [32], P('dp'), may hold values from 32 to 128, as said below
Outputs:
- query_gradient: bfloat16 [8, 32, 128, 4096], P('section', 'dp')
- image_grad: bfloat16 [32, 192, 8192], P('dp', 'section')
- key_weight_grad: bfloat16 [8, 8192, 512], P('section', 'dp')
- value_weight_grad: bfloat16 [8, 8192, 512], P('section', 'dp')
The draws below stay inside these ranges and needn't reach their ends.
Inputs may be any that keep to these rules, and one draw needn't show every extreme that they name: queries of one row share one scale. `text_lengths`: the live text tokens of a sample come first.
All inputs are finite; a program needn't handle non-finite values.
Results may differ from the reference program's by a relative error of at most 0.025.
The reference program's roundings to bfloat16 on the way count: a program that leaves them out, or rounds other values in their place, can miss the bound.
Values may be sent and summed in bfloat16 or wider, within the bound.
A program may use at most 192 MiB of HBM per device.

```python
import math
import jax
import jax.numpy as jnp
import numpy as np
from jax import lax

D = 8192
QUERY_HEADS = 32
KEY_VALUE_HEADS = 4
HEAD_SIZE = 128
MAX_TILES = 4
TEXT_LEN = 128
SAMP_DEV = 2
SAMPLES = 32
SECTIONS = 8
IMG = 192
HQD = 4096
KVD = 512
N_SECTION = 8
N_DP = 16


def draw_tile_counts(key, part):
    table = jnp.minimum(jnp.array(np.array([1, 1, 1, 1, 2, 2, 3, 4]), jnp.int32), MAX_TILES)
    picks = jax.random.randint(jax.random.fold_in(key, 11), (SAMPLES,), 0, 8)
    counts = table[picks]
    return counts.at[0].set(MAX_TILES).astype(jnp.int32)


def draw_text_lengths(key, part):
    lengths = jax.random.randint(jax.random.fold_in(key, 23), (SAMPLES,), TEXT_LEN // 4, TEXT_LEN + 1)
    return lengths.at[0].set(TEXT_LEN).astype(jnp.int32)


def draw_queries(key, part):
    shape_full = (SECTIONS, SAMPLES, TEXT_LEN, QUERY_HEADS * HEAD_SIZE)
    base = jax.random.truncated_normal(jax.random.fold_in(key, 31), -6.0, 6.0, shape_full, jnp.float32)
    return base.astype(jnp.bfloat16)


def levels(rng, shape, split, smallest, top_value):
    level = 1.0
    for dim, parts in split:
        draws = jax.random.uniform(jax.random.fold_in(jax.random.fold_in(rng, 6), dim), (parts,), jnp.float32, smallest / len(split), top_value / len(split))
        level = level * jnp.repeat(jnp.exp(draws), shape[dim] // parts).reshape((-1,) + (1,) * (len(shape) - 1 - dim))
    return level


def bell_draw(rng, dims, deviation, limit, pieces=(), held_as=jnp.bfloat16):
    result = jax.random.normal(rng, dims, jnp.float32) * deviation
    if len(pieces) > 0:
        result = levels(rng, dims, pieces, -0.22, 0.18) * result
    return jnp.clip(result, min=-limit, max=limit).astype(held_as)


def setup_inputs(seed: int = 0) -> dict:
    splits = jax.random.split(jax.random.key(seed), 8)
    queries = draw_queries(jax.random.fold_in(splits[7], 71), 0)
    image_tokens = bell_draw(splits[1], (SAMPLES, IMG, D), 1.0, 6.0, ((0, 16), (1, 8)))
    key_weight = bell_draw(splits[2], (SECTIONS, D, KVD), D ** -0.5, 0.0625, ((0, 8),))
    value_weight = bell_draw(splits[3], (SECTIONS, D, KVD), D ** -0.5, 0.0625, ((0, 8),))
    cotangent = bell_draw(splits[4], (SECTIONS, SAMPLES, TEXT_LEN, HQD), 1.0, 6.0, ((0, 8), (1, 16)))
    tile_counts = draw_tile_counts(jax.random.fold_in(splits[7], 71), 0)
    text_lengths = draw_text_lengths(jax.random.fold_in(splits[7], 71), 0)
    return {"queries": queries, "image_tokens": image_tokens, "key_weight": key_weight, "value_weight": value_weight, "cotangent": cotangent, "tile_counts": tile_counts, "text_lengths": text_lengths}


def attend_one(queries, key_rows, value_rows, cotangent, key_limit, row_limit):
    total_rows = queries.shape[0]
    total_keys = key_rows.shape[0]
    group_width = QUERY_HEADS // KEY_VALUE_HEADS
    heads_of_queries = queries.astype(jnp.float32).reshape(total_rows, KEY_VALUE_HEADS, group_width, HEAD_SIZE)
    heads_of_keys = key_rows.astype(jnp.float32).reshape(total_keys, KEY_VALUE_HEADS, HEAD_SIZE)
    heads_of_values = value_rows.astype(jnp.float32).reshape(total_keys, KEY_VALUE_HEADS, HEAD_SIZE)
    row_live = (jnp.arange(total_rows) < row_limit)[:, None]
    active_cotangent = jnp.where(row_live, cotangent, jnp.zeros_like(cotangent)).astype(jnp.float32)
    head_gradient = active_cotangent.reshape(total_rows, KEY_VALUE_HEADS, group_width, HEAD_SIZE)
    scaling = 1.0 / math.sqrt(HEAD_SIZE)
    scores = jnp.einsum('lhgd,nhd->hgln', heads_of_queries, heads_of_keys) * scaling
    key_live = jnp.arange(total_keys) < key_limit
    scores = jnp.where(key_live, scores, -jnp.inf)
    row_max = lax.optimization_barrier(jnp.max(scores, axis=-1, keepdims=True))
    raised = jnp.exp(scores - row_max)
    weights = raised / lax.optimization_barrier(jnp.sum(raised, axis=-1, keepdims=True))
    weights_low = weights.astype(jnp.bfloat16).astype(jnp.float32)
    value_gradient = jnp.einsum('hgln,lhgd->nhd', weights_low, head_gradient).astype(jnp.bfloat16)
    prob_grad = jnp.einsum('lhgd,nhd->hgln', head_gradient, heads_of_values)
    row_dot = lax.optimization_barrier(jnp.sum(weights * prob_grad, axis=-1, keepdims=True))
    score_grad = (weights * (prob_grad - row_dot) * scaling).astype(jnp.bfloat16).astype(jnp.float32)
    query_gradient = jnp.einsum('hgln,nhd->lhgd', score_grad, heads_of_keys).astype(jnp.bfloat16)
    key_gradient = jnp.einsum('hgln,lhgd->nhd', score_grad, heads_of_queries).astype(jnp.bfloat16)
    return (query_gradient.reshape(total_rows, QUERY_HEADS * HEAD_SIZE), key_gradient.reshape(total_keys, KEY_VALUE_HEADS * HEAD_SIZE), value_gradient.reshape(total_keys, KEY_VALUE_HEADS * HEAD_SIZE))

def rounded(term):
    return lax.optimization_barrier(term.astype(jnp.bfloat16)).astype(jnp.float32)

def reference(queries, image_tokens, key_weight, value_weight, cotangent, tile_counts, text_lengths):
    tile_len = IMG // MAX_TILES
    key_limits = tile_counts * tile_len
    image_float = image_tokens.astype(jnp.float32)
    image_sum = jnp.zeros(image_tokens.shape, jnp.float32)
    query_list = []
    key_list = []
    value_list = []
    for section_index in range(N_SECTION):
        w_key = key_weight[section_index].astype(jnp.float32)
        w_value = value_weight[section_index].astype(jnp.float32)
        key_rows = jnp.einsum('std,dk->stk', image_float, w_key).astype(jnp.bfloat16)
        value_rows = jnp.einsum('std,dk->stk', image_float, w_value).astype(jnp.bfloat16)
        query_gradient, key_gradient, value_gradient = jax.vmap(attend_one)(queries[section_index], key_rows, value_rows, cotangent[section_index], key_limits, text_lengths)
        query_list.append(query_gradient)
        key_float = key_gradient.astype(jnp.float32)
        value_float = value_gradient.astype(jnp.float32)
        image_term = jnp.einsum('stk,dk->std', key_float, w_key) + jnp.einsum('stk,dk->std', value_float, w_value)
        image_sum = image_sum + rounded(image_term)
        grouped = image_float.reshape(N_DP, SAMP_DEV * IMG, D)
        key_groups = key_float.reshape(N_DP, SAMP_DEV * IMG, KVD)
        value_groups = value_float.reshape(N_DP, SAMP_DEV * IMG, KVD)
        key_parts = rounded(jnp.einsum('rtd,rtk->rdk', grouped, key_groups))
        value_parts = rounded(jnp.einsum('rtd,rtk->rdk', grouped, value_groups))
        key_list.append(lax.optimization_barrier(jnp.sum(key_parts, axis=0)).astype(jnp.bfloat16))
        value_list.append(lax.optimization_barrier(jnp.sum(value_parts, axis=0)).astype(jnp.bfloat16))
    return (jnp.stack(query_list), image_sum.astype(jnp.bfloat16), jnp.stack(key_list), jnp.stack(value_list))
```

```python
import functools
import math

import jax
import jax.numpy as jnp
from jax import lax
from jax.experimental import pallas as pl
from jax.experimental.pallas import tpu as pltpu
from jax.sharding import PartitionSpec as P

QUERY_HEADS = 32
KEY_VALUE_HEADS = 4
HEAD_SIZE = 128
MAX_TILES = 4
MESH_ID = pl.DeviceIdType.MESH


def attend_one(queries, key_rows, value_rows, cotangent, key_limit, row_limit):
    total_rows = queries.shape[0]
    total_keys = key_rows.shape[0]
    group_width = QUERY_HEADS // KEY_VALUE_HEADS
    heads_of_queries = queries.reshape(total_rows, KEY_VALUE_HEADS, group_width, HEAD_SIZE)
    heads_of_keys = key_rows.reshape(total_keys, KEY_VALUE_HEADS, HEAD_SIZE)
    heads_of_values = value_rows.reshape(total_keys, KEY_VALUE_HEADS, HEAD_SIZE)
    row_live = (jnp.arange(total_rows) < row_limit)[:, None]
    active_cotangent = jnp.where(row_live, cotangent, jnp.zeros_like(cotangent))
    head_gradient = active_cotangent.reshape(total_rows, KEY_VALUE_HEADS, group_width, HEAD_SIZE)
    scaling = 1.0 / math.sqrt(HEAD_SIZE)
    scores = (
        jnp.einsum(
            "lhgd,nhd->hgln", heads_of_queries, heads_of_keys, preferred_element_type=jnp.float32
        )
        * scaling
    )
    key_live = jnp.arange(total_keys) < key_limit
    scores = jnp.where(key_live, scores, -jnp.inf)
    row_max = jnp.max(scores, axis=-1, keepdims=True)
    raised = jnp.exp(scores - row_max)
    weights = raised / jnp.sum(raised, axis=-1, keepdims=True)
    weights_low = weights.astype(jnp.bfloat16)
    value_gradient = jnp.einsum(
        "hgln,lhgd->nhd", weights_low, head_gradient, preferred_element_type=jnp.float32
    ).astype(jnp.bfloat16)
    prob_grad = jnp.einsum(
        "lhgd,nhd->hgln", head_gradient, heads_of_values, preferred_element_type=jnp.float32
    )
    row_dot = jnp.sum(weights * prob_grad, axis=-1, keepdims=True)
    score_grad = (weights * (prob_grad - row_dot) * scaling).astype(jnp.bfloat16)
    query_gradient = jnp.einsum(
        "hgln,nhd->lhgd", score_grad, heads_of_keys, preferred_element_type=jnp.float32
    ).astype(jnp.bfloat16)
    key_gradient = jnp.einsum(
        "hgln,lhgd->nhd", score_grad, heads_of_queries, preferred_element_type=jnp.float32
    ).astype(jnp.bfloat16)
    return (
        query_gradient.reshape(total_rows, QUERY_HEADS * HEAD_SIZE),
        key_gradient.reshape(total_keys, KEY_VALUE_HEADS * HEAD_SIZE),
        value_gradient.reshape(total_keys, KEY_VALUE_HEADS * HEAD_SIZE),
    )


def exchange_kernel(n, scatter, x_ref, o_ref, send_sems, recv_sems, local_sem):
    me = lax.axis_index("section")
    row = lax.axis_index("dp")
    barrier = pltpu.get_barrier_semaphore()
    for k in range(1, n):
        pl.semaphore_signal(
            barrier, inc=1, device_id=(lax.rem(me + k, n), row), device_id_type=MESH_ID
        )
    pl.semaphore_wait(barrier, n - 1)
    own = x_ref.at[:, me] if scatter else x_ref
    local = pltpu.make_async_copy(own, o_ref.at[:, me], local_sem)
    local.start()
    copies = []
    for k in range(1, n):
        peer = lax.rem(me + k, n)
        src = x_ref.at[:, peer] if scatter else x_ref
        copy = pltpu.make_async_remote_copy(
            src_ref=src,
            dst_ref=o_ref.at[:, me],
            send_sem=send_sems.at[k],
            recv_sem=recv_sems.at[k],
            device_id=(peer, row),
            device_id_type=MESH_ID,
        )
        copy.start()
        copies.append(copy)
    for copy in copies:
        copy.wait()
    local.wait()


def exchange(x, n, scatter, collective_id):
    if scatter:
        out_shape = x.shape
    else:
        out_shape = (x.shape[0], n) + x.shape[1:]
    return pl.pallas_call(
        functools.partial(exchange_kernel, n, scatter),
        out_shape=jax.ShapeDtypeStruct(out_shape, x.dtype),
        in_specs=[pl.BlockSpec(memory_space=pl.ANY)],
        out_specs=pl.BlockSpec(memory_space=pl.ANY),
        scratch_shapes=[
            pltpu.SemaphoreType.DMA((n,)),
            pltpu.SemaphoreType.DMA((n,)),
            pltpu.SemaphoreType.DMA(()),
        ],
        compiler_params=pltpu.CompilerParams(collective_id=collective_id, has_side_effects=True),
    )(x)


def shards(queries, image_tokens, key_weight, value_weight, cotangent, tile_counts, text_lengths):
    n_section = lax.axis_size("section")
    samples_here, chunk, model_width = image_tokens.shape
    gathered = exchange(image_tokens, n_section, False, 0)
    image_len = n_section * chunk
    tile_len = image_len // MAX_TILES
    w_key = key_weight[0]
    w_value = value_weight[0]
    query_local = queries[0]
    cotan_local = cotangent[0]
    query_list = []
    key_list = []
    value_list = []
    keys_all = jnp.einsum(
        "bjtd,dk->bjtk", gathered, w_key, preferred_element_type=jnp.float32
    ).astype(jnp.bfloat16).reshape(samples_here, image_len, -1)
    values_all = jnp.einsum(
        "bjtd,dk->bjtk", gathered, w_value, preferred_element_type=jnp.float32
    ).astype(jnp.bfloat16).reshape(samples_here, image_len, -1)
    for sample_index in range(samples_here):
        query_gradient, key_gradient, value_gradient = attend_one(
            query_local[sample_index],
            keys_all[sample_index],
            values_all[sample_index],
            cotan_local[sample_index],
            tile_counts[sample_index] * tile_len,
            text_lengths[sample_index],
        )
        query_list.append(query_gradient)
        key_list.append(key_gradient)
        value_list.append(value_gradient)
    query_out = jnp.stack(query_list)[None]
    key_grads = jnp.stack(key_list).reshape(samples_here, n_section, chunk, -1)
    value_grads = jnp.stack(value_list).reshape(samples_here, n_section, chunk, -1)
    kv_grads = jnp.concatenate([key_grads, value_grads], axis=-1)
    kv_term = jnp.einsum(
        "bjtd,bjtk->dk", gathered, kv_grads, preferred_element_type=jnp.float32
    )
    kv_sum = lax.psum_scatter(kv_term.astype(jnp.bfloat16), "dp", scatter_dimension=0, tiled=True)
    kv_width = key_grads.shape[-1]
    image_term = jnp.einsum(
        "bjtk,dk->bjtd", key_grads, w_key, preferred_element_type=jnp.float32
    )
    image_term = image_term + jnp.einsum(
        "bjtk,dk->bjtd", value_grads, w_value, preferred_element_type=jnp.float32
    )
    received = exchange(image_term.astype(jnp.bfloat16), n_section, True, 1)
    image_out = jnp.sum(received.astype(jnp.float32), axis=1).astype(jnp.bfloat16)
    return (
        query_out,
        image_out,
        kv_sum[:, :kv_width][None],
        kv_sum[:, kv_width:][None],
    )


def solution(mesh):
    placed = (
        P("section", "dp", None, None),
        P("dp", "section", None),
        P("section", None, None),
        P("section", None, None),
        P("section", "dp", None, None),
        P("dp"),
        P("dp"),
    )
    return jax.shard_map(
        shards,
        mesh=mesh,
        in_specs=placed,
        out_specs=(
            P("section", "dp", None, None),
            P("dp", "section", None),
            P("section", "dp", None),
            P("section", "dp", None),
        ),
        check_vma=False,
    )
```

```python
import functools
import math

import jax
import jax.numpy as jnp
from jax import lax
from jax.experimental import pallas as pl
from jax.experimental.pallas import tpu as pltpu
from jax.sharding import PartitionSpec as P

QUERY_HEADS = 32
KEY_VALUE_HEADS = 4
HEAD_SIZE = 128
MAX_TILES = 4
MESH_ID = pl.DeviceIdType.MESH


def attend_one(queries, key_rows, value_rows, cotangent, key_limit, row_limit):
    total_rows = queries.shape[0]
    total_keys = key_rows.shape[0]
    group_width = QUERY_HEADS // KEY_VALUE_HEADS
    heads_of_queries = queries.reshape(total_rows, KEY_VALUE_HEADS, group_width, HEAD_SIZE)
    heads_of_keys = key_rows.reshape(total_keys, KEY_VALUE_HEADS, HEAD_SIZE)
    heads_of_values = value_rows.reshape(total_keys, KEY_VALUE_HEADS, HEAD_SIZE)
    row_live = (jnp.arange(total_rows) < row_limit)[:, None]
    active_cotangent = jnp.where(row_live, cotangent, jnp.zeros_like(cotangent))
    head_gradient = active_cotangent.reshape(total_rows, KEY_VALUE_HEADS, group_width, HEAD_SIZE)
    scaling = 1.0 / math.sqrt(HEAD_SIZE)
    scores = (
        jnp.einsum(
            "lhgd,nhd->hgln", heads_of_queries, heads_of_keys, preferred_element_type=jnp.float32
        )
        * scaling
    )
    key_live = jnp.arange(total_keys) < key_limit
    scores = jnp.where(key_live, scores, -jnp.inf)
    row_max = jnp.max(scores, axis=-1, keepdims=True)
    raised = jnp.exp(scores - row_max)
    weights = raised / jnp.sum(raised, axis=-1, keepdims=True)
    weights_low = weights.astype(jnp.bfloat16)
    value_gradient = jnp.einsum(
        "hgln,lhgd->nhd", weights_low, head_gradient, preferred_element_type=jnp.float32
    ).astype(jnp.bfloat16)
    prob_grad = jnp.einsum(
        "lhgd,nhd->hgln", head_gradient, heads_of_values, preferred_element_type=jnp.float32
    )
    row_dot = jnp.sum(weights * prob_grad, axis=-1, keepdims=True)
    score_grad = (weights * (prob_grad - row_dot) * scaling).astype(jnp.bfloat16)
    query_gradient = jnp.einsum(
        "hgln,nhd->lhgd", score_grad, heads_of_keys, preferred_element_type=jnp.float32
    ).astype(jnp.bfloat16)
    key_gradient = jnp.einsum(
        "hgln,lhgd->nhd", score_grad, heads_of_queries, preferred_element_type=jnp.float32
    ).astype(jnp.bfloat16)
    return (
        query_gradient.reshape(total_rows, QUERY_HEADS * HEAD_SIZE),
        key_gradient.reshape(total_keys, KEY_VALUE_HEADS * HEAD_SIZE),
        value_gradient.reshape(total_keys, KEY_VALUE_HEADS * HEAD_SIZE),
    )


def exchange_kernel(n, scatter, x_ref, o_ref, send_sems, recv_sems, local_sem):
    me = lax.axis_index("section")
    row = lax.axis_index("dp")
    barrier = pltpu.get_barrier_semaphore()
    for k in range(1, n):
        pl.semaphore_signal(
            barrier, inc=1, device_id=(lax.rem(me + k, n), row), device_id_type=MESH_ID
        )
    pl.semaphore_wait(barrier, n - 1)
    own = x_ref.at[:, me] if scatter else x_ref
    local = pltpu.make_async_copy(own, o_ref.at[:, me], local_sem)
    local.start()
    copies = []
    for k in range(1, n):
        peer = lax.rem(me + k, n)
        src = x_ref.at[:, peer] if scatter else x_ref
        copy = pltpu.make_async_remote_copy(
            src_ref=src,
            dst_ref=o_ref.at[:, me],
            send_sem=send_sems.at[k],
            recv_sem=recv_sems.at[k],
            device_id=(peer, row),
            device_id_type=MESH_ID,
        )
        copy.start()
        copies.append(copy)
    for copy in copies:
        copy.wait()
    local.wait()


def exchange(x, n, scatter, collective_id):
    if scatter:
        out_shape = x.shape
    else:
        out_shape = (x.shape[0], n) + x.shape[1:]
    return pl.pallas_call(
        functools.partial(exchange_kernel, n, scatter),
        out_shape=jax.ShapeDtypeStruct(out_shape, x.dtype),
        in_specs=[pl.BlockSpec(memory_space=pl.ANY)],
        out_specs=pl.BlockSpec(memory_space=pl.ANY),
        scratch_shapes=[
            pltpu.SemaphoreType.DMA((n,)),
            pltpu.SemaphoreType.DMA((n,)),
            pltpu.SemaphoreType.DMA(()),
        ],
        compiler_params=pltpu.CompilerParams(collective_id=collective_id, has_side_effects=True),
    )(x)


def chip_then_core_scatter(term):
    n_dp = lax.axis_size("dp")
    rows, width = term.shape
    me = lax.axis_index("dp")
    core = lax.rem(me, 2)
    chunks = term.reshape(n_dp // 2, 2, rows // n_dp, width)
    mine = jnp.where(core == 0, chunks[:, 0], chunks[:, 1])
    theirs = jnp.where(core == 0, chunks[:, 1], chunks[:, 0])
    pairs = [(i, i ^ 1) for i in range(n_dp)]
    arrived = lax.ppermute(theirs, "dp", perm=pairs)
    paired = (mine.astype(jnp.float32) + arrived.astype(jnp.float32)).astype(jnp.bfloat16)
    groups = [list(range(c, n_dp, 2)) for c in range(2)]
    return lax.psum_scatter(
        paired.reshape(rows // 2, width),
        "dp",
        scatter_dimension=0,
        axis_index_groups=groups,
        tiled=True,
    )


def shards(queries, image_tokens, key_weight, value_weight, cotangent, tile_counts, text_lengths):
    n_section = lax.axis_size("section")
    samples_here, chunk, model_width = image_tokens.shape
    gathered = exchange(image_tokens, n_section, False, 0)
    image_len = n_section * chunk
    tile_len = image_len // MAX_TILES
    w_key = key_weight[0]
    w_value = value_weight[0]
    query_local = queries[0]
    cotan_local = cotangent[0]
    query_list = []
    key_list = []
    value_list = []
    keys_all = jnp.einsum(
        "bjtd,dk->bjtk", gathered, w_key, preferred_element_type=jnp.float32
    ).astype(jnp.bfloat16).reshape(samples_here, image_len, -1)
    values_all = jnp.einsum(
        "bjtd,dk->bjtk", gathered, w_value, preferred_element_type=jnp.float32
    ).astype(jnp.bfloat16).reshape(samples_here, image_len, -1)
    for sample_index in range(samples_here):
        query_gradient, key_gradient, value_gradient = attend_one(
            query_local[sample_index],
            keys_all[sample_index],
            values_all[sample_index],
            cotan_local[sample_index],
            tile_counts[sample_index] * tile_len,
            text_lengths[sample_index],
        )
        query_list.append(query_gradient)
        key_list.append(key_gradient)
        value_list.append(value_gradient)
    query_out = jnp.stack(query_list)[None]
    key_grads = jnp.stack(key_list).reshape(samples_here, n_section, chunk, -1)
    value_grads = jnp.stack(value_list).reshape(samples_here, n_section, chunk, -1)
    kv_grads = jnp.concatenate([key_grads, value_grads], axis=-1)
    kv_term = jnp.einsum(
        "bjtd,bjtk->dk", gathered, kv_grads, preferred_element_type=jnp.float32
    )
    kv_sum = chip_then_core_scatter(kv_term.astype(jnp.bfloat16))
    kv_width = key_grads.shape[-1]
    image_term = jnp.einsum(
        "bjtk,dk->bjtd", key_grads, w_key, preferred_element_type=jnp.float32
    )
    image_term = image_term + jnp.einsum(
        "bjtk,dk->bjtd", value_grads, w_value, preferred_element_type=jnp.float32
    )
    received = exchange(image_term.astype(jnp.bfloat16), n_section, True, 1)
    image_out = jnp.sum(received.astype(jnp.float32), axis=1).astype(jnp.bfloat16)
    return (
        query_out,
        image_out,
        kv_sum[:, :kv_width][None],
        kv_sum[:, kv_width:][None],
    )


def solution(mesh):
    placed = (
        P("section", "dp", None, None),
        P("dp", "section", None),
        P("section", None, None),
        P("section", None, None),
        P("section", "dp", None, None),
        P("dp"),
        P("dp"),
    )
    return jax.shard_map(
        shards,
        mesh=mesh,
        in_specs=placed,
        out_specs=(
            P("section", "dp", None, None),
            P("dp", "section", None),
            P("section", "dp", None),
            P("section", "dp", None),
        ),
        check_vma=False,
    )
```

```python
import functools
import math

import jax
import jax.numpy as jnp
from jax import lax
from jax.experimental import pallas as pl
from jax.experimental.pallas import tpu as pltpu
from jax.sharding import PartitionSpec as P

QUERY_HEADS = 32
KEY_VALUE_HEADS = 4
HEAD_SIZE = 128
MAX_TILES = 4
MESH_ID = pl.DeviceIdType.MESH


def attend_one(queries, key_rows, value_rows, cotangent, key_limit, row_limit):
    total_rows = queries.shape[0]
    total_keys = key_rows.shape[0]
    group_width = QUERY_HEADS // KEY_VALUE_HEADS
    heads_of_queries = queries.reshape(total_rows, KEY_VALUE_HEADS, group_width, HEAD_SIZE)
    heads_of_keys = key_rows.reshape(total_keys, KEY_VALUE_HEADS, HEAD_SIZE)
    heads_of_values = value_rows.reshape(total_keys, KEY_VALUE_HEADS, HEAD_SIZE)
    row_live = (jnp.arange(total_rows) < row_limit)[:, None]
    active_cotangent = jnp.where(row_live, cotangent, jnp.zeros_like(cotangent))
    head_gradient = active_cotangent.reshape(total_rows, KEY_VALUE_HEADS, group_width, HEAD_SIZE)
    scaling = 1.0 / math.sqrt(HEAD_SIZE)
    scores = (
        jnp.einsum(
            "lhgd,nhd->hgln", heads_of_queries, heads_of_keys, preferred_element_type=jnp.float32
        )
        * scaling
    )
    key_live = jnp.arange(total_keys) < key_limit
    scores = jnp.where(key_live, scores, -jnp.inf)
    row_max = jnp.max(scores, axis=-1, keepdims=True)
    raised = jnp.exp(scores - row_max)
    weights = raised / jnp.sum(raised, axis=-1, keepdims=True)
    weights_low = weights.astype(jnp.bfloat16)
    value_gradient = jnp.einsum(
        "hgln,lhgd->nhd", weights_low, head_gradient, preferred_element_type=jnp.float32
    ).astype(jnp.bfloat16)
    prob_grad = jnp.einsum(
        "lhgd,nhd->hgln", head_gradient, heads_of_values, preferred_element_type=jnp.float32
    )
    row_dot = jnp.sum(weights * prob_grad, axis=-1, keepdims=True)
    score_grad = (weights * (prob_grad - row_dot) * scaling).astype(jnp.bfloat16)
    query_gradient = jnp.einsum(
        "hgln,nhd->lhgd", score_grad, heads_of_keys, preferred_element_type=jnp.float32
    ).astype(jnp.bfloat16)
    key_gradient = jnp.einsum(
        "hgln,lhgd->nhd", score_grad, heads_of_queries, preferred_element_type=jnp.float32
    ).astype(jnp.bfloat16)
    return (
        query_gradient.reshape(total_rows, QUERY_HEADS * HEAD_SIZE),
        key_gradient.reshape(total_keys, KEY_VALUE_HEADS * HEAD_SIZE),
        value_gradient.reshape(total_keys, KEY_VALUE_HEADS * HEAD_SIZE),
    )


def exchange_kernel(n, scatter, x_ref, o_ref, send_sems, recv_sems, local_sem):
    me = lax.axis_index("section")
    row = lax.axis_index("dp")
    barrier = pltpu.get_barrier_semaphore()
    for k in range(1, n):
        pl.semaphore_signal(
            barrier, inc=1, device_id=(lax.rem(me + k, n), row), device_id_type=MESH_ID
        )
    pl.semaphore_wait(barrier, n - 1)
    own = x_ref.at[:, me] if scatter else x_ref
    local = pltpu.make_async_copy(own, o_ref.at[:, me], local_sem)
    local.start()
    copies = []
    for k in range(1, n):
        peer = lax.rem(me + k, n)
        src = x_ref.at[:, peer] if scatter else x_ref
        copy = pltpu.make_async_remote_copy(
            src_ref=src,
            dst_ref=o_ref.at[:, me],
            send_sem=send_sems.at[k],
            recv_sem=recv_sems.at[k],
            device_id=(peer, row),
            device_id_type=MESH_ID,
        )
        copy.start()
        copies.append(copy)
    for copy in copies:
        copy.wait()
    local.wait()


def exchange(x, n, scatter, collective_id):
    if scatter:
        out_shape = x.shape
    else:
        out_shape = (x.shape[0], n) + x.shape[1:]
    return pl.pallas_call(
        functools.partial(exchange_kernel, n, scatter),
        out_shape=jax.ShapeDtypeStruct(out_shape, x.dtype),
        in_specs=[pl.BlockSpec(memory_space=pl.ANY)],
        out_specs=pl.BlockSpec(memory_space=pl.ANY),
        scratch_shapes=[
            pltpu.SemaphoreType.DMA((n,)),
            pltpu.SemaphoreType.DMA((n,)),
            pltpu.SemaphoreType.DMA(()),
        ],
        compiler_params=pltpu.CompilerParams(collective_id=collective_id, has_side_effects=True),
    )(x)


def shards(queries, image_tokens, key_weight, value_weight, cotangent, tile_counts, text_lengths):
    n_section = lax.axis_size("section")
    samples_here, chunk, model_width = image_tokens.shape
    image_len = n_section * chunk
    tile_len = image_len // MAX_TILES
    w_key = key_weight[0]
    w_value = value_weight[0]
    query_local = queries[0]
    cotan_local = cotangent[0]
    query_list = []
    kv_term = None
    image_list = []
    for sample_index in range(samples_here):
        tokens = lax.all_gather(image_tokens[sample_index], "section", axis=0, tiled=True)
        keys = jnp.dot(tokens, w_key, preferred_element_type=jnp.float32).astype(jnp.bfloat16)
        values = jnp.dot(tokens, w_value, preferred_element_type=jnp.float32).astype(jnp.bfloat16)
        query_gradient, key_gradient, value_gradient = attend_one(
            query_local[sample_index],
            keys,
            values,
            cotan_local[sample_index],
            tile_counts[sample_index] * tile_len,
            text_lengths[sample_index],
        )
        query_list.append(query_gradient)
        kv_grads = jnp.concatenate([key_gradient, value_gradient], axis=-1)
        part = jnp.einsum("td,tk->dk", tokens, kv_grads, preferred_element_type=jnp.float32)
        kv_term = part if kv_term is None else kv_term + part
        term = jnp.einsum("tk,dk->td", key_gradient, w_key, preferred_element_type=jnp.float32)
        term = term + jnp.einsum("tk,dk->td", value_gradient, w_value, preferred_element_type=jnp.float32)
        image_list.append(term.astype(jnp.bfloat16).reshape(n_section, chunk, model_width))
    query_out = jnp.stack(query_list)[None]
    kv_sum = lax.psum_scatter(kv_term.astype(jnp.bfloat16), "dp", scatter_dimension=0, tiled=True)
    kv_width = kv_sum.shape[-1] // 2
    received = exchange(jnp.stack(image_list), n_section, True, 1)
    image_out = jnp.sum(received.astype(jnp.float32), axis=1).astype(jnp.bfloat16)
    return (
        query_out,
        image_out,
        kv_sum[:, :kv_width][None],
        kv_sum[:, kv_width:][None],
    )


def solution(mesh):
    placed = (
        P("section", "dp", None, None),
        P("dp", "section", None),
        P("section", None, None),
        P("section", None, None),
        P("section", "dp", None, None),
        P("dp"),
        P("dp"),
    )
    return jax.shard_map(
        shards,
        mesh=mesh,
        in_specs=placed,
        out_specs=(
            P("section", "dp", None, None),
            P("dp", "section", None),
            P("section", "dp", None),
            P("section", "dp", None),
        ),
        check_vma=False,
    )
```

```python
import functools
import math

import jax
import jax.numpy as jnp
from jax import lax
from jax.experimental import pallas as pl
from jax.experimental.pallas import tpu as pltpu
from jax.sharding import PartitionSpec as P

QUERY_HEADS = 32
KEY_VALUE_HEADS = 4
HEAD_SIZE = 128
MAX_TILES = 4
MESH_ID = pl.DeviceIdType.MESH


def attend_one(queries, key_rows, value_rows, cotangent, key_limit, row_limit):
    total_rows = queries.shape[0]
    total_keys = key_rows.shape[0]
    group_width = QUERY_HEADS // KEY_VALUE_HEADS
    heads_of_queries = queries.reshape(total_rows, KEY_VALUE_HEADS, group_width, HEAD_SIZE)
    heads_of_keys = key_rows.reshape(total_keys, KEY_VALUE_HEADS, HEAD_SIZE)
    heads_of_values = value_rows.reshape(total_keys, KEY_VALUE_HEADS, HEAD_SIZE)
    row_live = (jnp.arange(total_rows) < row_limit)[:, None]
    active_cotangent = jnp.where(row_live, cotangent, jnp.zeros_like(cotangent))
    head_gradient = active_cotangent.reshape(total_rows, KEY_VALUE_HEADS, group_width, HEAD_SIZE)
    scaling = 1.0 / math.sqrt(HEAD_SIZE)
    scores = (
        jnp.einsum(
            "lhgd,nhd->hgln", heads_of_queries, heads_of_keys, preferred_element_type=jnp.float32
        )
        * scaling
    )
    key_live = jnp.arange(total_keys) < key_limit
    scores = jnp.where(key_live, scores, -jnp.inf)
    row_max = jnp.max(scores, axis=-1, keepdims=True)
    raised = jnp.exp(scores - row_max)
    weights = raised / jnp.sum(raised, axis=-1, keepdims=True)
    weights_low = weights.astype(jnp.bfloat16)
    value_gradient = jnp.einsum(
        "hgln,lhgd->nhd", weights_low, head_gradient, preferred_element_type=jnp.float32
    ).astype(jnp.bfloat16)
    prob_grad = jnp.einsum(
        "lhgd,nhd->hgln", head_gradient, heads_of_values, preferred_element_type=jnp.float32
    )
    row_dot = jnp.sum(weights * prob_grad, axis=-1, keepdims=True)
    score_grad = (weights * (prob_grad - row_dot) * scaling).astype(jnp.bfloat16)
    query_gradient = jnp.einsum(
        "hgln,nhd->lhgd", score_grad, heads_of_keys, preferred_element_type=jnp.float32
    ).astype(jnp.bfloat16)
    key_gradient = jnp.einsum(
        "hgln,lhgd->nhd", score_grad, heads_of_queries, preferred_element_type=jnp.float32
    ).astype(jnp.bfloat16)
    return (
        query_gradient.reshape(total_rows, QUERY_HEADS * HEAD_SIZE),
        key_gradient.reshape(total_keys, KEY_VALUE_HEADS * HEAD_SIZE),
        value_gradient.reshape(total_keys, KEY_VALUE_HEADS * HEAD_SIZE),
    )


def exchange_kernel(n, scatter, x_ref, o_ref, send_sems, recv_sems, local_sem):
    me = lax.axis_index("section")
    row = lax.axis_index("dp")
    barrier = pltpu.get_barrier_semaphore()
    for k in range(1, n):
        pl.semaphore_signal(
            barrier, inc=1, device_id=(lax.rem(me + k, n), row), device_id_type=MESH_ID
        )
    pl.semaphore_wait(barrier, n - 1)
    own = x_ref.at[:, me] if scatter else x_ref
    local = pltpu.make_async_copy(own, o_ref.at[:, me], local_sem)
    local.start()
    copies = []
    for k in range(1, n):
        peer = lax.rem(me + k, n)
        src = x_ref.at[:, peer] if scatter else x_ref
        copy = pltpu.make_async_remote_copy(
            src_ref=src,
            dst_ref=o_ref.at[:, me],
            send_sem=send_sems.at[k],
            recv_sem=recv_sems.at[k],
            device_id=(peer, row),
            device_id_type=MESH_ID,
        )
        copy.start()
        copies.append(copy)
    for copy in copies:
        copy.wait()
    local.wait()


def relay_gather_kernel(x_ref, o_ref, stage, local_sem, direct_send, direct_recv,
                        hop_send, hop_recv, fwd_send, fwd_recv):
    s = lax.axis_index("section")
    r = lax.axis_index("dp")
    y = lax.rem(s, 4)
    z = (s // 4) * 2 + r // 8
    xc = lax.rem(r, 8)
    half = x_ref.shape[-1] // 2

    def sec(zz, yy):
        return (lax.rem(zz, 4) // 2) * 4 + yy

    def dpi(zz):
        return lax.rem(zz, 2) * 8 + xc

    up, down = z + 1, z + 3
    peers = [(sec(z, lax.rem(y + j, 4)), r) for j in range(1, 4)]
    for yy in range(4):
        peers.append((sec(up, yy), dpi(up)))
        peers.append((sec(down, yy), dpi(down)))
    barrier = pltpu.get_barrier_semaphore()
    for peer in peers:
        pl.semaphore_signal(barrier, inc=1, device_id=peer, device_id_type=MESH_ID)
    pl.semaphore_wait(barrier, len(peers))

    local = pltpu.make_async_copy(x_ref, o_ref.at[:, s], local_sem)
    local.start()
    sends = []
    for j in range(1, 4):
        copy = pltpu.make_async_remote_copy(
            src_ref=x_ref,
            dst_ref=o_ref.at[:, s],
            send_sem=direct_send.at[j],
            recv_sem=direct_recv.at[j],
            device_id=peers[j - 1],
            device_id_type=MESH_ID,
        )
        copy.start()
        sends.append(copy)
    hops = []
    for side, (target, lanes) in enumerate(((up, pl.ds(0, half)), (down, pl.ds(half, half)))):
        copy = pltpu.make_async_remote_copy(
            src_ref=x_ref.at[:, :, lanes],
            dst_ref=stage.at[side],
            send_sem=hop_send.at[side],
            recv_sem=hop_recv.at[side],
            device_id=(sec(target, y), dpi(target)),
            device_id_type=MESH_ID,
        )
        copy.start()
        hops.append(copy)
    forwards = []
    for side, (origin, target, lanes) in enumerate(
        ((down, up, pl.ds(0, half)), (up, down, pl.ds(half, half)))
    ):
        hops[side].wait_recv()
        for yy in range(4):
            copy = pltpu.make_async_remote_copy(
                src_ref=stage.at[side],
                dst_ref=o_ref.at[:, sec(origin, y), :, lanes],
                send_sem=fwd_send.at[side, yy],
                recv_sem=fwd_recv.at[side, y],
                device_id=(sec(target, yy), dpi(target)),
                device_id_type=MESH_ID,
            )
            copy.start()
            forwards.append(copy)
    for copy in sends:
        copy.wait()
    for copy in hops:
        copy.wait_send()
    for copy in forwards:
        copy.wait_send()
    for side, (origin, target, lanes) in enumerate(
        ((down, up, pl.ds(0, half)), (up, down, pl.ds(half, half)))
    ):
        for yy in range(4):
            pltpu.make_async_remote_copy(
                src_ref=stage.at[side],
                dst_ref=o_ref.at[:, sec(origin, y), :, lanes],
                send_sem=fwd_send.at[side, yy],
                recv_sem=fwd_recv.at[side, yy],
                device_id=(sec(target, yy), dpi(target)),
                device_id_type=MESH_ID,
            ).wait_recv()
    local.wait()


def relay_gather(x, n):
    samples, chunk, width = x.shape
    return pl.pallas_call(
        relay_gather_kernel,
        out_shape=jax.ShapeDtypeStruct((samples, n, chunk, width), x.dtype),
        in_specs=[pl.BlockSpec(memory_space=pl.ANY)],
        out_specs=pl.BlockSpec(memory_space=pl.ANY),
        scratch_shapes=[
            pltpu.VMEM((2, samples, chunk, width // 2), x.dtype),
            pltpu.SemaphoreType.DMA(()),
            pltpu.SemaphoreType.DMA((4,)),
            pltpu.SemaphoreType.DMA((4,)),
            pltpu.SemaphoreType.DMA((2,)),
            pltpu.SemaphoreType.DMA((2,)),
            pltpu.SemaphoreType.DMA((2, 4)),
            pltpu.SemaphoreType.DMA((2, 4)),
        ],
        compiler_params=pltpu.CompilerParams(collective_id=2, has_side_effects=True),
    )(x)


def exchange(x, n, scatter, collective_id):
    if scatter:
        out_shape = x.shape
    else:
        out_shape = (x.shape[0], n) + x.shape[1:]
    return pl.pallas_call(
        functools.partial(exchange_kernel, n, scatter),
        out_shape=jax.ShapeDtypeStruct(out_shape, x.dtype),
        in_specs=[pl.BlockSpec(memory_space=pl.ANY)],
        out_specs=pl.BlockSpec(memory_space=pl.ANY),
        scratch_shapes=[
            pltpu.SemaphoreType.DMA((n,)),
            pltpu.SemaphoreType.DMA((n,)),
            pltpu.SemaphoreType.DMA(()),
        ],
        compiler_params=pltpu.CompilerParams(collective_id=collective_id, has_side_effects=True),
    )(x)


def shards(queries, image_tokens, key_weight, value_weight, cotangent, tile_counts, text_lengths):
    n_section = lax.axis_size("section")
    samples_here, chunk, model_width = image_tokens.shape
    if n_section == 8 and lax.axis_size("dp") == 16:
        gathered = relay_gather(image_tokens, n_section)
    else:
        gathered = exchange(image_tokens, n_section, False, 0)
    image_len = n_section * chunk
    tile_len = image_len // MAX_TILES
    w_key = key_weight[0]
    w_value = value_weight[0]
    query_local = queries[0]
    cotan_local = cotangent[0]
    query_list = []
    key_list = []
    value_list = []
    keys_all = jnp.einsum(
        "bjtd,dk->bjtk", gathered, w_key, preferred_element_type=jnp.float32
    ).astype(jnp.bfloat16).reshape(samples_here, image_len, -1)
    values_all = jnp.einsum(
        "bjtd,dk->bjtk", gathered, w_value, preferred_element_type=jnp.float32
    ).astype(jnp.bfloat16).reshape(samples_here, image_len, -1)
    for sample_index in range(samples_here):
        query_gradient, key_gradient, value_gradient = attend_one(
            query_local[sample_index],
            keys_all[sample_index],
            values_all[sample_index],
            cotan_local[sample_index],
            tile_counts[sample_index] * tile_len,
            text_lengths[sample_index],
        )
        query_list.append(query_gradient)
        key_list.append(key_gradient)
        value_list.append(value_gradient)
    query_out = jnp.stack(query_list)[None]
    key_grads = jnp.stack(key_list).reshape(samples_here, n_section, chunk, -1)
    value_grads = jnp.stack(value_list).reshape(samples_here, n_section, chunk, -1)
    kv_grads = jnp.concatenate([key_grads, value_grads], axis=-1)
    kv_term = jnp.einsum(
        "bjtd,bjtk->dk", gathered, kv_grads, preferred_element_type=jnp.float32
    )
    kv_sum = lax.psum_scatter(kv_term.astype(jnp.bfloat16), "dp", scatter_dimension=0, tiled=True)
    kv_width = key_grads.shape[-1]
    image_term = jnp.einsum(
        "bjtk,dk->bjtd", key_grads, w_key, preferred_element_type=jnp.float32
    )
    image_term = image_term + jnp.einsum(
        "bjtk,dk->bjtd", value_grads, w_value, preferred_element_type=jnp.float32
    )
    received = exchange(image_term.astype(jnp.bfloat16), n_section, True, 1)
    image_out = jnp.sum(received.astype(jnp.float32), axis=1).astype(jnp.bfloat16)
    return (
        query_out,
        image_out,
        kv_sum[:, :kv_width][None],
        kv_sum[:, kv_width:][None],
    )


def solution(mesh):
    placed = (
        P("section", "dp", None, None),
        P("dp", "section", None),
        P("section", None, None),
        P("section", None, None),
        P("section", "dp", None, None),
        P("dp"),
        P("dp"),
    )
    return jax.shard_map(
        shards,
        mesh=mesh,
        in_specs=placed,
        out_specs=(
            P("section", "dp", None, None),
            P("dp", "section", None),
            P("section", "dp", None),
            P("section", "dp", None),
        ),
        check_vma=False,
    )
```

```python
import functools
import math

import jax
import jax.numpy as jnp
from jax import lax
from jax.experimental import pallas as pl
from jax.experimental.pallas import tpu as pltpu
from jax.sharding import PartitionSpec as P

QUERY_HEADS = 32
KEY_VALUE_HEADS = 4
HEAD_SIZE = 128
MAX_TILES = 4
MESH_ID = pl.DeviceIdType.MESH


def attend_one(queries, key_rows, value_rows, cotangent, key_limit, row_limit):
    total_rows = queries.shape[0]
    total_keys = key_rows.shape[0]
    group_width = QUERY_HEADS // KEY_VALUE_HEADS
    heads_of_queries = queries.reshape(total_rows, KEY_VALUE_HEADS, group_width, HEAD_SIZE)
    heads_of_keys = key_rows.reshape(total_keys, KEY_VALUE_HEADS, HEAD_SIZE)
    heads_of_values = value_rows.reshape(total_keys, KEY_VALUE_HEADS, HEAD_SIZE)
    row_live = (jnp.arange(total_rows) < row_limit)[:, None]
    active_cotangent = jnp.where(row_live, cotangent, jnp.zeros_like(cotangent))
    head_gradient = active_cotangent.reshape(total_rows, KEY_VALUE_HEADS, group_width, HEAD_SIZE)
    scaling = 1.0 / math.sqrt(HEAD_SIZE)
    scores = (
        jnp.einsum(
            "lhgd,nhd->hgln", heads_of_queries, heads_of_keys, preferred_element_type=jnp.float32
        )
        * scaling
    )
    key_live = jnp.arange(total_keys) < key_limit
    scores = jnp.where(key_live, scores, -jnp.inf)
    row_max = jnp.max(scores, axis=-1, keepdims=True)
    raised = jnp.exp(scores - row_max)
    weights = raised / jnp.sum(raised, axis=-1, keepdims=True)
    weights_low = weights.astype(jnp.bfloat16)
    value_gradient = jnp.einsum(
        "hgln,lhgd->nhd", weights_low, head_gradient, preferred_element_type=jnp.float32
    ).astype(jnp.bfloat16)
    prob_grad = jnp.einsum(
        "lhgd,nhd->hgln", head_gradient, heads_of_values, preferred_element_type=jnp.float32
    )
    row_dot = jnp.sum(weights * prob_grad, axis=-1, keepdims=True)
    score_grad = (weights * (prob_grad - row_dot) * scaling).astype(jnp.bfloat16)
    query_gradient = jnp.einsum(
        "hgln,nhd->lhgd", score_grad, heads_of_keys, preferred_element_type=jnp.float32
    ).astype(jnp.bfloat16)
    key_gradient = jnp.einsum(
        "hgln,lhgd->nhd", score_grad, heads_of_queries, preferred_element_type=jnp.float32
    ).astype(jnp.bfloat16)
    return (
        query_gradient.reshape(total_rows, QUERY_HEADS * HEAD_SIZE),
        key_gradient.reshape(total_keys, KEY_VALUE_HEADS * HEAD_SIZE),
        value_gradient.reshape(total_keys, KEY_VALUE_HEADS * HEAD_SIZE),
    )


def exchange_kernel(n, scatter, x_ref, o_ref, send_sems, recv_sems, local_sem):
    me = lax.axis_index("section")
    row = lax.axis_index("dp")
    barrier = pltpu.get_barrier_semaphore()
    for k in range(1, n):
        pl.semaphore_signal(
            barrier, inc=1, device_id=(lax.rem(me + k, n), row), device_id_type=MESH_ID
        )
    pl.semaphore_wait(barrier, n - 1)
    own = x_ref.at[:, me] if scatter else x_ref
    local = pltpu.make_async_copy(own, o_ref.at[:, me], local_sem)
    local.start()
    copies = []
    for k in range(1, n):
        peer = lax.rem(me + k, n)
        src = x_ref.at[:, peer] if scatter else x_ref
        copy = pltpu.make_async_remote_copy(
            src_ref=src,
            dst_ref=o_ref.at[:, me],
            send_sem=send_sems.at[k],
            recv_sem=recv_sems.at[k],
            device_id=(peer, row),
            device_id_type=MESH_ID,
        )
        copy.start()
        copies.append(copy)
    for copy in copies:
        copy.wait()
    local.wait()


def relay_gather_kernel(x_ref, o_ref, stage, local_sem, direct_send, direct_recv,
                        hop_send, hop_recv, fwd_send, fwd_recv):
    s = lax.axis_index("section")
    r = lax.axis_index("dp")
    y = lax.rem(s, 4)
    z = (s // 4) * 2 + r // 8
    xc = lax.rem(r, 8)
    half = x_ref.shape[-1] // 2

    def sec(zz, yy):
        return (lax.rem(zz, 4) // 2) * 4 + yy

    def dpi(zz):
        return lax.rem(zz, 2) * 8 + xc

    up, down = z + 1, z + 3
    peers = [(sec(z, lax.rem(y + j, 4)), r) for j in range(1, 4)]
    for yy in range(4):
        peers.append((sec(up, yy), dpi(up)))
        peers.append((sec(down, yy), dpi(down)))
    barrier = pltpu.get_barrier_semaphore()
    for peer in peers:
        pl.semaphore_signal(barrier, inc=1, device_id=peer, device_id_type=MESH_ID)
    pl.semaphore_wait(barrier, len(peers))

    local = pltpu.make_async_copy(x_ref, o_ref.at[:, s], local_sem)
    local.start()
    sends = []
    for j in range(1, 4):
        copy = pltpu.make_async_remote_copy(
            src_ref=x_ref,
            dst_ref=o_ref.at[:, s],
            send_sem=direct_send.at[j],
            recv_sem=direct_recv.at[j],
            device_id=peers[j - 1],
            device_id_type=MESH_ID,
        )
        copy.start()
        sends.append(copy)
    hops = []
    for side, (target, lanes) in enumerate(((up, pl.ds(0, half)), (down, pl.ds(half, half)))):
        copy = pltpu.make_async_remote_copy(
            src_ref=x_ref.at[:, :, lanes],
            dst_ref=stage.at[side],
            send_sem=hop_send.at[side],
            recv_sem=hop_recv.at[side],
            device_id=(sec(target, y), dpi(target)),
            device_id_type=MESH_ID,
        )
        copy.start()
        hops.append(copy)
    forwards = []
    for side, (origin, target, lanes) in enumerate(
        ((down, up, pl.ds(0, half)), (up, down, pl.ds(half, half)))
    ):
        hops[side].wait_recv()
        for yy in range(4):
            copy = pltpu.make_async_remote_copy(
                src_ref=stage.at[side],
                dst_ref=o_ref.at[:, sec(origin, y), :, lanes],
                send_sem=fwd_send.at[side, yy],
                recv_sem=fwd_recv.at[side, y],
                device_id=(sec(target, yy), dpi(target)),
                device_id_type=MESH_ID,
            )
            copy.start()
            forwards.append(copy)
    for copy in sends:
        copy.wait()
    for copy in hops:
        copy.wait_send()
    for copy in forwards:
        copy.wait_send()
    for side, (origin, target, lanes) in enumerate(
        ((down, up, pl.ds(0, half)), (up, down, pl.ds(half, half)))
    ):
        for yy in range(4):
            pltpu.make_async_remote_copy(
                src_ref=stage.at[side],
                dst_ref=o_ref.at[:, sec(origin, y), :, lanes],
                send_sem=fwd_send.at[side, yy],
                recv_sem=fwd_recv.at[side, yy],
                device_id=(sec(target, yy), dpi(target)),
                device_id_type=MESH_ID,
            ).wait_recv()
    local.wait()


def relay_gather(x, n):
    samples, chunk, width = x.shape
    return pl.pallas_call(
        relay_gather_kernel,
        out_shape=jax.ShapeDtypeStruct((samples, n, chunk, width), x.dtype),
        in_specs=[pl.BlockSpec(memory_space=pl.ANY)],
        out_specs=pl.BlockSpec(memory_space=pl.ANY),
        scratch_shapes=[
            pltpu.VMEM((2, samples, chunk, width // 2), x.dtype),
            pltpu.SemaphoreType.DMA(()),
            pltpu.SemaphoreType.DMA((4,)),
            pltpu.SemaphoreType.DMA((4,)),
            pltpu.SemaphoreType.DMA((2,)),
            pltpu.SemaphoreType.DMA((2,)),
            pltpu.SemaphoreType.DMA((2, 4)),
            pltpu.SemaphoreType.DMA((2, 4)),
        ],
        compiler_params=pltpu.CompilerParams(collective_id=2, has_side_effects=True),
    )(x)


def exchange(x, n, scatter, collective_id):
    if scatter:
        out_shape = x.shape
    else:
        out_shape = (x.shape[0], n) + x.shape[1:]
    return pl.pallas_call(
        functools.partial(exchange_kernel, n, scatter),
        out_shape=jax.ShapeDtypeStruct(out_shape, x.dtype),
        in_specs=[pl.BlockSpec(memory_space=pl.ANY)],
        out_specs=pl.BlockSpec(memory_space=pl.ANY),
        scratch_shapes=[
            pltpu.SemaphoreType.DMA((n,)),
            pltpu.SemaphoreType.DMA((n,)),
            pltpu.SemaphoreType.DMA(()),
        ],
        compiler_params=pltpu.CompilerParams(collective_id=collective_id, has_side_effects=True),
    )(x)


def shards(queries, image_tokens, key_weight, value_weight, cotangent, tile_counts, text_lengths):
    n_section = lax.axis_size("section")
    samples_here, chunk, model_width = image_tokens.shape
    image_len = n_section * chunk
    tile_len = image_len // MAX_TILES
    w_key = key_weight[0]
    w_value = value_weight[0]
    query_local = queries[0]
    cotan_local = cotangent[0]
    late = [
        lax.all_gather(image_tokens[i], "section", axis=0, tiled=True)
        for i in range(1, samples_here)
    ]
    if n_section == 8 and lax.axis_size("dp") == 16:
        first = relay_gather(image_tokens[:1], n_section)
    else:
        first = exchange(image_tokens[:1], n_section, False, 0)
    token_list = [first.reshape(image_len, model_width)] + late
    query_list = []
    kv_term = None
    image_list = []
    for sample_index in range(samples_here):
        tokens = token_list[sample_index]
        keys = jnp.dot(tokens, w_key, preferred_element_type=jnp.float32).astype(jnp.bfloat16)
        values = jnp.dot(tokens, w_value, preferred_element_type=jnp.float32).astype(jnp.bfloat16)
        query_gradient, key_gradient, value_gradient = attend_one(
            query_local[sample_index],
            keys,
            values,
            cotan_local[sample_index],
            tile_counts[sample_index] * tile_len,
            text_lengths[sample_index],
        )
        query_list.append(query_gradient)
        kv_grads = jnp.concatenate([key_gradient, value_gradient], axis=-1)
        part = jnp.einsum("td,tk->dk", tokens, kv_grads, preferred_element_type=jnp.float32)
        kv_term = part if kv_term is None else kv_term + part
        term = jnp.einsum("tk,dk->td", key_gradient, w_key, preferred_element_type=jnp.float32)
        term = term + jnp.einsum("tk,dk->td", value_gradient, w_value, preferred_element_type=jnp.float32)
        image_list.append(term.astype(jnp.bfloat16).reshape(n_section, chunk, model_width))
    query_out = jnp.stack(query_list)[None]
    kv_sum = lax.psum_scatter(kv_term.astype(jnp.bfloat16), "dp", scatter_dimension=0, tiled=True)
    kv_width = kv_sum.shape[-1] // 2
    received = exchange(jnp.stack(image_list), n_section, True, 1)
    image_out = jnp.sum(received.astype(jnp.float32), axis=1).astype(jnp.bfloat16)
    return (
        query_out,
        image_out,
        kv_sum[:, :kv_width][None],
        kv_sum[:, kv_width:][None],
    )


def solution(mesh):
    placed = (
        P("section", "dp", None, None),
        P("dp", "section", None),
        P("section", None, None),
        P("section", None, None),
        P("section", "dp", None, None),
        P("dp"),
        P("dp"),
    )
    return jax.shard_map(
        shards,
        mesh=mesh,
        in_specs=placed,
        out_specs=(
            P("section", "dp", None, None),
            P("dp", "section", None),
            P("section", "dp", None),
            P("section", "dp", None),
        ),
        check_vma=False,
    )
```

```python
import functools
import math

import jax
import jax.numpy as jnp
from jax import lax
from jax.experimental import pallas as pl
from jax.experimental.pallas import tpu as pltpu
from jax.sharding import PartitionSpec as P

QUERY_HEADS = 32
KEY_VALUE_HEADS = 4
HEAD_SIZE = 128
MAX_TILES = 4
MESH_ID = pl.DeviceIdType.MESH


def attend_one(queries, key_rows, value_rows, cotangent, key_limit, row_limit):
    total_rows = queries.shape[0]
    total_keys = key_rows.shape[0]
    group_width = QUERY_HEADS // KEY_VALUE_HEADS
    heads_of_queries = queries.reshape(total_rows, KEY_VALUE_HEADS, group_width, HEAD_SIZE)
    heads_of_keys = key_rows.reshape(total_keys, KEY_VALUE_HEADS, HEAD_SIZE)
    heads_of_values = value_rows.reshape(total_keys, KEY_VALUE_HEADS, HEAD_SIZE)
    row_live = (jnp.arange(total_rows) < row_limit)[:, None]
    active_cotangent = jnp.where(row_live, cotangent, jnp.zeros_like(cotangent))
    head_gradient = active_cotangent.reshape(total_rows, KEY_VALUE_HEADS, group_width, HEAD_SIZE)
    scaling = 1.0 / math.sqrt(HEAD_SIZE)
    scores = (
        jnp.einsum(
            "lhgd,nhd->hgln", heads_of_queries, heads_of_keys, preferred_element_type=jnp.float32
        )
        * scaling
    )
    key_live = jnp.arange(total_keys) < key_limit
    scores = jnp.where(key_live, scores, -jnp.inf)
    row_max = jnp.max(scores, axis=-1, keepdims=True)
    raised = jnp.exp(scores - row_max)
    weights = raised / jnp.sum(raised, axis=-1, keepdims=True)
    weights_low = weights.astype(jnp.bfloat16)
    value_gradient = jnp.einsum(
        "hgln,lhgd->nhd", weights_low, head_gradient, preferred_element_type=jnp.float32
    ).astype(jnp.bfloat16)
    prob_grad = jnp.einsum(
        "lhgd,nhd->hgln", head_gradient, heads_of_values, preferred_element_type=jnp.float32
    )
    row_dot = jnp.sum(weights * prob_grad, axis=-1, keepdims=True)
    score_grad = (weights * (prob_grad - row_dot) * scaling).astype(jnp.bfloat16)
    query_gradient = jnp.einsum(
        "hgln,nhd->lhgd", score_grad, heads_of_keys, preferred_element_type=jnp.float32
    ).astype(jnp.bfloat16)
    key_gradient = jnp.einsum(
        "hgln,lhgd->nhd", score_grad, heads_of_queries, preferred_element_type=jnp.float32
    ).astype(jnp.bfloat16)
    return (
        query_gradient.reshape(total_rows, QUERY_HEADS * HEAD_SIZE),
        key_gradient.reshape(total_keys, KEY_VALUE_HEADS * HEAD_SIZE),
        value_gradient.reshape(total_keys, KEY_VALUE_HEADS * HEAD_SIZE),
    )


def exchange_kernel(n, scatter, x_ref, o_ref, send_sems, recv_sems, local_sem):
    me = lax.axis_index("section")
    row = lax.axis_index("dp")
    barrier = pltpu.get_barrier_semaphore()
    for k in range(1, n):
        pl.semaphore_signal(
            barrier, inc=1, device_id=(lax.rem(me + k, n), row), device_id_type=MESH_ID
        )
    pl.semaphore_wait(barrier, n - 1)
    own = x_ref.at[:, me] if scatter else x_ref
    local = pltpu.make_async_copy(own, o_ref.at[:, me], local_sem)
    local.start()
    copies = []
    for k in range(1, n):
        peer = lax.rem(me + k, n)
        src = x_ref.at[:, peer] if scatter else x_ref
        copy = pltpu.make_async_remote_copy(
            src_ref=src,
            dst_ref=o_ref.at[:, me],
            send_sem=send_sems.at[k],
            recv_sem=recv_sems.at[k],
            device_id=(peer, row),
            device_id_type=MESH_ID,
        )
        copy.start()
        copies.append(copy)
    for copy in copies:
        copy.wait()
    local.wait()


def relay_gather_kernel(x_ref, o_ref, stage, local_sem, direct_send, direct_recv,
                        hop_send, hop_recv, fwd_send, fwd_recv):
    s = lax.axis_index("section")
    r = lax.axis_index("dp")
    y = lax.rem(s, 4)
    z = (s // 4) * 2 + r // 8
    xc = lax.rem(r, 8)
    half = x_ref.shape[-1] // 2

    def sec(zz, yy):
        return (lax.rem(zz, 4) // 2) * 4 + yy

    def dpi(zz):
        return lax.rem(zz, 2) * 8 + xc

    up, down = z + 1, z + 3
    peers = [(sec(z, lax.rem(y + j, 4)), r) for j in range(1, 4)]
    for yy in range(4):
        peers.append((sec(up, yy), dpi(up)))
        peers.append((sec(down, yy), dpi(down)))
    barrier = pltpu.get_barrier_semaphore()
    for peer in peers:
        pl.semaphore_signal(barrier, inc=1, device_id=peer, device_id_type=MESH_ID)
    pl.semaphore_wait(barrier, len(peers))

    local = pltpu.make_async_copy(x_ref, o_ref.at[:, s], local_sem)
    local.start()
    sends = []
    for j in range(1, 4):
        copy = pltpu.make_async_remote_copy(
            src_ref=x_ref,
            dst_ref=o_ref.at[:, s],
            send_sem=direct_send.at[j],
            recv_sem=direct_recv.at[j],
            device_id=peers[j - 1],
            device_id_type=MESH_ID,
        )
        copy.start()
        sends.append(copy)
    hops = []
    for side, (target, lanes) in enumerate(((up, pl.ds(0, half)), (down, pl.ds(half, half)))):
        copy = pltpu.make_async_remote_copy(
            src_ref=x_ref.at[:, :, lanes],
            dst_ref=stage.at[side],
            send_sem=hop_send.at[side],
            recv_sem=hop_recv.at[side],
            device_id=(sec(target, y), dpi(target)),
            device_id_type=MESH_ID,
        )
        copy.start()
        hops.append(copy)
    forwards = []
    for side, (origin, target, lanes) in enumerate(
        ((down, up, pl.ds(0, half)), (up, down, pl.ds(half, half)))
    ):
        hops[side].wait_recv()
        for yy in range(4):
            copy = pltpu.make_async_remote_copy(
                src_ref=stage.at[side],
                dst_ref=o_ref.at[:, sec(origin, y), :, lanes],
                send_sem=fwd_send.at[side, yy],
                recv_sem=fwd_recv.at[side, y],
                device_id=(sec(target, yy), dpi(target)),
                device_id_type=MESH_ID,
            )
            copy.start()
            forwards.append(copy)
    for copy in sends:
        copy.wait()
    for copy in hops:
        copy.wait_send()
    for copy in forwards:
        copy.wait_send()
    for side, (origin, target, lanes) in enumerate(
        ((down, up, pl.ds(0, half)), (up, down, pl.ds(half, half)))
    ):
        for yy in range(4):
            pltpu.make_async_remote_copy(
                src_ref=stage.at[side],
                dst_ref=o_ref.at[:, sec(origin, y), :, lanes],
                send_sem=fwd_send.at[side, yy],
                recv_sem=fwd_recv.at[side, yy],
                device_id=(sec(target, yy), dpi(target)),
                device_id_type=MESH_ID,
            ).wait_recv()
    local.wait()


def relay_gather(x, n):
    samples, chunk, width = x.shape
    return pl.pallas_call(
        relay_gather_kernel,
        out_shape=jax.ShapeDtypeStruct((samples, n, chunk, width), x.dtype),
        in_specs=[pl.BlockSpec(memory_space=pl.ANY)],
        out_specs=pl.BlockSpec(memory_space=pl.ANY),
        scratch_shapes=[
            pltpu.VMEM((2, samples, chunk, width // 2), x.dtype),
            pltpu.SemaphoreType.DMA(()),
            pltpu.SemaphoreType.DMA((4,)),
            pltpu.SemaphoreType.DMA((4,)),
            pltpu.SemaphoreType.DMA((2,)),
            pltpu.SemaphoreType.DMA((2,)),
            pltpu.SemaphoreType.DMA((2, 4)),
            pltpu.SemaphoreType.DMA((2, 4)),
        ],
        compiler_params=pltpu.CompilerParams(collective_id=2, has_side_effects=True),
    )(x)


def exchange(x, n, scatter, collective_id):
    if scatter:
        out_shape = x.shape
    else:
        out_shape = (x.shape[0], n) + x.shape[1:]
    return pl.pallas_call(
        functools.partial(exchange_kernel, n, scatter),
        out_shape=jax.ShapeDtypeStruct(out_shape, x.dtype),
        in_specs=[pl.BlockSpec(memory_space=pl.ANY)],
        out_specs=pl.BlockSpec(memory_space=pl.ANY),
        scratch_shapes=[
            pltpu.SemaphoreType.DMA((n,)),
            pltpu.SemaphoreType.DMA((n,)),
            pltpu.SemaphoreType.DMA(()),
        ],
        compiler_params=pltpu.CompilerParams(collective_id=collective_id, has_side_effects=True),
    )(x)


def shards(queries, image_tokens, key_weight, value_weight, cotangent, tile_counts, text_lengths):
    n_section = lax.axis_size("section")
    samples_here, chunk, model_width = image_tokens.shape
    image_len = n_section * chunk
    tile_len = image_len // MAX_TILES
    w_key = key_weight[0]
    w_value = value_weight[0]
    query_local = queries[0]
    cotan_local = cotangent[0]
    late = [
        lax.all_gather(image_tokens[i], "section", axis=0, tiled=True)
        for i in range(1, samples_here)
    ]
    if n_section == 8 and lax.axis_size("dp") == 16:
        first = relay_gather(image_tokens[:1], n_section)
    else:
        first = exchange(image_tokens[:1], n_section, False, 0)
    token_list = [first.reshape(image_len, model_width)] + late
    query_list = []
    key_list = []
    value_list = []
    image_list = []
    for sample_index in range(samples_here):
        tokens = token_list[sample_index]
        keys = jnp.dot(tokens, w_key, preferred_element_type=jnp.float32).astype(jnp.bfloat16)
        values = jnp.dot(tokens, w_value, preferred_element_type=jnp.float32).astype(jnp.bfloat16)
        query_gradient, key_gradient, value_gradient = attend_one(
            query_local[sample_index],
            keys,
            values,
            cotan_local[sample_index],
            tile_counts[sample_index] * tile_len,
            text_lengths[sample_index],
        )
        query_list.append(query_gradient)
        key_list.append(key_gradient)
        value_list.append(value_gradient)
        term = jnp.einsum("tk,dk->td", key_gradient, w_key, preferred_element_type=jnp.float32)
        term = term + jnp.einsum("tk,dk->td", value_gradient, w_value, preferred_element_type=jnp.float32)
        image_list.append(term.astype(jnp.bfloat16).reshape(n_section, chunk, model_width))
    all_tokens = jnp.concatenate(token_list, axis=0)
    value_term = jnp.einsum(
        "td,tk->dk", all_tokens, jnp.concatenate(value_list, axis=0),
        preferred_element_type=jnp.float32,
    ).astype(jnp.bfloat16)
    value_sum = lax.psum_scatter(value_term, "dp", scatter_dimension=0, tiled=True)
    key_term = jnp.einsum(
        "td,tk->dk", all_tokens, jnp.concatenate(key_list, axis=0),
        preferred_element_type=jnp.float32,
    ).astype(jnp.bfloat16)
    key_sum = lax.psum_scatter(key_term, "dp", scatter_dimension=0, tiled=True)
    query_out = jnp.stack(query_list)[None]
    received = exchange(jnp.stack(image_list), n_section, True, 1)
    image_out = jnp.sum(received.astype(jnp.float32), axis=1).astype(jnp.bfloat16)
    return (
        query_out,
        image_out,
        key_sum[None],
        value_sum[None],
    )


def solution(mesh):
    placed = (
        P("section", "dp", None, None),
        P("dp", "section", None),
        P("section", None, None),
        P("section", None, None),
        P("section", "dp", None, None),
        P("dp"),
        P("dp"),
    )
    return jax.shard_map(
        shards,
        mesh=mesh,
        in_specs=placed,
        out_specs=(
            P("section", "dp", None, None),
            P("dp", "section", None),
            P("section", "dp", None),
            P("section", "dp", None),
        ),
        check_vma=False,
    )
```

```python
import functools
import math

import jax
import jax.numpy as jnp
from jax import lax
from jax.experimental import pallas as pl
from jax.experimental.pallas import tpu as pltpu
from jax.sharding import PartitionSpec as P

QUERY_HEADS = 32
KEY_VALUE_HEADS = 4
HEAD_SIZE = 128
MAX_TILES = 4
MESH_ID = pl.DeviceIdType.MESH


def attend_one(queries, key_rows, value_rows, cotangent, key_limit, row_limit):
    total_rows = queries.shape[0]
    total_keys = key_rows.shape[0]
    group_width = QUERY_HEADS // KEY_VALUE_HEADS
    heads_of_queries = queries.reshape(total_rows, KEY_VALUE_HEADS, group_width, HEAD_SIZE)
    heads_of_keys = key_rows.reshape(total_keys, KEY_VALUE_HEADS, HEAD_SIZE)
    heads_of_values = value_rows.reshape(total_keys, KEY_VALUE_HEADS, HEAD_SIZE)
    row_live = (jnp.arange(total_rows) < row_limit)[:, None]
    active_cotangent = jnp.where(row_live, cotangent, jnp.zeros_like(cotangent))
    head_gradient = active_cotangent.reshape(total_rows, KEY_VALUE_HEADS, group_width, HEAD_SIZE)
    scaling = 1.0 / math.sqrt(HEAD_SIZE)
    scores = (
        jnp.einsum(
            "lhgd,nhd->hgln", heads_of_queries, heads_of_keys, preferred_element_type=jnp.float32
        )
        * scaling
    )
    key_live = jnp.arange(total_keys) < key_limit
    scores = jnp.where(key_live, scores, -jnp.inf)
    row_max = jnp.max(scores, axis=-1, keepdims=True)
    raised = jnp.exp(scores - row_max)
    weights = raised / jnp.sum(raised, axis=-1, keepdims=True)
    weights_low = weights.astype(jnp.bfloat16)
    value_gradient = jnp.einsum(
        "hgln,lhgd->nhd", weights_low, head_gradient, preferred_element_type=jnp.float32
    ).astype(jnp.bfloat16)
    prob_grad = jnp.einsum(
        "lhgd,nhd->hgln", head_gradient, heads_of_values, preferred_element_type=jnp.float32
    )
    row_dot = jnp.sum(weights * prob_grad, axis=-1, keepdims=True)
    score_grad = (weights * (prob_grad - row_dot) * scaling).astype(jnp.bfloat16)
    query_gradient = jnp.einsum(
        "hgln,nhd->lhgd", score_grad, heads_of_keys, preferred_element_type=jnp.float32
    ).astype(jnp.bfloat16)
    key_gradient = jnp.einsum(
        "hgln,lhgd->nhd", score_grad, heads_of_queries, preferred_element_type=jnp.float32
    ).astype(jnp.bfloat16)
    return (
        query_gradient.reshape(total_rows, QUERY_HEADS * HEAD_SIZE),
        key_gradient.reshape(total_keys, KEY_VALUE_HEADS * HEAD_SIZE),
        value_gradient.reshape(total_keys, KEY_VALUE_HEADS * HEAD_SIZE),
    )


def exchange_kernel(n, scatter, x_ref, o_ref, send_sems, recv_sems, local_sem):
    me = lax.axis_index("section")
    row = lax.axis_index("dp")
    barrier = pltpu.get_barrier_semaphore()
    for k in range(1, n):
        pl.semaphore_signal(
            barrier, inc=1, device_id=(lax.rem(me + k, n), row), device_id_type=MESH_ID
        )
    pl.semaphore_wait(barrier, n - 1)
    own = x_ref.at[:, me] if scatter else x_ref
    local = pltpu.make_async_copy(own, o_ref.at[:, me], local_sem)
    local.start()
    copies = []
    for k in range(1, n):
        peer = lax.rem(me + k, n)
        src = x_ref.at[:, peer] if scatter else x_ref
        copy = pltpu.make_async_remote_copy(
            src_ref=src,
            dst_ref=o_ref.at[:, me],
            send_sem=send_sems.at[k],
            recv_sem=recv_sems.at[k],
            device_id=(peer, row),
            device_id_type=MESH_ID,
        )
        copy.start()
        copies.append(copy)
    for copy in copies:
        copy.wait()
    local.wait()


def relay_gather_kernel(x_ref, o_ref, stage, local_sem, direct_send, direct_recv,
                        hop_send, hop_recv, fwd_send, fwd_recv):
    s = lax.axis_index("section")
    r = lax.axis_index("dp")
    y = lax.rem(s, 4)
    z = (s // 4) * 2 + r // 8
    xc = lax.rem(r, 8)
    half = x_ref.shape[-1] // 2

    def sec(zz, yy):
        return (lax.rem(zz, 4) // 2) * 4 + yy

    def dpi(zz):
        return lax.rem(zz, 2) * 8 + xc

    up, down = z + 1, z + 3
    peers = [(sec(z, lax.rem(y + j, 4)), r) for j in range(1, 4)]
    for yy in range(4):
        peers.append((sec(up, yy), dpi(up)))
        peers.append((sec(down, yy), dpi(down)))
    barrier = pltpu.get_barrier_semaphore()
    for peer in peers:
        pl.semaphore_signal(barrier, inc=1, device_id=peer, device_id_type=MESH_ID)
    pl.semaphore_wait(barrier, len(peers))

    local = pltpu.make_async_copy(x_ref, o_ref.at[:, s], local_sem)
    local.start()
    sends = []
    for j in range(1, 4):
        copy = pltpu.make_async_remote_copy(
            src_ref=x_ref,
            dst_ref=o_ref.at[:, s],
            send_sem=direct_send.at[j],
            recv_sem=direct_recv.at[j],
            device_id=peers[j - 1],
            device_id_type=MESH_ID,
        )
        copy.start()
        sends.append(copy)
    hops = []
    for side, (target, lanes) in enumerate(((up, pl.ds(0, half)), (down, pl.ds(half, half)))):
        copy = pltpu.make_async_remote_copy(
            src_ref=x_ref.at[:, :, lanes],
            dst_ref=stage.at[side],
            send_sem=hop_send.at[side],
            recv_sem=hop_recv.at[side],
            device_id=(sec(target, y), dpi(target)),
            device_id_type=MESH_ID,
        )
        copy.start()
        hops.append(copy)
    forwards = []
    for side, (origin, target, lanes) in enumerate(
        ((down, up, pl.ds(0, half)), (up, down, pl.ds(half, half)))
    ):
        hops[side].wait_recv()
        for yy in range(4):
            copy = pltpu.make_async_remote_copy(
                src_ref=stage.at[side],
                dst_ref=o_ref.at[:, sec(origin, y), :, lanes],
                send_sem=fwd_send.at[side, yy],
                recv_sem=fwd_recv.at[side, y],
                device_id=(sec(target, yy), dpi(target)),
                device_id_type=MESH_ID,
            )
            copy.start()
            forwards.append(copy)
    for copy in sends:
        copy.wait()
    for copy in hops:
        copy.wait_send()
    for copy in forwards:
        copy.wait_send()
    for side, (origin, target, lanes) in enumerate(
        ((down, up, pl.ds(0, half)), (up, down, pl.ds(half, half)))
    ):
        for yy in range(4):
            pltpu.make_async_remote_copy(
                src_ref=stage.at[side],
                dst_ref=o_ref.at[:, sec(origin, y), :, lanes],
                send_sem=fwd_send.at[side, yy],
                recv_sem=fwd_recv.at[side, yy],
                device_id=(sec(target, yy), dpi(target)),
                device_id_type=MESH_ID,
            ).wait_recv()
    local.wait()


def relay_gather(x, n):
    samples, chunk, width = x.shape
    return pl.pallas_call(
        relay_gather_kernel,
        out_shape=jax.ShapeDtypeStruct((samples, n, chunk, width), x.dtype),
        in_specs=[pl.BlockSpec(memory_space=pl.ANY)],
        out_specs=pl.BlockSpec(memory_space=pl.ANY),
        scratch_shapes=[
            pltpu.VMEM((2, samples, chunk, width // 2), x.dtype),
            pltpu.SemaphoreType.DMA(()),
            pltpu.SemaphoreType.DMA((4,)),
            pltpu.SemaphoreType.DMA((4,)),
            pltpu.SemaphoreType.DMA((2,)),
            pltpu.SemaphoreType.DMA((2,)),
            pltpu.SemaphoreType.DMA((2, 4)),
            pltpu.SemaphoreType.DMA((2, 4)),
        ],
        compiler_params=pltpu.CompilerParams(collective_id=2, has_side_effects=True),
    )(x)


def exchange(x, n, scatter, collective_id):
    if scatter:
        out_shape = x.shape
    else:
        out_shape = (x.shape[0], n) + x.shape[1:]
    return pl.pallas_call(
        functools.partial(exchange_kernel, n, scatter),
        out_shape=jax.ShapeDtypeStruct(out_shape, x.dtype),
        in_specs=[pl.BlockSpec(memory_space=pl.ANY)],
        out_specs=pl.BlockSpec(memory_space=pl.ANY),
        scratch_shapes=[
            pltpu.SemaphoreType.DMA((n,)),
            pltpu.SemaphoreType.DMA((n,)),
            pltpu.SemaphoreType.DMA(()),
        ],
        compiler_params=pltpu.CompilerParams(collective_id=collective_id, has_side_effects=True),
    )(x)


def scatter_by_permutes(blocks, n):
    me = lax.axis_index("section")
    total = lax.dynamic_index_in_dim(blocks, me, axis=0, keepdims=False).astype(jnp.float32)
    for k in range(1, n):
        outgoing = lax.dynamic_index_in_dim(blocks, lax.rem(me + k, n), axis=0, keepdims=False)
        incoming = lax.ppermute(outgoing, "section", perm=[(i, (i + k) % n) for i in range(n)])
        total = total + incoming.astype(jnp.float32)
    return total.astype(jnp.bfloat16)


def shards(queries, image_tokens, key_weight, value_weight, cotangent, tile_counts, text_lengths):
    n_section = lax.axis_size("section")
    samples_here, chunk, model_width = image_tokens.shape
    image_len = n_section * chunk
    tile_len = image_len // MAX_TILES
    w_key = key_weight[0]
    w_value = value_weight[0]
    query_local = queries[0]
    cotan_local = cotangent[0]
    late = [
        lax.all_gather(image_tokens[i], "section", axis=0, tiled=True)
        for i in range(1, samples_here)
    ]
    if n_section == 8 and lax.axis_size("dp") == 16:
        first = relay_gather(image_tokens[:1], n_section)
    else:
        first = exchange(image_tokens[:1], n_section, False, 0)
    token_list = [first.reshape(image_len, model_width)] + late
    query_list = []
    key_list = []
    value_list = []
    image_list = []
    for sample_index in range(samples_here):
        tokens = token_list[sample_index]
        keys = jnp.dot(tokens, w_key, preferred_element_type=jnp.float32).astype(jnp.bfloat16)
        values = jnp.dot(tokens, w_value, preferred_element_type=jnp.float32).astype(jnp.bfloat16)
        query_gradient, key_gradient, value_gradient = attend_one(
            query_local[sample_index],
            keys,
            values,
            cotan_local[sample_index],
            tile_counts[sample_index] * tile_len,
            text_lengths[sample_index],
        )
        query_list.append(query_gradient)
        key_list.append(key_gradient)
        value_list.append(value_gradient)
        term = jnp.einsum("tk,dk->td", key_gradient, w_key, preferred_element_type=jnp.float32)
        term = term + jnp.einsum("tk,dk->td", value_gradient, w_value, preferred_element_type=jnp.float32)
        image_list.append(term.astype(jnp.bfloat16).reshape(n_section, chunk, model_width))
        if sample_index == 0 and samples_here > 1:
            image_list[0], token_list[1] = lax.optimization_barrier((image_list[0], token_list[1]))
            image_list[0] = scatter_by_permutes(image_list[0], n_section)
    all_tokens = jnp.concatenate(token_list, axis=0)
    value_term = jnp.einsum(
        "td,tk->dk", all_tokens, jnp.concatenate(value_list, axis=0),
        preferred_element_type=jnp.float32,
    ).astype(jnp.bfloat16)
    value_sum = lax.psum_scatter(value_term, "dp", scatter_dimension=0, tiled=True)
    key_term = jnp.einsum(
        "td,tk->dk", all_tokens, jnp.concatenate(key_list, axis=0),
        preferred_element_type=jnp.float32,
    ).astype(jnp.bfloat16)
    key_sum = lax.psum_scatter(key_term, "dp", scatter_dimension=0, tiled=True)
    query_out = jnp.stack(query_list)[None]
    received = exchange(jnp.stack(image_list[1:]), n_section, True, 1)
    late_sums = jnp.sum(received.astype(jnp.float32), axis=1).astype(jnp.bfloat16)
    image_out = jnp.concatenate([image_list[0][None], late_sums], axis=0)
    return (
        query_out,
        image_out,
        key_sum[None],
        value_sum[None],
    )


def solution(mesh):
    placed = (
        P("section", "dp", None, None),
        P("dp", "section", None),
        P("section", None, None),
        P("section", None, None),
        P("section", "dp", None, None),
        P("dp"),
        P("dp"),
    )
    return jax.shard_map(
        shards,
        mesh=mesh,
        in_specs=placed,
        out_specs=(
            P("section", "dp", None, None),
            P("dp", "section", None),
            P("section", "dp", None),
            P("section", "dp", None),
        ),
        check_vma=False,
    )
```

```python
import functools
import math

import jax
import jax.numpy as jnp
from jax import lax
from jax.experimental import pallas as pl
from jax.experimental.pallas import tpu as pltpu
from jax.sharding import PartitionSpec as P

QUERY_HEADS = 32
KEY_VALUE_HEADS = 4
HEAD_SIZE = 128
MAX_TILES = 4
MESH_ID = pl.DeviceIdType.MESH


def attend_one(queries, key_rows, value_rows, cotangent, key_limit, row_limit):
    total_rows = queries.shape[0]
    total_keys = key_rows.shape[0]
    group_width = QUERY_HEADS // KEY_VALUE_HEADS
    heads_of_queries = queries.reshape(total_rows, KEY_VALUE_HEADS, group_width, HEAD_SIZE)
    heads_of_keys = key_rows.reshape(total_keys, KEY_VALUE_HEADS, HEAD_SIZE)
    heads_of_values = value_rows.reshape(total_keys, KEY_VALUE_HEADS, HEAD_SIZE)
    row_live = (jnp.arange(total_rows) < row_limit)[:, None]
    active_cotangent = jnp.where(row_live, cotangent, jnp.zeros_like(cotangent))
    head_gradient = active_cotangent.reshape(total_rows, KEY_VALUE_HEADS, group_width, HEAD_SIZE)
    scaling = 1.0 / math.sqrt(HEAD_SIZE)
    scores = (
        jnp.einsum(
            "lhgd,nhd->hgln", heads_of_queries, heads_of_keys, preferred_element_type=jnp.float32
        )
        * scaling
    )
    key_live = jnp.arange(total_keys) < key_limit
    scores = jnp.where(key_live, scores, -jnp.inf)
    row_max = jnp.max(scores, axis=-1, keepdims=True)
    raised = jnp.exp(scores - row_max)
    weights = raised / jnp.sum(raised, axis=-1, keepdims=True)
    weights_low = weights.astype(jnp.bfloat16)
    value_gradient = jnp.einsum(
        "hgln,lhgd->nhd", weights_low, head_gradient, preferred_element_type=jnp.float32
    ).astype(jnp.bfloat16)
    prob_grad = jnp.einsum(
        "lhgd,nhd->hgln", head_gradient, heads_of_values, preferred_element_type=jnp.float32
    )
    row_dot = jnp.sum(weights * prob_grad, axis=-1, keepdims=True)
    score_grad = (weights * (prob_grad - row_dot) * scaling).astype(jnp.bfloat16)
    query_gradient = jnp.einsum(
        "hgln,nhd->lhgd", score_grad, heads_of_keys, preferred_element_type=jnp.float32
    ).astype(jnp.bfloat16)
    key_gradient = jnp.einsum(
        "hgln,lhgd->nhd", score_grad, heads_of_queries, preferred_element_type=jnp.float32
    ).astype(jnp.bfloat16)
    return (
        query_gradient.reshape(total_rows, QUERY_HEADS * HEAD_SIZE),
        key_gradient.reshape(total_keys, KEY_VALUE_HEADS * HEAD_SIZE),
        value_gradient.reshape(total_keys, KEY_VALUE_HEADS * HEAD_SIZE),
    )


def exchange_kernel(n, scatter, x_ref, o_ref, send_sems, recv_sems, local_sem):
    me = lax.axis_index("section")
    row = lax.axis_index("dp")
    barrier = pltpu.get_barrier_semaphore()
    for k in range(1, n):
        pl.semaphore_signal(
            barrier, inc=1, device_id=(lax.rem(me + k, n), row), device_id_type=MESH_ID
        )
    pl.semaphore_wait(barrier, n - 1)
    own = x_ref.at[:, me] if scatter else x_ref
    local = pltpu.make_async_copy(own, o_ref.at[:, me], local_sem)
    local.start()
    copies = []
    for k in range(1, n):
        peer = lax.rem(me + k, n)
        src = x_ref.at[:, peer] if scatter else x_ref
        copy = pltpu.make_async_remote_copy(
            src_ref=src,
            dst_ref=o_ref.at[:, me],
            send_sem=send_sems.at[k],
            recv_sem=recv_sems.at[k],
            device_id=(peer, row),
            device_id_type=MESH_ID,
        )
        copy.start()
        copies.append(copy)
    for copy in copies:
        copy.wait()
    local.wait()


def relay_gather_kernel(x_ref, o_ref, stage, local_sem, direct_send, direct_recv,
                        hop_send, hop_recv, fwd_send, fwd_recv):
    s = lax.axis_index("section")
    r = lax.axis_index("dp")
    y = lax.rem(s, 4)
    z = (s // 4) * 2 + r // 8
    xc = lax.rem(r, 8)
    half = x_ref.shape[-1] // 2

    def sec(zz, yy):
        return (lax.rem(zz, 4) // 2) * 4 + yy

    def dpi(zz):
        return lax.rem(zz, 2) * 8 + xc

    up, down = z + 1, z + 3
    peers = [(sec(z, lax.rem(y + j, 4)), r) for j in range(1, 4)]
    for yy in range(4):
        peers.append((sec(up, yy), dpi(up)))
        peers.append((sec(down, yy), dpi(down)))
    barrier = pltpu.get_barrier_semaphore()
    for peer in peers:
        pl.semaphore_signal(barrier, inc=1, device_id=peer, device_id_type=MESH_ID)
    pl.semaphore_wait(barrier, len(peers))

    local = pltpu.make_async_copy(x_ref, o_ref.at[:, s], local_sem)
    local.start()
    sends = []
    for j in range(1, 4):
        copy = pltpu.make_async_remote_copy(
            src_ref=x_ref,
            dst_ref=o_ref.at[:, s],
            send_sem=direct_send.at[j],
            recv_sem=direct_recv.at[j],
            device_id=peers[j - 1],
            device_id_type=MESH_ID,
        )
        copy.start()
        sends.append(copy)
    hops = []
    for side, (target, lanes) in enumerate(((up, pl.ds(0, half)), (down, pl.ds(half, half)))):
        copy = pltpu.make_async_remote_copy(
            src_ref=x_ref.at[:, :, lanes],
            dst_ref=stage.at[side],
            send_sem=hop_send.at[side],
            recv_sem=hop_recv.at[side],
            device_id=(sec(target, y), dpi(target)),
            device_id_type=MESH_ID,
        )
        copy.start()
        hops.append(copy)
    forwards = []
    for side, (origin, target, lanes) in enumerate(
        ((down, up, pl.ds(0, half)), (up, down, pl.ds(half, half)))
    ):
        hops[side].wait_recv()
        for yy in range(4):
            copy = pltpu.make_async_remote_copy(
                src_ref=stage.at[side],
                dst_ref=o_ref.at[:, sec(origin, y), :, lanes],
                send_sem=fwd_send.at[side, yy],
                recv_sem=fwd_recv.at[side, y],
                device_id=(sec(target, yy), dpi(target)),
                device_id_type=MESH_ID,
            )
            copy.start()
            forwards.append(copy)
    for copy in sends:
        copy.wait()
    for copy in hops:
        copy.wait_send()
    for copy in forwards:
        copy.wait_send()
    for side, (origin, target, lanes) in enumerate(
        ((down, up, pl.ds(0, half)), (up, down, pl.ds(half, half)))
    ):
        for yy in range(4):
            pltpu.make_async_remote_copy(
                src_ref=stage.at[side],
                dst_ref=o_ref.at[:, sec(origin, y), :, lanes],
                send_sem=fwd_send.at[side, yy],
                recv_sem=fwd_recv.at[side, yy],
                device_id=(sec(target, yy), dpi(target)),
                device_id_type=MESH_ID,
            ).wait_recv()
    local.wait()


def relay_gather(x, n):
    samples, chunk, width = x.shape
    return pl.pallas_call(
        relay_gather_kernel,
        out_shape=jax.ShapeDtypeStruct((samples, n, chunk, width), x.dtype),
        in_specs=[pl.BlockSpec(memory_space=pl.ANY)],
        out_specs=pl.BlockSpec(memory_space=pl.ANY),
        scratch_shapes=[
            pltpu.VMEM((2, samples, chunk, width // 2), x.dtype),
            pltpu.SemaphoreType.DMA(()),
            pltpu.SemaphoreType.DMA((4,)),
            pltpu.SemaphoreType.DMA((4,)),
            pltpu.SemaphoreType.DMA((2,)),
            pltpu.SemaphoreType.DMA((2,)),
            pltpu.SemaphoreType.DMA((2, 4)),
            pltpu.SemaphoreType.DMA((2, 4)),
        ],
        compiler_params=pltpu.CompilerParams(collective_id=2, has_side_effects=True),
    )(x)


def exchange(x, n, scatter, collective_id):
    if scatter:
        out_shape = x.shape
    else:
        out_shape = (x.shape[0], n) + x.shape[1:]
    return pl.pallas_call(
        functools.partial(exchange_kernel, n, scatter),
        out_shape=jax.ShapeDtypeStruct(out_shape, x.dtype),
        in_specs=[pl.BlockSpec(memory_space=pl.ANY)],
        out_specs=pl.BlockSpec(memory_space=pl.ANY),
        scratch_shapes=[
            pltpu.SemaphoreType.DMA((n,)),
            pltpu.SemaphoreType.DMA((n,)),
            pltpu.SemaphoreType.DMA(()),
        ],
        compiler_params=pltpu.CompilerParams(collective_id=collective_id, has_side_effects=True),
    )(x)


def image_kernel(n, tiles, g_ref, wk_ref, wv_ref, o_ref, buf, send_sems, recv_sems, local_sem):
    me = lax.axis_index("section")
    row = lax.axis_index("dp")
    rows = g_ref.shape[0] // n
    half = g_ref.shape[1] // 2
    tile_w = wk_ref.shape[0] // tiles
    barrier = pltpu.get_barrier_semaphore()
    for k in range(1, n):
        pl.semaphore_signal(
            barrier, inc=1, device_id=(lax.rem(me + k, n), row), device_id_type=MESH_ID
        )
    pl.semaphore_wait(barrier, n - 1)

    def compute(t):
        cols = pl.ds(pl.multiple_of(t * tile_w, tile_w), tile_w)
        dims = (((1,), (1,)), ((), ()))
        acc = lax.dot_general(
            g_ref[:, pl.ds(0, half)], wk_ref[cols, :], dims, preferred_element_type=jnp.float32
        )
        acc = acc + lax.dot_general(
            g_ref[:, pl.ds(half, half)], wv_ref[cols, :], dims, preferred_element_type=jnp.float32
        )
        buf[:, cols] = acc.astype(buf.dtype)

    def send(t):
        cols = pl.ds(pl.multiple_of(t * tile_w, tile_w), tile_w)
        for k in range(1, n):
            peer = lax.rem(me + k, n)
            pltpu.make_async_remote_copy(
                src_ref=buf.at[pl.ds(pl.multiple_of(peer * rows, 16), rows), cols],
                dst_ref=o_ref.at[me, :, cols],
                send_sem=send_sems.at[k],
                recv_sem=recv_sems.at[k],
                device_id=(peer, row),
                device_id_type=MESH_ID,
            ).start()

    compute(0)

    def body(t, carry):
        compute(t)
        send(t - 1)
        return carry

    lax.fori_loop(1, tiles, body, 0)
    send(tiles - 1)
    own = pl.ds(pl.multiple_of(me * rows, 16), rows)
    local = pltpu.make_async_copy(buf.at[own, :], o_ref.at[me], local_sem)
    local.start()
    for k in range(1, n):
        peer = lax.rem(me + k, n)
        whole = pltpu.make_async_remote_copy(
            src_ref=buf.at[pl.ds(pl.multiple_of(peer * rows, 16), rows), :],
            dst_ref=o_ref.at[me],
            send_sem=send_sems.at[k],
            recv_sem=recv_sems.at[k],
            device_id=(peer, row),
            device_id_type=MESH_ID,
        )
        whole.wait_send()
        whole.wait_recv()
    local.wait()


def image_exchange(g, w_key, w_value, n):
    total_rows, kv = g.shape
    width = w_key.shape[0]
    tiles = 8
    return pl.pallas_call(
        functools.partial(image_kernel, n, tiles),
        out_shape=jax.ShapeDtypeStruct((n, total_rows // n, width), jnp.bfloat16),
        in_specs=[pl.BlockSpec(memory_space=pltpu.VMEM)] * 3,
        out_specs=pl.BlockSpec(memory_space=pl.ANY),
        scratch_shapes=[
            pltpu.VMEM((total_rows, width), jnp.bfloat16),
            pltpu.SemaphoreType.DMA((n,)),
            pltpu.SemaphoreType.DMA((n,)),
            pltpu.SemaphoreType.DMA(()),
        ],
        compiler_params=pltpu.CompilerParams(
            collective_id=3, has_side_effects=True, vmem_limit_bytes=60 * 1024 * 1024
        ),
        cost_estimate=pl.CostEstimate(
            flops=2 * total_rows * kv * width, bytes_accessed=2 * (kv + total_rows) * width,
            transcendentals=0,
        ),
    )(g, w_key, w_value)


def shards(queries, image_tokens, key_weight, value_weight, cotangent, tile_counts, text_lengths):
    n_section = lax.axis_size("section")
    samples_here, chunk, model_width = image_tokens.shape
    image_len = n_section * chunk
    tile_len = image_len // MAX_TILES
    w_key = key_weight[0]
    w_value = value_weight[0]
    query_local = queries[0]
    cotan_local = cotangent[0]
    late = [
        lax.all_gather(image_tokens[i], "section", axis=0, tiled=True)
        for i in range(1, samples_here)
    ]
    if n_section == 8 and lax.axis_size("dp") == 16:
        first = relay_gather(image_tokens[:1], n_section)
    else:
        first = exchange(image_tokens[:1], n_section, False, 0)
    token_list = [first.reshape(image_len, model_width)] + late
    query_list = []
    key_list = []
    value_list = []
    image_list = []
    for sample_index in range(samples_here):
        tokens = token_list[sample_index]
        keys = jnp.dot(tokens, w_key, preferred_element_type=jnp.float32).astype(jnp.bfloat16)
        values = jnp.dot(tokens, w_value, preferred_element_type=jnp.float32).astype(jnp.bfloat16)
        query_gradient, key_gradient, value_gradient = attend_one(
            query_local[sample_index],
            keys,
            values,
            cotan_local[sample_index],
            tile_counts[sample_index] * tile_len,
            text_lengths[sample_index],
        )
        query_list.append(query_gradient)
        key_list.append(key_gradient)
        value_list.append(value_gradient)
    all_tokens = jnp.concatenate(token_list, axis=0)
    value_term = jnp.einsum(
        "td,tk->dk", all_tokens, jnp.concatenate(value_list, axis=0),
        preferred_element_type=jnp.float32,
    ).astype(jnp.bfloat16)
    value_sum = lax.psum_scatter(value_term, "dp", scatter_dimension=0, tiled=True)
    key_term = jnp.einsum(
        "td,tk->dk", all_tokens, jnp.concatenate(key_list, axis=0),
        preferred_element_type=jnp.float32,
    ).astype(jnp.bfloat16)
    key_sum = lax.psum_scatter(key_term, "dp", scatter_dimension=0, tiled=True)
    query_out = jnp.stack(query_list)[None]
    kv_grads = jnp.concatenate([jnp.stack(key_list), jnp.stack(value_list)], axis=-1)
    by_slot = kv_grads.reshape(samples_here, n_section, chunk, -1).transpose(1, 0, 2, 3)
    received = image_exchange(
        by_slot.reshape(n_section * samples_here * chunk, -1), w_key, w_value, n_section
    )
    image_out = (
        jnp.sum(received.astype(jnp.float32), axis=0)
        .reshape(samples_here, chunk, model_width)
        .astype(jnp.bfloat16)
    )
    return (
        query_out,
        image_out,
        key_sum[None],
        value_sum[None],
    )


def solution(mesh):
    placed = (
        P("section", "dp", None, None),
        P("dp", "section", None),
        P("section", None, None),
        P("section", None, None),
        P("section", "dp", None, None),
        P("dp"),
        P("dp"),
    )
    return jax.shard_map(
        shards,
        mesh=mesh,
        in_specs=placed,
        out_specs=(
            P("section", "dp", None, None),
            P("dp", "section", None),
            P("section", "dp", None),
            P("section", "dp", None),
        ),
        check_vma=False,
    )
```

```python
import functools
import math

import jax
import jax.numpy as jnp
from jax import lax
from jax.experimental import pallas as pl
from jax.experimental.pallas import tpu as pltpu
from jax.sharding import PartitionSpec as P

QUERY_HEADS = 32
KEY_VALUE_HEADS = 4
HEAD_SIZE = 128
MAX_TILES = 4
MESH_ID = pl.DeviceIdType.MESH


def attend_one(queries, key_rows, value_rows, cotangent, key_limit, row_limit):
    total_rows = queries.shape[0]
    total_keys = key_rows.shape[0]
    group_width = QUERY_HEADS // KEY_VALUE_HEADS
    heads_of_queries = queries.reshape(total_rows, KEY_VALUE_HEADS, group_width, HEAD_SIZE)
    heads_of_keys = key_rows.reshape(total_keys, KEY_VALUE_HEADS, HEAD_SIZE)
    heads_of_values = value_rows.reshape(total_keys, KEY_VALUE_HEADS, HEAD_SIZE)
    row_live = (jnp.arange(total_rows) < row_limit)[:, None]
    active_cotangent = jnp.where(row_live, cotangent, jnp.zeros_like(cotangent))
    head_gradient = active_cotangent.reshape(total_rows, KEY_VALUE_HEADS, group_width, HEAD_SIZE)
    scaling = 1.0 / math.sqrt(HEAD_SIZE)
    scores = (
        jnp.einsum(
            "lhgd,nhd->hgln", heads_of_queries, heads_of_keys, preferred_element_type=jnp.float32
        )
        * scaling
    )
    key_live = jnp.arange(total_keys) < key_limit
    scores = jnp.where(key_live, scores, -jnp.inf)
    row_max = jnp.max(scores, axis=-1, keepdims=True)
    raised = jnp.exp(scores - row_max)
    weights = raised / jnp.sum(raised, axis=-1, keepdims=True)
    weights_low = weights.astype(jnp.bfloat16)
    value_gradient = jnp.einsum(
        "hgln,lhgd->nhd", weights_low, head_gradient, preferred_element_type=jnp.float32
    ).astype(jnp.bfloat16)
    prob_grad = jnp.einsum(
        "lhgd,nhd->hgln", head_gradient, heads_of_values, preferred_element_type=jnp.float32
    )
    row_dot = jnp.sum(weights * prob_grad, axis=-1, keepdims=True)
    score_grad = (weights * (prob_grad - row_dot) * scaling).astype(jnp.bfloat16)
    query_gradient = jnp.einsum(
        "hgln,nhd->lhgd", score_grad, heads_of_keys, preferred_element_type=jnp.float32
    ).astype(jnp.bfloat16)
    key_gradient = jnp.einsum(
        "hgln,lhgd->nhd", score_grad, heads_of_queries, preferred_element_type=jnp.float32
    ).astype(jnp.bfloat16)
    return (
        query_gradient.reshape(total_rows, QUERY_HEADS * HEAD_SIZE),
        key_gradient.reshape(total_keys, KEY_VALUE_HEADS * HEAD_SIZE),
        value_gradient.reshape(total_keys, KEY_VALUE_HEADS * HEAD_SIZE),
    )


def exchange_kernel(n, scatter, x_ref, o_ref, send_sems, recv_sems, local_sem):
    me = lax.axis_index("section")
    row = lax.axis_index("dp")
    barrier = pltpu.get_barrier_semaphore()
    for k in range(1, n):
        pl.semaphore_signal(
            barrier, inc=1, device_id=(lax.rem(me + k, n), row), device_id_type=MESH_ID
        )
    pl.semaphore_wait(barrier, n - 1)
    own = x_ref.at[:, me] if scatter else x_ref
    local = pltpu.make_async_copy(own, o_ref.at[:, me], local_sem)
    local.start()
    copies = []
    for k in range(1, n):
        peer = lax.rem(me + k, n)
        src = x_ref.at[:, peer] if scatter else x_ref
        copy = pltpu.make_async_remote_copy(
            src_ref=src,
            dst_ref=o_ref.at[:, me],
            send_sem=send_sems.at[k],
            recv_sem=recv_sems.at[k],
            device_id=(peer, row),
            device_id_type=MESH_ID,
        )
        copy.start()
        copies.append(copy)
    for copy in copies:
        copy.wait()
    local.wait()


def relay_gather_kernel(x_ref, o_ref, stage, local_sem, direct_send, direct_recv,
                        hop_send, hop_recv, fwd_send, fwd_recv):
    s = lax.axis_index("section")
    r = lax.axis_index("dp")
    y = lax.rem(s, 4)
    z = (s // 4) * 2 + r // 8
    xc = lax.rem(r, 8)
    half = x_ref.shape[-1] // 2

    def sec(zz, yy):
        return (lax.rem(zz, 4) // 2) * 4 + yy

    def dpi(zz):
        return lax.rem(zz, 2) * 8 + xc

    up, down = z + 1, z + 3
    peers = [(sec(z, lax.rem(y + j, 4)), r) for j in range(1, 4)]
    for yy in range(4):
        peers.append((sec(up, yy), dpi(up)))
        peers.append((sec(down, yy), dpi(down)))
    barrier = pltpu.get_barrier_semaphore()
    for peer in peers:
        pl.semaphore_signal(barrier, inc=1, device_id=peer, device_id_type=MESH_ID)
    pl.semaphore_wait(barrier, len(peers))

    local = pltpu.make_async_copy(x_ref, o_ref.at[:, s], local_sem)
    local.start()
    sends = []
    for j in range(1, 4):
        copy = pltpu.make_async_remote_copy(
            src_ref=x_ref,
            dst_ref=o_ref.at[:, s],
            send_sem=direct_send.at[j],
            recv_sem=direct_recv.at[j],
            device_id=peers[j - 1],
            device_id_type=MESH_ID,
        )
        copy.start()
        sends.append(copy)
    hops = []
    for side, (target, lanes) in enumerate(((up, pl.ds(0, half)), (down, pl.ds(half, half)))):
        copy = pltpu.make_async_remote_copy(
            src_ref=x_ref.at[:, :, lanes],
            dst_ref=stage.at[side],
            send_sem=hop_send.at[side],
            recv_sem=hop_recv.at[side],
            device_id=(sec(target, y), dpi(target)),
            device_id_type=MESH_ID,
        )
        copy.start()
        hops.append(copy)
    forwards = []
    for side, (origin, target, lanes) in enumerate(
        ((down, up, pl.ds(0, half)), (up, down, pl.ds(half, half)))
    ):
        hops[side].wait_recv()
        for yy in range(4):
            copy = pltpu.make_async_remote_copy(
                src_ref=stage.at[side],
                dst_ref=o_ref.at[:, sec(origin, y), :, lanes],
                send_sem=fwd_send.at[side, yy],
                recv_sem=fwd_recv.at[side, y],
                device_id=(sec(target, yy), dpi(target)),
                device_id_type=MESH_ID,
            )
            copy.start()
            forwards.append(copy)
    for copy in sends:
        copy.wait()
    for copy in hops:
        copy.wait_send()
    for copy in forwards:
        copy.wait_send()
    for side, (origin, target, lanes) in enumerate(
        ((down, up, pl.ds(0, half)), (up, down, pl.ds(half, half)))
    ):
        for yy in range(4):
            pltpu.make_async_remote_copy(
                src_ref=stage.at[side],
                dst_ref=o_ref.at[:, sec(origin, y), :, lanes],
                send_sem=fwd_send.at[side, yy],
                recv_sem=fwd_recv.at[side, yy],
                device_id=(sec(target, yy), dpi(target)),
                device_id_type=MESH_ID,
            ).wait_recv()
    local.wait()


def relay_gather(x, n):
    samples, chunk, width = x.shape
    return pl.pallas_call(
        relay_gather_kernel,
        out_shape=jax.ShapeDtypeStruct((samples, n, chunk, width), x.dtype),
        in_specs=[pl.BlockSpec(memory_space=pl.ANY)],
        out_specs=pl.BlockSpec(memory_space=pl.ANY),
        scratch_shapes=[
            pltpu.VMEM((2, samples, chunk, width // 2), x.dtype),
            pltpu.SemaphoreType.DMA(()),
            pltpu.SemaphoreType.DMA((4,)),
            pltpu.SemaphoreType.DMA((4,)),
            pltpu.SemaphoreType.DMA((2,)),
            pltpu.SemaphoreType.DMA((2,)),
            pltpu.SemaphoreType.DMA((2, 4)),
            pltpu.SemaphoreType.DMA((2, 4)),
        ],
        compiler_params=pltpu.CompilerParams(collective_id=2, has_side_effects=True),
    )(x)


def exchange(x, n, scatter, collective_id):
    if scatter:
        out_shape = x.shape
    else:
        out_shape = (x.shape[0], n) + x.shape[1:]
    return pl.pallas_call(
        functools.partial(exchange_kernel, n, scatter),
        out_shape=jax.ShapeDtypeStruct(out_shape, x.dtype),
        in_specs=[pl.BlockSpec(memory_space=pl.ANY)],
        out_specs=pl.BlockSpec(memory_space=pl.ANY),
        scratch_shapes=[
            pltpu.SemaphoreType.DMA((n,)),
            pltpu.SemaphoreType.DMA((n,)),
            pltpu.SemaphoreType.DMA(()),
        ],
        compiler_params=pltpu.CompilerParams(collective_id=collective_id, has_side_effects=True),
    )(x)


def image_kernel(n, tiles, g_ref, wk_ref, wv_ref, o_ref, buf, send_sems, recv_sems, local_sem):
    me = lax.axis_index("section")
    row = lax.axis_index("dp")
    rows = g_ref.shape[0] // n
    half = g_ref.shape[1] // 2
    tile_w = wk_ref.shape[0] // tiles
    barrier = pltpu.get_barrier_semaphore()
    for k in range(1, n):
        pl.semaphore_signal(
            barrier, inc=1, device_id=(lax.rem(me + k, n), row), device_id_type=MESH_ID
        )
    pl.semaphore_wait(barrier, n - 1)

    def compute(t):
        cols = pl.ds(pl.multiple_of(t * tile_w, tile_w), tile_w)
        dims = (((1,), (1,)), ((), ()))
        acc = lax.dot_general(
            g_ref[:, pl.ds(0, half)], wk_ref[cols, :], dims, preferred_element_type=jnp.float32
        )
        acc = acc + lax.dot_general(
            g_ref[:, pl.ds(half, half)], wv_ref[cols, :], dims, preferred_element_type=jnp.float32
        )
        buf[:, cols] = acc.astype(buf.dtype)

    def send(t):
        cols = pl.ds(pl.multiple_of(t * tile_w, tile_w), tile_w)
        for k in range(1, n):
            peer = lax.rem(me + k, n)
            pltpu.make_async_remote_copy(
                src_ref=buf.at[pl.ds(pl.multiple_of(peer * rows, 16), rows), cols],
                dst_ref=o_ref.at[me, :, cols],
                send_sem=send_sems.at[k],
                recv_sem=recv_sems.at[k],
                device_id=(peer, row),
                device_id_type=MESH_ID,
            ).start()

    compute(0)

    def body(t, carry):
        compute(t)
        send(t - 1)
        return carry

    lax.fori_loop(1, tiles, body, 0)
    send(tiles - 1)
    own = pl.ds(pl.multiple_of(me * rows, 16), rows)
    local = pltpu.make_async_copy(buf.at[own, :], o_ref.at[me], local_sem)
    local.start()
    for k in range(1, n):
        peer = lax.rem(me + k, n)
        whole = pltpu.make_async_remote_copy(
            src_ref=buf.at[pl.ds(pl.multiple_of(peer * rows, 16), rows), :],
            dst_ref=o_ref.at[me],
            send_sem=send_sems.at[k],
            recv_sem=recv_sems.at[k],
            device_id=(peer, row),
            device_id_type=MESH_ID,
        )
        whole.wait_send()
        whole.wait_recv()
    local.wait()


def image_relay_kernel(tiles, g_ref, wk_ref, wv_ref, o_ref, buf, stage, local_sem,
                       direct_send, direct_recv, hop_send, hop_recv, fwd_send, fwd_recv):
    s = lax.axis_index("section")
    r = lax.axis_index("dp")
    y = lax.rem(s, 4)
    z = (s // 4) * 2 + r // 8
    xc = lax.rem(r, 8)
    rows = g_ref.shape[0] // 8
    half = g_ref.shape[1] // 2
    lanes = wk_ref.shape[0] // 2
    tile_w = wk_ref.shape[0] // tiles

    def sec(zz, yy):
        return (lax.rem(zz, 4) // 2) * 4 + yy

    def dpi(zz):
        return lax.rem(zz, 2) * 8 + xc

    def block(section):
        return pl.ds(pl.multiple_of(section * rows, 16), rows)

    up, down = z + 1, z + 3
    near = [(sec(z, lax.rem(y + j, 4)), r) for j in range(1, 4)]
    peers = list(near)
    for yy in range(4):
        peers.append((sec(up, yy), dpi(up)))
        peers.append((sec(down, yy), dpi(down)))
    barrier = pltpu.get_barrier_semaphore()
    for peer in peers:
        pl.semaphore_signal(barrier, inc=1, device_id=peer, device_id_type=MESH_ID)
    pl.semaphore_wait(barrier, len(peers))

    def compute(t, carry):
        cols = pl.ds(pl.multiple_of(t * tile_w, tile_w), tile_w)
        dims = (((1,), (1,)), ((), ()))
        acc = lax.dot_general(
            g_ref[:, pl.ds(0, half)], wk_ref[cols, :], dims, preferred_element_type=jnp.float32
        )
        acc = acc + lax.dot_general(
            g_ref[:, pl.ds(half, half)], wv_ref[cols, :], dims, preferred_element_type=jnp.float32
        )
        buf[:, cols] = acc.astype(buf.dtype)
        return carry

    lax.fori_loop(0, tiles, compute, 0)
    local = pltpu.make_async_copy(buf.at[block(s), :], o_ref.at[s], local_sem)
    local.start()
    sends = []
    for j in range(1, 4):
        copy = pltpu.make_async_remote_copy(
            src_ref=buf.at[block(near[j - 1][0]), :],
            dst_ref=o_ref.at[s],
            send_sem=direct_send.at[j],
            recv_sem=direct_recv.at[j],
            device_id=near[j - 1],
            device_id_type=MESH_ID,
        )
        copy.start()
        sends.append(copy)
    far_plane = z + 2
    hops = {}
    for side, (target, part) in enumerate(((up, pl.ds(0, lanes)), (down, pl.ds(lanes, lanes)))):
        for yy in range(4):
            copy = pltpu.make_async_remote_copy(
                src_ref=buf.at[block(sec(far_plane, yy)), part],
                dst_ref=stage.at[side, yy],
                send_sem=hop_send.at[side, yy],
                recv_sem=hop_recv.at[side, yy],
                device_id=(sec(target, y), dpi(target)),
                device_id_type=MESH_ID,
            )
            copy.start()
            hops[side, yy] = copy
    routes = ((down, up, pl.ds(0, lanes)), (up, down, pl.ds(lanes, lanes)))
    forwards = []
    for side, (origin, target, part) in enumerate(routes):
        for yy in range(4):
            hops[side, yy].wait_recv()
            copy = pltpu.make_async_remote_copy(
                src_ref=stage.at[side, yy],
                dst_ref=o_ref.at[sec(origin, y), :, part],
                send_sem=fwd_send.at[side, yy],
                recv_sem=fwd_recv.at[side, y],
                device_id=(sec(target, yy), dpi(target)),
                device_id_type=MESH_ID,
            )
            copy.start()
            forwards.append(copy)
    for copy in sends:
        copy.wait()
    for copy in hops.values():
        copy.wait_send()
    for copy in forwards:
        copy.wait_send()
    for side, (origin, target, part) in enumerate(routes):
        for yy in range(4):
            pltpu.make_async_remote_copy(
                src_ref=stage.at[side, yy],
                dst_ref=o_ref.at[sec(origin, y), :, part],
                send_sem=fwd_send.at[side, yy],
                recv_sem=fwd_recv.at[side, yy],
                device_id=(sec(target, yy), dpi(target)),
                device_id_type=MESH_ID,
            ).wait_recv()
    local.wait()


def image_exchange(g, w_key, w_value, n):
    total_rows, kv = g.shape
    width = w_key.shape[0]
    tiles = 8
    if n == 8 and lax.axis_size("dp") == 16:
        body = functools.partial(image_relay_kernel, tiles)
        scratch = [
            pltpu.VMEM((total_rows, width), jnp.bfloat16),
            pltpu.VMEM((2, 4, total_rows // n, width // 2), jnp.bfloat16),
            pltpu.SemaphoreType.DMA(()),
            pltpu.SemaphoreType.DMA((4,)),
            pltpu.SemaphoreType.DMA((4,)),
            pltpu.SemaphoreType.DMA((2, 4)),
            pltpu.SemaphoreType.DMA((2, 4)),
            pltpu.SemaphoreType.DMA((2, 4)),
            pltpu.SemaphoreType.DMA((2, 4)),
        ]
    else:
        body = functools.partial(image_kernel, n, tiles)
        scratch = [
            pltpu.VMEM((total_rows, width), jnp.bfloat16),
            pltpu.SemaphoreType.DMA((n,)),
            pltpu.SemaphoreType.DMA((n,)),
            pltpu.SemaphoreType.DMA(()),
        ]
    return pl.pallas_call(
        body,
        out_shape=jax.ShapeDtypeStruct((n, total_rows // n, width), jnp.bfloat16),
        in_specs=[pl.BlockSpec(memory_space=pltpu.VMEM)] * 3,
        out_specs=pl.BlockSpec(memory_space=pl.ANY),
        scratch_shapes=scratch,
        compiler_params=pltpu.CompilerParams(
            collective_id=3, has_side_effects=True, vmem_limit_bytes=60 * 1024 * 1024
        ),
        cost_estimate=pl.CostEstimate(
            flops=2 * total_rows * kv * width, bytes_accessed=2 * (kv + total_rows) * width,
            transcendentals=0,
        ),
    )(g, w_key, w_value)


def shards(queries, image_tokens, key_weight, value_weight, cotangent, tile_counts, text_lengths):
    n_section = lax.axis_size("section")
    samples_here, chunk, model_width = image_tokens.shape
    image_len = n_section * chunk
    tile_len = image_len // MAX_TILES
    w_key = key_weight[0]
    w_value = value_weight[0]
    query_local = queries[0]
    cotan_local = cotangent[0]
    late = [
        lax.all_gather(image_tokens[i], "section", axis=0, tiled=True)
        for i in range(1, samples_here)
    ]
    if n_section == 8 and lax.axis_size("dp") == 16:
        first = relay_gather(image_tokens[:1], n_section)
    else:
        first = exchange(image_tokens[:1], n_section, False, 0)
    token_list = [first.reshape(image_len, model_width)] + late
    query_list = []
    key_list = []
    value_list = []
    image_list = []
    for sample_index in range(samples_here):
        tokens = token_list[sample_index]
        keys = jnp.dot(tokens, w_key, preferred_element_type=jnp.float32).astype(jnp.bfloat16)
        values = jnp.dot(tokens, w_value, preferred_element_type=jnp.float32).astype(jnp.bfloat16)
        query_gradient, key_gradient, value_gradient = attend_one(
            query_local[sample_index],
            keys,
            values,
            cotan_local[sample_index],
            tile_counts[sample_index] * tile_len,
            text_lengths[sample_index],
        )
        query_list.append(query_gradient)
        key_list.append(key_gradient)
        value_list.append(value_gradient)
    all_tokens = jnp.concatenate(token_list, axis=0)
    value_term = jnp.einsum(
        "td,tk->dk", all_tokens, jnp.concatenate(value_list, axis=0),
        preferred_element_type=jnp.float32,
    ).astype(jnp.bfloat16)
    value_sum = lax.psum_scatter(value_term, "dp", scatter_dimension=0, tiled=True)
    key_term = jnp.einsum(
        "td,tk->dk", all_tokens, jnp.concatenate(key_list, axis=0),
        preferred_element_type=jnp.float32,
    ).astype(jnp.bfloat16)
    key_sum = lax.psum_scatter(key_term, "dp", scatter_dimension=0, tiled=True)
    query_out = jnp.stack(query_list)[None]
    kv_grads = jnp.concatenate([jnp.stack(key_list), jnp.stack(value_list)], axis=-1)
    by_slot = kv_grads.reshape(samples_here, n_section, chunk, -1).transpose(1, 0, 2, 3)
    received = image_exchange(
        by_slot.reshape(n_section * samples_here * chunk, -1), w_key, w_value, n_section
    )
    image_out = (
        jnp.sum(received.astype(jnp.float32), axis=0)
        .reshape(samples_here, chunk, model_width)
        .astype(jnp.bfloat16)
    )
    return (
        query_out,
        image_out,
        key_sum[None],
        value_sum[None],
    )


def solution(mesh):
    placed = (
        P("section", "dp", None, None),
        P("dp", "section", None),
        P("section", None, None),
        P("section", None, None),
        P("section", "dp", None, None),
        P("dp"),
        P("dp"),
    )
    return jax.shard_map(
        shards,
        mesh=mesh,
        in_specs=placed,
        out_specs=(
            P("section", "dp", None, None),
            P("dp", "section", None),
            P("section", "dp", None),
            P("section", "dp", None),
        ),
        check_vma=False,
    )
```

```python
import functools
import math

import jax
import jax.numpy as jnp
from jax import lax
from jax.experimental import pallas as pl
from jax.experimental.pallas import tpu as pltpu
from jax.sharding import PartitionSpec as P

QUERY_HEADS = 32
KEY_VALUE_HEADS = 4
HEAD_SIZE = 128
MAX_TILES = 4
MESH_ID = pl.DeviceIdType.MESH


def attend_one(queries, key_rows, value_rows, cotangent, key_limit, row_limit):
    total_rows = queries.shape[0]
    total_keys = key_rows.shape[0]
    group_width = QUERY_HEADS // KEY_VALUE_HEADS
    heads_of_queries = queries.reshape(total_rows, KEY_VALUE_HEADS, group_width, HEAD_SIZE)
    heads_of_keys = key_rows.reshape(total_keys, KEY_VALUE_HEADS, HEAD_SIZE)
    heads_of_values = value_rows.reshape(total_keys, KEY_VALUE_HEADS, HEAD_SIZE)
    row_live = (jnp.arange(total_rows) < row_limit)[:, None]
    active_cotangent = jnp.where(row_live, cotangent, jnp.zeros_like(cotangent))
    head_gradient = active_cotangent.reshape(total_rows, KEY_VALUE_HEADS, group_width, HEAD_SIZE)
    scaling = 1.0 / math.sqrt(HEAD_SIZE)
    scores = (
        jnp.einsum(
            "lhgd,nhd->hgln", heads_of_queries, heads_of_keys, preferred_element_type=jnp.float32
        )
        * scaling
    )
    key_live = jnp.arange(total_keys) < key_limit
    scores = jnp.where(key_live, scores, -jnp.inf)
    row_max = jnp.max(scores, axis=-1, keepdims=True)
    raised = jnp.exp(scores - row_max)
    weights = raised / jnp.sum(raised, axis=-1, keepdims=True)
    weights_low = weights.astype(jnp.bfloat16)
    value_gradient = jnp.einsum(
        "hgln,lhgd->nhd", weights_low, head_gradient, preferred_element_type=jnp.float32
    ).astype(jnp.bfloat16)
    prob_grad = jnp.einsum(
        "lhgd,nhd->hgln", head_gradient, heads_of_values, preferred_element_type=jnp.float32
    )
    row_dot = jnp.sum(weights * prob_grad, axis=-1, keepdims=True)
    score_grad = (weights * (prob_grad - row_dot) * scaling).astype(jnp.bfloat16)
    query_gradient = jnp.einsum(
        "hgln,nhd->lhgd", score_grad, heads_of_keys, preferred_element_type=jnp.float32
    ).astype(jnp.bfloat16)
    key_gradient = jnp.einsum(
        "hgln,lhgd->nhd", score_grad, heads_of_queries, preferred_element_type=jnp.float32
    ).astype(jnp.bfloat16)
    return (
        query_gradient.reshape(total_rows, QUERY_HEADS * HEAD_SIZE),
        key_gradient.reshape(total_keys, KEY_VALUE_HEADS * HEAD_SIZE),
        value_gradient.reshape(total_keys, KEY_VALUE_HEADS * HEAD_SIZE),
    )


def exchange_kernel(n, scatter, x_ref, o_ref, send_sems, recv_sems, local_sem):
    me = lax.axis_index("section")
    row = lax.axis_index("dp")
    barrier = pltpu.get_barrier_semaphore()
    for k in range(1, n):
        pl.semaphore_signal(
            barrier, inc=1, device_id=(lax.rem(me + k, n), row), device_id_type=MESH_ID
        )
    pl.semaphore_wait(barrier, n - 1)
    own = x_ref.at[:, me] if scatter else x_ref
    local = pltpu.make_async_copy(own, o_ref.at[:, me], local_sem)
    local.start()
    copies = []
    for k in range(1, n):
        peer = lax.rem(me + k, n)
        src = x_ref.at[:, peer] if scatter else x_ref
        copy = pltpu.make_async_remote_copy(
            src_ref=src,
            dst_ref=o_ref.at[:, me],
            send_sem=send_sems.at[k],
            recv_sem=recv_sems.at[k],
            device_id=(peer, row),
            device_id_type=MESH_ID,
        )
        copy.start()
        copies.append(copy)
    for copy in copies:
        copy.wait()
    local.wait()


def relay_gather_kernel(x_ref, o_ref, stage, local_sem, direct_send, direct_recv,
                        hop_send, hop_recv, fwd_send, fwd_recv):
    s = lax.axis_index("section")
    r = lax.axis_index("dp")
    y = lax.rem(s, 4)
    z = (s // 4) * 2 + r // 8
    xc = lax.rem(r, 8)
    half = x_ref.shape[-1] // 2

    def sec(zz, yy):
        return (lax.rem(zz, 4) // 2) * 4 + yy

    def dpi(zz):
        return lax.rem(zz, 2) * 8 + xc

    up, down = z + 1, z + 3
    peers = [(sec(z, lax.rem(y + j, 4)), r) for j in range(1, 4)]
    for yy in range(4):
        peers.append((sec(up, yy), dpi(up)))
        peers.append((sec(down, yy), dpi(down)))
    barrier = pltpu.get_barrier_semaphore()
    for peer in peers:
        pl.semaphore_signal(barrier, inc=1, device_id=peer, device_id_type=MESH_ID)
    pl.semaphore_wait(barrier, len(peers))

    local = pltpu.make_async_copy(x_ref, o_ref.at[:, s], local_sem)
    local.start()
    sends = []
    for j in range(1, 4):
        copy = pltpu.make_async_remote_copy(
            src_ref=x_ref,
            dst_ref=o_ref.at[:, s],
            send_sem=direct_send.at[j],
            recv_sem=direct_recv.at[j],
            device_id=peers[j - 1],
            device_id_type=MESH_ID,
        )
        copy.start()
        sends.append(copy)
    hops = []
    for side, (target, lanes) in enumerate(((up, pl.ds(0, half)), (down, pl.ds(half, half)))):
        copy = pltpu.make_async_remote_copy(
            src_ref=x_ref.at[:, :, lanes],
            dst_ref=stage.at[side],
            send_sem=hop_send.at[side],
            recv_sem=hop_recv.at[side],
            device_id=(sec(target, y), dpi(target)),
            device_id_type=MESH_ID,
        )
        copy.start()
        hops.append(copy)
    forwards = []
    for side, (origin, target, lanes) in enumerate(
        ((down, up, pl.ds(0, half)), (up, down, pl.ds(half, half)))
    ):
        hops[side].wait_recv()
        for yy in range(4):
            copy = pltpu.make_async_remote_copy(
                src_ref=stage.at[side],
                dst_ref=o_ref.at[:, sec(origin, y), :, lanes],
                send_sem=fwd_send.at[side, yy],
                recv_sem=fwd_recv.at[side, y],
                device_id=(sec(target, yy), dpi(target)),
                device_id_type=MESH_ID,
            )
            copy.start()
            forwards.append(copy)
    for copy in sends:
        copy.wait()
    for copy in hops:
        copy.wait_send()
    for copy in forwards:
        copy.wait_send()
    for side, (origin, target, lanes) in enumerate(
        ((down, up, pl.ds(0, half)), (up, down, pl.ds(half, half)))
    ):
        for yy in range(4):
            pltpu.make_async_remote_copy(
                src_ref=stage.at[side],
                dst_ref=o_ref.at[:, sec(origin, y), :, lanes],
                send_sem=fwd_send.at[side, yy],
                recv_sem=fwd_recv.at[side, yy],
                device_id=(sec(target, yy), dpi(target)),
                device_id_type=MESH_ID,
            ).wait_recv()
    local.wait()


def relay_gather(x, n):
    samples, chunk, width = x.shape
    return pl.pallas_call(
        relay_gather_kernel,
        out_shape=jax.ShapeDtypeStruct((samples, n, chunk, width), x.dtype),
        in_specs=[pl.BlockSpec(memory_space=pl.ANY)],
        out_specs=pl.BlockSpec(memory_space=pl.ANY),
        scratch_shapes=[
            pltpu.VMEM((2, samples, chunk, width // 2), x.dtype),
            pltpu.SemaphoreType.DMA(()),
            pltpu.SemaphoreType.DMA((4,)),
            pltpu.SemaphoreType.DMA((4,)),
            pltpu.SemaphoreType.DMA((2,)),
            pltpu.SemaphoreType.DMA((2,)),
            pltpu.SemaphoreType.DMA((2, 4)),
            pltpu.SemaphoreType.DMA((2, 4)),
        ],
        compiler_params=pltpu.CompilerParams(collective_id=2, has_side_effects=True),
    )(x)


def exchange(x, n, scatter, collective_id):
    if scatter:
        out_shape = x.shape
    else:
        out_shape = (x.shape[0], n) + x.shape[1:]
    return pl.pallas_call(
        functools.partial(exchange_kernel, n, scatter),
        out_shape=jax.ShapeDtypeStruct(out_shape, x.dtype),
        in_specs=[pl.BlockSpec(memory_space=pl.ANY)],
        out_specs=pl.BlockSpec(memory_space=pl.ANY),
        scratch_shapes=[
            pltpu.SemaphoreType.DMA((n,)),
            pltpu.SemaphoreType.DMA((n,)),
            pltpu.SemaphoreType.DMA(()),
        ],
        compiler_params=pltpu.CompilerParams(collective_id=collective_id, has_side_effects=True),
    )(x)


def image_kernel(n, tiles, g_ref, wk_ref, wv_ref, o_ref, buf, send_sems, recv_sems, local_sem):
    me = lax.axis_index("section")
    row = lax.axis_index("dp")
    rows = g_ref.shape[0] // n
    half = g_ref.shape[1] // 2
    tile_w = wk_ref.shape[0] // tiles
    barrier = pltpu.get_barrier_semaphore()
    for k in range(1, n):
        pl.semaphore_signal(
            barrier, inc=1, device_id=(lax.rem(me + k, n), row), device_id_type=MESH_ID
        )
    pl.semaphore_wait(barrier, n - 1)

    def compute(t):
        cols = pl.ds(pl.multiple_of(t * tile_w, tile_w), tile_w)
        dims = (((1,), (1,)), ((), ()))
        acc = lax.dot_general(
            g_ref[:, pl.ds(0, half)], wk_ref[cols, :], dims, preferred_element_type=jnp.float32
        )
        acc = acc + lax.dot_general(
            g_ref[:, pl.ds(half, half)], wv_ref[cols, :], dims, preferred_element_type=jnp.float32
        )
        buf[:, cols] = acc.astype(buf.dtype)

    def send(t):
        cols = pl.ds(pl.multiple_of(t * tile_w, tile_w), tile_w)
        for k in range(1, n):
            peer = lax.rem(me + k, n)
            pltpu.make_async_remote_copy(
                src_ref=buf.at[pl.ds(pl.multiple_of(peer * rows, 16), rows), cols],
                dst_ref=o_ref.at[me, :, cols],
                send_sem=send_sems.at[k],
                recv_sem=recv_sems.at[k],
                device_id=(peer, row),
                device_id_type=MESH_ID,
            ).start()

    compute(0)

    def body(t, carry):
        compute(t)
        send(t - 1)
        return carry

    lax.fori_loop(1, tiles, body, 0)
    send(tiles - 1)
    own = pl.ds(pl.multiple_of(me * rows, 16), rows)
    local = pltpu.make_async_copy(buf.at[own, :], o_ref.at[me], local_sem)
    local.start()
    for k in range(1, n):
        peer = lax.rem(me + k, n)
        whole = pltpu.make_async_remote_copy(
            src_ref=buf.at[pl.ds(pl.multiple_of(peer * rows, 16), rows), :],
            dst_ref=o_ref.at[me],
            send_sem=send_sems.at[k],
            recv_sem=recv_sems.at[k],
            device_id=(peer, row),
            device_id_type=MESH_ID,
        )
        whole.wait_send()
        whole.wait_recv()
    local.wait()


def image_exchange(g, w_key, w_value, n):
    total_rows, kv = g.shape
    width = w_key.shape[0]
    tiles = 8
    return pl.pallas_call(
        functools.partial(image_kernel, n, tiles),
        out_shape=jax.ShapeDtypeStruct((n, total_rows // n, width), jnp.bfloat16),
        in_specs=[pl.BlockSpec(memory_space=pltpu.VMEM)] * 3,
        out_specs=pl.BlockSpec(memory_space=pl.ANY),
        scratch_shapes=[
            pltpu.VMEM((total_rows, width), jnp.bfloat16),
            pltpu.SemaphoreType.DMA((n,)),
            pltpu.SemaphoreType.DMA((n,)),
            pltpu.SemaphoreType.DMA(()),
        ],
        compiler_params=pltpu.CompilerParams(
            collective_id=3, has_side_effects=True, vmem_limit_bytes=60 * 1024 * 1024
        ),
        cost_estimate=pl.CostEstimate(
            flops=2 * total_rows * kv * width, bytes_accessed=2 * (kv + total_rows) * width,
            transcendentals=0,
        ),
    )(g, w_key, w_value)


def shards(queries, image_tokens, key_weight, value_weight, cotangent, tile_counts, text_lengths):
    n_section = lax.axis_size("section")
    samples_here, chunk, model_width = image_tokens.shape
    image_len = n_section * chunk
    tile_len = image_len // MAX_TILES
    w_key = key_weight[0]
    w_value = value_weight[0]
    query_local = queries[0]
    cotan_local = cotangent[0]
    late = [
        lax.all_gather(image_tokens[i], "section", axis=0, tiled=True)
        for i in range(1, samples_here)
    ]
    if n_section == 8 and lax.axis_size("dp") == 16:
        first = relay_gather(image_tokens[:1], n_section)
    else:
        first = exchange(image_tokens[:1], n_section, False, 0)
    token_list = [first.reshape(image_len, model_width)] + late
    keys_list = []
    values_list = []
    for sample_index in range(samples_here):
        tokens = token_list[sample_index]
        keys_list.append(
            jnp.dot(tokens, w_key, preferred_element_type=jnp.float32).astype(jnp.bfloat16)
        )
        values_list.append(
            jnp.dot(tokens, w_value, preferred_element_type=jnp.float32).astype(jnp.bfloat16)
        )
    query_grads, key_grads, value_grads = jax.vmap(attend_one)(
        query_local,
        jnp.stack(keys_list),
        jnp.stack(values_list),
        cotan_local,
        tile_counts * tile_len,
        text_lengths,
    )
    all_tokens = jnp.concatenate(token_list, axis=0)
    value_term = jnp.einsum(
        "td,tk->dk", all_tokens, value_grads.reshape(samples_here * image_len, -1),
        preferred_element_type=jnp.float32,
    ).astype(jnp.bfloat16)
    value_sum = lax.psum_scatter(value_term, "dp", scatter_dimension=0, tiled=True)
    key_term = jnp.einsum(
        "td,tk->dk", all_tokens, key_grads.reshape(samples_here * image_len, -1),
        preferred_element_type=jnp.float32,
    ).astype(jnp.bfloat16)
    key_sum = lax.psum_scatter(key_term, "dp", scatter_dimension=0, tiled=True)
    query_out = query_grads[None]
    kv_grads = jnp.concatenate([key_grads, value_grads], axis=-1)
    by_slot = kv_grads.reshape(samples_here, n_section, chunk, -1).transpose(1, 0, 2, 3)
    received = image_exchange(
        by_slot.reshape(n_section * samples_here * chunk, -1), w_key, w_value, n_section
    )
    image_out = (
        jnp.sum(received.astype(jnp.float32), axis=0)
        .reshape(samples_here, chunk, model_width)
        .astype(jnp.bfloat16)
    )
    return (
        query_out,
        image_out,
        key_sum[None],
        value_sum[None],
    )


def solution(mesh):
    placed = (
        P("section", "dp", None, None),
        P("dp", "section", None),
        P("section", None, None),
        P("section", None, None),
        P("section", "dp", None, None),
        P("dp"),
        P("dp"),
    )
    return jax.shard_map(
        shards,
        mesh=mesh,
        in_specs=placed,
        out_specs=(
            P("section", "dp", None, None),
            P("dp", "section", None),
            P("section", "dp", None),
            P("section", "dp", None),
        ),
        check_vma=False,
    )
```

```python
import functools
import math

import jax
import jax.numpy as jnp
from jax import lax
from jax.experimental import pallas as pl
from jax.experimental.pallas import tpu as pltpu
from jax.sharding import PartitionSpec as P

QUERY_HEADS = 32
KEY_VALUE_HEADS = 4
HEAD_SIZE = 128
MAX_TILES = 4
MESH_ID = pl.DeviceIdType.MESH


def attend_one(queries, key_rows, value_rows, cotangent, key_limit, row_limit):
    total_rows = queries.shape[0]
    total_keys = key_rows.shape[0]
    group_width = QUERY_HEADS // KEY_VALUE_HEADS
    heads_of_queries = queries.reshape(total_rows, KEY_VALUE_HEADS, group_width, HEAD_SIZE)
    heads_of_keys = key_rows.reshape(total_keys, KEY_VALUE_HEADS, HEAD_SIZE)
    heads_of_values = value_rows.reshape(total_keys, KEY_VALUE_HEADS, HEAD_SIZE)
    row_live = (jnp.arange(total_rows) < row_limit)[:, None]
    active_cotangent = jnp.where(row_live, cotangent, jnp.zeros_like(cotangent))
    head_gradient = active_cotangent.reshape(total_rows, KEY_VALUE_HEADS, group_width, HEAD_SIZE)
    scaling = 1.0 / math.sqrt(HEAD_SIZE)
    scores = (
        jnp.einsum(
            "lhgd,nhd->hgln", heads_of_queries, heads_of_keys, preferred_element_type=jnp.float32
        )
        * scaling
    )
    key_live = jnp.arange(total_keys) < key_limit
    scores = jnp.where(key_live, scores, -jnp.inf)
    row_max = jnp.max(scores, axis=-1, keepdims=True)
    raised = jnp.exp(scores - row_max)
    weights = raised / jnp.sum(raised, axis=-1, keepdims=True)
    weights_low = weights.astype(jnp.bfloat16)
    value_gradient = jnp.einsum(
        "hgln,lhgd->nhd", weights_low, head_gradient, preferred_element_type=jnp.float32
    ).astype(jnp.bfloat16)
    prob_grad = jnp.einsum(
        "lhgd,nhd->hgln", head_gradient, heads_of_values, preferred_element_type=jnp.float32
    )
    row_dot = jnp.sum(weights * prob_grad, axis=-1, keepdims=True)
    score_grad = (weights * (prob_grad - row_dot) * scaling).astype(jnp.bfloat16)
    query_gradient = jnp.einsum(
        "hgln,nhd->lhgd", score_grad, heads_of_keys, preferred_element_type=jnp.float32
    ).astype(jnp.bfloat16)
    key_gradient = jnp.einsum(
        "hgln,lhgd->nhd", score_grad, heads_of_queries, preferred_element_type=jnp.float32
    ).astype(jnp.bfloat16)
    return (
        query_gradient.reshape(total_rows, QUERY_HEADS * HEAD_SIZE),
        key_gradient.reshape(total_keys, KEY_VALUE_HEADS * HEAD_SIZE),
        value_gradient.reshape(total_keys, KEY_VALUE_HEADS * HEAD_SIZE),
    )


def attend_front(queries, key_rows, cotangent, key_limit, row_limit):
    total_rows = queries.shape[0]
    total_keys = key_rows.shape[0]
    group_width = QUERY_HEADS // KEY_VALUE_HEADS
    heads_of_queries = queries.reshape(total_rows, KEY_VALUE_HEADS, group_width, HEAD_SIZE)
    heads_of_keys = key_rows.reshape(total_keys, KEY_VALUE_HEADS, HEAD_SIZE)
    row_live = (jnp.arange(total_rows) < row_limit)[:, None]
    active_cotangent = jnp.where(row_live, cotangent, jnp.zeros_like(cotangent))
    head_gradient = active_cotangent.reshape(total_rows, KEY_VALUE_HEADS, group_width, HEAD_SIZE)
    scaling = 1.0 / math.sqrt(HEAD_SIZE)
    scores = (
        jnp.einsum(
            "lhgd,nhd->hgln", heads_of_queries, heads_of_keys, preferred_element_type=jnp.float32
        )
        * scaling
    )
    key_live = jnp.arange(total_keys) < key_limit
    scores = jnp.where(key_live, scores, -jnp.inf)
    row_max = jnp.max(scores, axis=-1, keepdims=True)
    raised = jnp.exp(scores - row_max)
    weights = raised / jnp.sum(raised, axis=-1, keepdims=True)
    weights_low = weights.astype(jnp.bfloat16)
    value_gradient = jnp.einsum(
        "hgln,lhgd->nhd", weights_low, head_gradient, preferred_element_type=jnp.float32
    ).astype(jnp.bfloat16)
    return weights, value_gradient.reshape(total_keys, KEY_VALUE_HEADS * HEAD_SIZE)


def attend_back(queries, key_rows, value_rows, cotangent, row_limit, weights):
    total_rows = queries.shape[0]
    total_keys = key_rows.shape[0]
    group_width = QUERY_HEADS // KEY_VALUE_HEADS
    heads_of_queries = queries.reshape(total_rows, KEY_VALUE_HEADS, group_width, HEAD_SIZE)
    heads_of_keys = key_rows.reshape(total_keys, KEY_VALUE_HEADS, HEAD_SIZE)
    heads_of_values = value_rows.reshape(total_keys, KEY_VALUE_HEADS, HEAD_SIZE)
    row_live = (jnp.arange(total_rows) < row_limit)[:, None]
    active_cotangent = jnp.where(row_live, cotangent, jnp.zeros_like(cotangent))
    head_gradient = active_cotangent.reshape(total_rows, KEY_VALUE_HEADS, group_width, HEAD_SIZE)
    scaling = 1.0 / math.sqrt(HEAD_SIZE)
    prob_grad = jnp.einsum(
        "lhgd,nhd->hgln", head_gradient, heads_of_values, preferred_element_type=jnp.float32
    )
    row_dot = jnp.sum(weights * prob_grad, axis=-1, keepdims=True)
    score_grad = (weights * (prob_grad - row_dot) * scaling).astype(jnp.bfloat16)
    query_gradient = jnp.einsum(
        "hgln,nhd->lhgd", score_grad, heads_of_keys, preferred_element_type=jnp.float32
    ).astype(jnp.bfloat16)
    key_gradient = jnp.einsum(
        "hgln,lhgd->nhd", score_grad, heads_of_queries, preferred_element_type=jnp.float32
    ).astype(jnp.bfloat16)
    return (
        query_gradient.reshape(total_rows, QUERY_HEADS * HEAD_SIZE),
        key_gradient.reshape(total_keys, KEY_VALUE_HEADS * HEAD_SIZE),
    )


def exchange_kernel(n, scatter, x_ref, o_ref, send_sems, recv_sems, local_sem):
    me = lax.axis_index("section")
    row = lax.axis_index("dp")
    barrier = pltpu.get_barrier_semaphore()
    for k in range(1, n):
        pl.semaphore_signal(
            barrier, inc=1, device_id=(lax.rem(me + k, n), row), device_id_type=MESH_ID
        )
    pl.semaphore_wait(barrier, n - 1)
    own = x_ref.at[:, me] if scatter else x_ref
    local = pltpu.make_async_copy(own, o_ref.at[:, me], local_sem)
    local.start()
    copies = []
    for k in range(1, n):
        peer = lax.rem(me + k, n)
        src = x_ref.at[:, peer] if scatter else x_ref
        copy = pltpu.make_async_remote_copy(
            src_ref=src,
            dst_ref=o_ref.at[:, me],
            send_sem=send_sems.at[k],
            recv_sem=recv_sems.at[k],
            device_id=(peer, row),
            device_id_type=MESH_ID,
        )
        copy.start()
        copies.append(copy)
    for copy in copies:
        copy.wait()
    local.wait()


def relay_gather_kernel(x_ref, o_ref, stage, local_sem, direct_send, direct_recv,
                        hop_send, hop_recv, fwd_send, fwd_recv):
    s = lax.axis_index("section")
    r = lax.axis_index("dp")
    y = lax.rem(s, 4)
    z = (s // 4) * 2 + r // 8
    xc = lax.rem(r, 8)
    half = x_ref.shape[-1] // 2

    def sec(zz, yy):
        return (lax.rem(zz, 4) // 2) * 4 + yy

    def dpi(zz):
        return lax.rem(zz, 2) * 8 + xc

    up, down = z + 1, z + 3
    peers = [(sec(z, lax.rem(y + j, 4)), r) for j in range(1, 4)]
    for yy in range(4):
        peers.append((sec(up, yy), dpi(up)))
        peers.append((sec(down, yy), dpi(down)))
    barrier = pltpu.get_barrier_semaphore()
    for peer in peers:
        pl.semaphore_signal(barrier, inc=1, device_id=peer, device_id_type=MESH_ID)
    pl.semaphore_wait(barrier, len(peers))

    local = pltpu.make_async_copy(x_ref, o_ref.at[:, s], local_sem)
    local.start()
    sends = []
    for j in range(1, 4):
        copy = pltpu.make_async_remote_copy(
            src_ref=x_ref,
            dst_ref=o_ref.at[:, s],
            send_sem=direct_send.at[j],
            recv_sem=direct_recv.at[j],
            device_id=peers[j - 1],
            device_id_type=MESH_ID,
        )
        copy.start()
        sends.append(copy)
    hops = []
    for side, (target, lanes) in enumerate(((up, pl.ds(0, half)), (down, pl.ds(half, half)))):
        copy = pltpu.make_async_remote_copy(
            src_ref=x_ref.at[:, :, lanes],
            dst_ref=stage.at[side],
            send_sem=hop_send.at[side],
            recv_sem=hop_recv.at[side],
            device_id=(sec(target, y), dpi(target)),
            device_id_type=MESH_ID,
        )
        copy.start()
        hops.append(copy)
    forwards = []
    for side, (origin, target, lanes) in enumerate(
        ((down, up, pl.ds(0, half)), (up, down, pl.ds(half, half)))
    ):
        hops[side].wait_recv()
        for yy in range(4):
            copy = pltpu.make_async_remote_copy(
                src_ref=stage.at[side],
                dst_ref=o_ref.at[:, sec(origin, y), :, lanes],
                send_sem=fwd_send.at[side, yy],
                recv_sem=fwd_recv.at[side, y],
                device_id=(sec(target, yy), dpi(target)),
                device_id_type=MESH_ID,
            )
            copy.start()
            forwards.append(copy)
    for copy in sends:
        copy.wait()
    for copy in hops:
        copy.wait_send()
    for copy in forwards:
        copy.wait_send()
    for side, (origin, target, lanes) in enumerate(
        ((down, up, pl.ds(0, half)), (up, down, pl.ds(half, half)))
    ):
        for yy in range(4):
            pltpu.make_async_remote_copy(
                src_ref=stage.at[side],
                dst_ref=o_ref.at[:, sec(origin, y), :, lanes],
                send_sem=fwd_send.at[side, yy],
                recv_sem=fwd_recv.at[side, yy],
                device_id=(sec(target, yy), dpi(target)),
                device_id_type=MESH_ID,
            ).wait_recv()
    local.wait()


def relay_gather(x, n):
    samples, chunk, width = x.shape
    return pl.pallas_call(
        relay_gather_kernel,
        out_shape=jax.ShapeDtypeStruct((samples, n, chunk, width), x.dtype),
        in_specs=[pl.BlockSpec(memory_space=pl.ANY)],
        out_specs=pl.BlockSpec(memory_space=pl.ANY),
        scratch_shapes=[
            pltpu.VMEM((2, samples, chunk, width // 2), x.dtype),
            pltpu.SemaphoreType.DMA(()),
            pltpu.SemaphoreType.DMA((4,)),
            pltpu.SemaphoreType.DMA((4,)),
            pltpu.SemaphoreType.DMA((2,)),
            pltpu.SemaphoreType.DMA((2,)),
            pltpu.SemaphoreType.DMA((2, 4)),
            pltpu.SemaphoreType.DMA((2, 4)),
        ],
        compiler_params=pltpu.CompilerParams(collective_id=2, has_side_effects=True),
    )(x)


def exchange(x, n, scatter, collective_id):
    if scatter:
        out_shape = x.shape
    else:
        out_shape = (x.shape[0], n) + x.shape[1:]
    return pl.pallas_call(
        functools.partial(exchange_kernel, n, scatter),
        out_shape=jax.ShapeDtypeStruct(out_shape, x.dtype),
        in_specs=[pl.BlockSpec(memory_space=pl.ANY)],
        out_specs=pl.BlockSpec(memory_space=pl.ANY),
        scratch_shapes=[
            pltpu.SemaphoreType.DMA((n,)),
            pltpu.SemaphoreType.DMA((n,)),
            pltpu.SemaphoreType.DMA(()),
        ],
        compiler_params=pltpu.CompilerParams(collective_id=collective_id, has_side_effects=True),
    )(x)


def image_kernel(n, tiles, g_ref, wk_ref, wv_ref, o_ref, buf, send_sems, recv_sems, local_sem):
    me = lax.axis_index("section")
    row = lax.axis_index("dp")
    rows = g_ref.shape[0] // n
    half = g_ref.shape[1] // 2
    tile_w = wk_ref.shape[0] // tiles
    barrier = pltpu.get_barrier_semaphore()
    for k in range(1, n):
        pl.semaphore_signal(
            barrier, inc=1, device_id=(lax.rem(me + k, n), row), device_id_type=MESH_ID
        )
    pl.semaphore_wait(barrier, n - 1)

    def compute(t):
        cols = pl.ds(pl.multiple_of(t * tile_w, tile_w), tile_w)
        dims = (((1,), (1,)), ((), ()))
        acc = lax.dot_general(
            g_ref[:, pl.ds(0, half)], wk_ref[cols, :], dims, preferred_element_type=jnp.float32
        )
        acc = acc + lax.dot_general(
            g_ref[:, pl.ds(half, half)], wv_ref[cols, :], dims, preferred_element_type=jnp.float32
        )
        buf[:, cols] = acc.astype(buf.dtype)

    def send(t):
        cols = pl.ds(pl.multiple_of(t * tile_w, tile_w), tile_w)
        for k in range(1, n):
            peer = lax.rem(me + k, n)
            pltpu.make_async_remote_copy(
                src_ref=buf.at[pl.ds(pl.multiple_of(peer * rows, 16), rows), cols],
                dst_ref=o_ref.at[me, :, cols],
                send_sem=send_sems.at[k],
                recv_sem=recv_sems.at[k],
                device_id=(peer, row),
                device_id_type=MESH_ID,
            ).start()

    compute(0)

    def body(t, carry):
        compute(t)
        send(t - 1)
        return carry

    lax.fori_loop(1, tiles, body, 0)
    send(tiles - 1)
    own = pl.ds(pl.multiple_of(me * rows, 16), rows)
    local = pltpu.make_async_copy(buf.at[own, :], o_ref.at[me], local_sem)
    local.start()
    for k in range(1, n):
        peer = lax.rem(me + k, n)
        whole = pltpu.make_async_remote_copy(
            src_ref=buf.at[pl.ds(pl.multiple_of(peer * rows, 16), rows), :],
            dst_ref=o_ref.at[me],
            send_sem=send_sems.at[k],
            recv_sem=recv_sems.at[k],
            device_id=(peer, row),
            device_id_type=MESH_ID,
        )
        whole.wait_send()
        whole.wait_recv()
    local.wait()


def image_exchange(g, w_key, w_value, n):
    total_rows, kv = g.shape
    width = w_key.shape[0]
    tiles = 8
    return pl.pallas_call(
        functools.partial(image_kernel, n, tiles),
        out_shape=jax.ShapeDtypeStruct((n, total_rows // n, width), jnp.bfloat16),
        in_specs=[pl.BlockSpec(memory_space=pltpu.VMEM)] * 3,
        out_specs=pl.BlockSpec(memory_space=pl.ANY),
        scratch_shapes=[
            pltpu.VMEM((total_rows, width), jnp.bfloat16),
            pltpu.SemaphoreType.DMA((n,)),
            pltpu.SemaphoreType.DMA((n,)),
            pltpu.SemaphoreType.DMA(()),
        ],
        compiler_params=pltpu.CompilerParams(
            collective_id=3, has_side_effects=True, vmem_limit_bytes=60 * 1024 * 1024
        ),
        cost_estimate=pl.CostEstimate(
            flops=2 * total_rows * kv * width, bytes_accessed=2 * (kv + total_rows) * width,
            transcendentals=0,
        ),
    )(g, w_key, w_value)


def shards(queries, image_tokens, key_weight, value_weight, cotangent, tile_counts, text_lengths):
    n_section = lax.axis_size("section")
    samples_here, chunk, model_width = image_tokens.shape
    image_len = n_section * chunk
    tile_len = image_len // MAX_TILES
    w_key = key_weight[0]
    w_value = value_weight[0]
    query_local = queries[0]
    cotan_local = cotangent[0]
    late = [
        lax.all_gather(image_tokens[i], "section", axis=0, tiled=True)
        for i in range(1, samples_here)
    ]
    if n_section == 8 and lax.axis_size("dp") == 16:
        first = relay_gather(image_tokens[:1], n_section)
    else:
        first = exchange(image_tokens[:1], n_section, False, 0)
    token_list = [first.reshape(image_len, model_width)] + late
    keys_list = []
    values_list = []
    for sample_index in range(samples_here):
        tokens = token_list[sample_index]
        keys_list.append(
            jnp.dot(tokens, w_key, preferred_element_type=jnp.float32).astype(jnp.bfloat16)
        )
        values_list.append(
            jnp.dot(tokens, w_value, preferred_element_type=jnp.float32).astype(jnp.bfloat16)
        )
    keys_both = jnp.stack(keys_list)
    values_both = jnp.stack(values_list)
    key_limits = tile_counts * tile_len
    weights, value_grads = jax.vmap(attend_front)(
        query_local, keys_both, cotan_local, key_limits, text_lengths
    )
    all_tokens = jnp.concatenate(token_list, axis=0)
    value_term = jnp.einsum(
        "td,tk->dk", all_tokens, value_grads.reshape(samples_here * image_len, -1),
        preferred_element_type=jnp.float32,
    ).astype(jnp.bfloat16)
    value_term, weights = lax.optimization_barrier((value_term, weights))
    value_sum = lax.psum_scatter(value_term, "dp", scatter_dimension=0, tiled=True)
    query_grads, key_grads = jax.vmap(attend_back)(
        query_local, keys_both, values_both, cotan_local, text_lengths, weights
    )
    key_term = jnp.einsum(
        "td,tk->dk", all_tokens, key_grads.reshape(samples_here * image_len, -1),
        preferred_element_type=jnp.float32,
    ).astype(jnp.bfloat16)
    key_sum = lax.psum_scatter(key_term, "dp", scatter_dimension=0, tiled=True)
    query_out = query_grads[None]
    kv_grads = jnp.concatenate([key_grads, value_grads], axis=-1)
    by_slot = kv_grads.reshape(samples_here, n_section, chunk, -1).transpose(1, 0, 2, 3)
    received = image_exchange(
        by_slot.reshape(n_section * samples_here * chunk, -1), w_key, w_value, n_section
    )
    image_out = (
        jnp.sum(received.astype(jnp.float32), axis=0)
        .reshape(samples_here, chunk, model_width)
        .astype(jnp.bfloat16)
    )
    return (
        query_out,
        image_out,
        key_sum[None],
        value_sum[None],
    )


def solution(mesh):
    placed = (
        P("section", "dp", None, None),
        P("dp", "section", None),
        P("section", None, None),
        P("section", None, None),
        P("section", "dp", None, None),
        P("dp"),
        P("dp"),
    )
    return jax.shard_map(
        shards,
        mesh=mesh,
        in_specs=placed,
        out_specs=(
            P("section", "dp", None, None),
            P("dp", "section", None),
            P("section", "dp", None),
            P("section", "dp", None),
        ),
        check_vma=False,
    )
```

```python
import functools
import math

import jax
import jax.numpy as jnp
from jax import lax
from jax.experimental import pallas as pl
from jax.experimental.pallas import tpu as pltpu
from jax.sharding import PartitionSpec as P

QUERY_HEADS = 32
KEY_VALUE_HEADS = 4
HEAD_SIZE = 128
MAX_TILES = 4
MESH_ID = pl.DeviceIdType.MESH


def attend_one(queries, key_rows, value_rows, cotangent, key_limit, row_limit):
    total_rows = queries.shape[0]
    total_keys = key_rows.shape[0]
    group_width = QUERY_HEADS // KEY_VALUE_HEADS
    heads_of_queries = queries.reshape(total_rows, KEY_VALUE_HEADS, group_width, HEAD_SIZE)
    heads_of_keys = key_rows.reshape(total_keys, KEY_VALUE_HEADS, HEAD_SIZE)
    heads_of_values = value_rows.reshape(total_keys, KEY_VALUE_HEADS, HEAD_SIZE)
    row_live = (jnp.arange(total_rows) < row_limit)[:, None]
    active_cotangent = jnp.where(row_live, cotangent, jnp.zeros_like(cotangent))
    head_gradient = active_cotangent.reshape(total_rows, KEY_VALUE_HEADS, group_width, HEAD_SIZE)
    scaling = 1.0 / math.sqrt(HEAD_SIZE)
    scores = (
        jnp.einsum(
            "lhgd,nhd->hgln", heads_of_queries, heads_of_keys, preferred_element_type=jnp.float32
        )
        * scaling
    )
    key_live = jnp.arange(total_keys) < key_limit
    scores = jnp.where(key_live, scores, -jnp.inf)
    row_max = jnp.max(scores, axis=-1, keepdims=True)
    raised = jnp.exp(scores - row_max)
    weights = raised / jnp.sum(raised, axis=-1, keepdims=True)
    weights_low = weights.astype(jnp.bfloat16)
    value_gradient = jnp.einsum(
        "hgln,lhgd->nhd", weights_low, head_gradient, preferred_element_type=jnp.float32
    ).astype(jnp.bfloat16)
    prob_grad = jnp.einsum(
        "lhgd,nhd->hgln", head_gradient, heads_of_values, preferred_element_type=jnp.float32
    )
    row_dot = jnp.sum(weights * prob_grad, axis=-1, keepdims=True)
    score_grad = (weights * (prob_grad - row_dot) * scaling).astype(jnp.bfloat16)
    query_gradient = jnp.einsum(
        "hgln,nhd->lhgd", score_grad, heads_of_keys, preferred_element_type=jnp.float32
    ).astype(jnp.bfloat16)
    key_gradient = jnp.einsum(
        "hgln,lhgd->nhd", score_grad, heads_of_queries, preferred_element_type=jnp.float32
    ).astype(jnp.bfloat16)
    return (
        query_gradient.reshape(total_rows, QUERY_HEADS * HEAD_SIZE),
        key_gradient.reshape(total_keys, KEY_VALUE_HEADS * HEAD_SIZE),
        value_gradient.reshape(total_keys, KEY_VALUE_HEADS * HEAD_SIZE),
    )


def attend_front(queries, key_rows, cotangent, key_limit, row_limit):
    total_rows = queries.shape[0]
    total_keys = key_rows.shape[0]
    group_width = QUERY_HEADS // KEY_VALUE_HEADS
    heads_of_queries = queries.reshape(total_rows, KEY_VALUE_HEADS, group_width, HEAD_SIZE)
    heads_of_keys = key_rows.reshape(total_keys, KEY_VALUE_HEADS, HEAD_SIZE)
    row_live = (jnp.arange(total_rows) < row_limit)[:, None]
    active_cotangent = jnp.where(row_live, cotangent, jnp.zeros_like(cotangent))
    head_gradient = active_cotangent.reshape(total_rows, KEY_VALUE_HEADS, group_width, HEAD_SIZE)
    scaling = 1.0 / math.sqrt(HEAD_SIZE)
    scores = (
        jnp.einsum(
            "lhgd,nhd->hgln", heads_of_queries, heads_of_keys, preferred_element_type=jnp.float32
        )
        * scaling
    )
    key_live = jnp.arange(total_keys) < key_limit
    scores = jnp.where(key_live, scores, -jnp.inf)
    row_max = jnp.max(scores, axis=-1, keepdims=True)
    raised = jnp.exp(scores - row_max)
    weights = raised / jnp.sum(raised, axis=-1, keepdims=True)
    weights_low = weights.astype(jnp.bfloat16)
    value_gradient = jnp.einsum(
        "hgln,lhgd->nhd", weights_low, head_gradient, preferred_element_type=jnp.float32
    ).astype(jnp.bfloat16)
    return weights, value_gradient.reshape(total_keys, KEY_VALUE_HEADS * HEAD_SIZE)


def attend_back(queries, key_rows, value_rows, cotangent, row_limit, weights):
    total_rows = queries.shape[0]
    total_keys = key_rows.shape[0]
    group_width = QUERY_HEADS // KEY_VALUE_HEADS
    heads_of_queries = queries.reshape(total_rows, KEY_VALUE_HEADS, group_width, HEAD_SIZE)
    heads_of_keys = key_rows.reshape(total_keys, KEY_VALUE_HEADS, HEAD_SIZE)
    heads_of_values = value_rows.reshape(total_keys, KEY_VALUE_HEADS, HEAD_SIZE)
    row_live = (jnp.arange(total_rows) < row_limit)[:, None]
    active_cotangent = jnp.where(row_live, cotangent, jnp.zeros_like(cotangent))
    head_gradient = active_cotangent.reshape(total_rows, KEY_VALUE_HEADS, group_width, HEAD_SIZE)
    scaling = 1.0 / math.sqrt(HEAD_SIZE)
    prob_grad = jnp.einsum(
        "lhgd,nhd->hgln", head_gradient, heads_of_values, preferred_element_type=jnp.float32
    )
    row_dot = jnp.sum(weights * prob_grad, axis=-1, keepdims=True)
    score_grad = (weights * (prob_grad - row_dot) * scaling).astype(jnp.bfloat16)
    query_gradient = jnp.einsum(
        "hgln,nhd->lhgd", score_grad, heads_of_keys, preferred_element_type=jnp.float32
    ).astype(jnp.bfloat16)
    key_gradient = jnp.einsum(
        "hgln,lhgd->nhd", score_grad, heads_of_queries, preferred_element_type=jnp.float32
    ).astype(jnp.bfloat16)
    return (
        query_gradient.reshape(total_rows, QUERY_HEADS * HEAD_SIZE),
        key_gradient.reshape(total_keys, KEY_VALUE_HEADS * HEAD_SIZE),
    )


def exchange_kernel(n, scatter, x_ref, o_ref, send_sems, recv_sems, local_sem):
    me = lax.axis_index("section")
    row = lax.axis_index("dp")
    barrier = pltpu.get_barrier_semaphore()
    for k in range(1, n):
        pl.semaphore_signal(
            barrier, inc=1, device_id=(lax.rem(me + k, n), row), device_id_type=MESH_ID
        )
    pl.semaphore_wait(barrier, n - 1)
    own = x_ref.at[:, me] if scatter else x_ref
    local = pltpu.make_async_copy(own, o_ref.at[:, me], local_sem)
    local.start()
    copies = []
    for k in range(1, n):
        peer = lax.rem(me + k, n)
        src = x_ref.at[:, peer] if scatter else x_ref
        copy = pltpu.make_async_remote_copy(
            src_ref=src,
            dst_ref=o_ref.at[:, me],
            send_sem=send_sems.at[k],
            recv_sem=recv_sems.at[k],
            device_id=(peer, row),
            device_id_type=MESH_ID,
        )
        copy.start()
        copies.append(copy)
    for copy in copies:
        copy.wait()
    local.wait()


def relay_gather_kernel(x_ref, o_ref, stage, local_sem, direct_send, direct_recv,
                        hop_send, hop_recv, fwd_send, fwd_recv):
    s = lax.axis_index("section")
    r = lax.axis_index("dp")
    y = lax.rem(s, 4)
    z = (s // 4) * 2 + r // 8
    xc = lax.rem(r, 8)
    half = x_ref.shape[-1] // 2

    def sec(zz, yy):
        return (lax.rem(zz, 4) // 2) * 4 + yy

    def dpi(zz):
        return lax.rem(zz, 2) * 8 + xc

    up, down = z + 1, z + 3
    peers = [(sec(z, lax.rem(y + j, 4)), r) for j in range(1, 4)]
    for yy in range(4):
        peers.append((sec(up, yy), dpi(up)))
        peers.append((sec(down, yy), dpi(down)))
    barrier = pltpu.get_barrier_semaphore()
    for peer in peers:
        pl.semaphore_signal(barrier, inc=1, device_id=peer, device_id_type=MESH_ID)
    pl.semaphore_wait(barrier, len(peers))

    local = pltpu.make_async_copy(x_ref, o_ref.at[:, s], local_sem)
    local.start()
    sends = []
    for j in range(1, 4):
        copy = pltpu.make_async_remote_copy(
            src_ref=x_ref,
            dst_ref=o_ref.at[:, s],
            send_sem=direct_send.at[j],
            recv_sem=direct_recv.at[j],
            device_id=peers[j - 1],
            device_id_type=MESH_ID,
        )
        copy.start()
        sends.append(copy)
    hops = []
    for side, (target, lanes) in enumerate(((up, pl.ds(0, half)), (down, pl.ds(half, half)))):
        copy = pltpu.make_async_remote_copy(
            src_ref=x_ref.at[:, :, lanes],
            dst_ref=stage.at[side],
            send_sem=hop_send.at[side],
            recv_sem=hop_recv.at[side],
            device_id=(sec(target, y), dpi(target)),
            device_id_type=MESH_ID,
        )
        copy.start()
        hops.append(copy)
    forwards = []
    for side, (origin, target, lanes) in enumerate(
        ((down, up, pl.ds(0, half)), (up, down, pl.ds(half, half)))
    ):
        hops[side].wait_recv()
        for yy in range(4):
            copy = pltpu.make_async_remote_copy(
                src_ref=stage.at[side],
                dst_ref=o_ref.at[:, sec(origin, y), :, lanes],
                send_sem=fwd_send.at[side, yy],
                recv_sem=fwd_recv.at[side, y],
                device_id=(sec(target, yy), dpi(target)),
                device_id_type=MESH_ID,
            )
            copy.start()
            forwards.append(copy)
    for copy in sends:
        copy.wait()
    for copy in hops:
        copy.wait_send()
    for copy in forwards:
        copy.wait_send()
    for side, (origin, target, lanes) in enumerate(
        ((down, up, pl.ds(0, half)), (up, down, pl.ds(half, half)))
    ):
        for yy in range(4):
            pltpu.make_async_remote_copy(
                src_ref=stage.at[side],
                dst_ref=o_ref.at[:, sec(origin, y), :, lanes],
                send_sem=fwd_send.at[side, yy],
                recv_sem=fwd_recv.at[side, yy],
                device_id=(sec(target, yy), dpi(target)),
                device_id_type=MESH_ID,
            ).wait_recv()
    local.wait()


def relay_gather(x, n):
    samples, chunk, width = x.shape
    return pl.pallas_call(
        relay_gather_kernel,
        out_shape=jax.ShapeDtypeStruct((samples, n, chunk, width), x.dtype),
        in_specs=[pl.BlockSpec(memory_space=pl.ANY)],
        out_specs=pl.BlockSpec(memory_space=pl.ANY),
        scratch_shapes=[
            pltpu.VMEM((2, samples, chunk, width // 2), x.dtype),
            pltpu.SemaphoreType.DMA(()),
            pltpu.SemaphoreType.DMA((4,)),
            pltpu.SemaphoreType.DMA((4,)),
            pltpu.SemaphoreType.DMA((2,)),
            pltpu.SemaphoreType.DMA((2,)),
            pltpu.SemaphoreType.DMA((2, 4)),
            pltpu.SemaphoreType.DMA((2, 4)),
        ],
        compiler_params=pltpu.CompilerParams(collective_id=2, has_side_effects=True),
    )(x)


def exchange(x, n, scatter, collective_id):
    if scatter:
        out_shape = x.shape
    else:
        out_shape = (x.shape[0], n) + x.shape[1:]
    return pl.pallas_call(
        functools.partial(exchange_kernel, n, scatter),
        out_shape=jax.ShapeDtypeStruct(out_shape, x.dtype),
        in_specs=[pl.BlockSpec(memory_space=pl.ANY)],
        out_specs=pl.BlockSpec(memory_space=pl.ANY),
        scratch_shapes=[
            pltpu.SemaphoreType.DMA((n,)),
            pltpu.SemaphoreType.DMA((n,)),
            pltpu.SemaphoreType.DMA(()),
        ],
        compiler_params=pltpu.CompilerParams(collective_id=collective_id, has_side_effects=True),
    )(x)


def image_kernel(n, tiles, g_ref, wk_ref, wv_ref, o_ref, buf, send_sems, recv_sems, local_sem):
    me = lax.axis_index("section")
    row = lax.axis_index("dp")
    rows = g_ref.shape[0] // n
    half = g_ref.shape[1] // 2
    tile_w = wk_ref.shape[0] // tiles
    barrier = pltpu.get_barrier_semaphore()
    for k in range(1, n):
        pl.semaphore_signal(
            barrier, inc=1, device_id=(lax.rem(me + k, n), row), device_id_type=MESH_ID
        )
    pl.semaphore_wait(barrier, n - 1)

    def compute(t):
        cols = pl.ds(pl.multiple_of(t * tile_w, tile_w), tile_w)
        dims = (((1,), (1,)), ((), ()))
        acc = lax.dot_general(
            g_ref[:, pl.ds(0, half)], wk_ref[cols, :], dims, preferred_element_type=jnp.float32
        )
        acc = acc + lax.dot_general(
            g_ref[:, pl.ds(half, half)], wv_ref[cols, :], dims, preferred_element_type=jnp.float32
        )
        buf[:, cols] = acc.astype(buf.dtype)

    def send(t):
        cols = pl.ds(pl.multiple_of(t * tile_w, tile_w), tile_w)
        for k in range(1, n):
            peer = lax.rem(me + k, n)
            pltpu.make_async_remote_copy(
                src_ref=buf.at[pl.ds(pl.multiple_of(peer * rows, 16), rows), cols],
                dst_ref=o_ref.at[me, :, cols],
                send_sem=send_sems.at[k],
                recv_sem=recv_sems.at[k],
                device_id=(peer, row),
                device_id_type=MESH_ID,
            ).start()

    compute(0)

    def body(t, carry):
        compute(t)
        send(t - 1)
        return carry

    lax.fori_loop(1, tiles, body, 0)
    send(tiles - 1)
    own = pl.ds(pl.multiple_of(me * rows, 16), rows)
    local = pltpu.make_async_copy(buf.at[own, :], o_ref.at[me], local_sem)
    local.start()
    for k in range(1, n):
        peer = lax.rem(me + k, n)
        whole = pltpu.make_async_remote_copy(
            src_ref=buf.at[pl.ds(pl.multiple_of(peer * rows, 16), rows), :],
            dst_ref=o_ref.at[me],
            send_sem=send_sems.at[k],
            recv_sem=recv_sems.at[k],
            device_id=(peer, row),
            device_id_type=MESH_ID,
        )
        whole.wait_send()
        whole.wait_recv()
    local.wait()


def image_exchange(g, w_key, w_value, n):
    total_rows, kv = g.shape
    width = w_key.shape[0]
    tiles = 8
    return pl.pallas_call(
        functools.partial(image_kernel, n, tiles),
        out_shape=jax.ShapeDtypeStruct((n, total_rows // n, width), jnp.bfloat16),
        in_specs=[pl.BlockSpec(memory_space=pltpu.VMEM)] * 3,
        out_specs=pl.BlockSpec(memory_space=pl.ANY),
        scratch_shapes=[
            pltpu.VMEM((total_rows, width), jnp.bfloat16),
            pltpu.SemaphoreType.DMA((n,)),
            pltpu.SemaphoreType.DMA((n,)),
            pltpu.SemaphoreType.DMA(()),
        ],
        compiler_params=pltpu.CompilerParams(
            collective_id=3, has_side_effects=True, vmem_limit_bytes=60 * 1024 * 1024
        ),
        cost_estimate=pl.CostEstimate(
            flops=2 * total_rows * kv * width, bytes_accessed=2 * (kv + total_rows) * width,
            transcendentals=0,
        ),
    )(g, w_key, w_value)


def shards(queries, image_tokens, key_weight, value_weight, cotangent, tile_counts, text_lengths):
    n_section = lax.axis_size("section")
    samples_here, chunk, model_width = image_tokens.shape
    image_len = n_section * chunk
    tile_len = image_len // MAX_TILES
    w_key = key_weight[0]
    w_value = value_weight[0]
    query_local = queries[0]
    cotan_local = cotangent[0]
    late = [
        lax.all_gather(image_tokens[i], "section", axis=0, tiled=True)
        for i in range(1, samples_here)
    ]
    if n_section == 8 and lax.axis_size("dp") == 16:
        first = relay_gather(image_tokens[:1], n_section)
    else:
        first = exchange(image_tokens[:1], n_section, False, 0)
    token_list = [first.reshape(image_len, model_width)] + late
    keys_list = []
    values_list = []
    for sample_index in range(samples_here):
        tokens = token_list[sample_index]
        keys_list.append(
            jnp.dot(tokens, w_key, preferred_element_type=jnp.float32).astype(jnp.bfloat16)
        )
        values_list.append(
            jnp.dot(tokens, w_value, preferred_element_type=jnp.float32).astype(jnp.bfloat16)
        )
    keys_both = jnp.stack(keys_list)
    values_both = jnp.stack(values_list)
    key_limits = tile_counts * tile_len
    fronts = [
        attend_front(
            query_local[i], keys_list[i], cotan_local[i], key_limits[i], text_lengths[i]
        )
        for i in range(samples_here)
    ]
    weights = jnp.stack([front[0] for front in fronts])
    value_grads = jnp.stack([front[1] for front in fronts])
    all_tokens = jnp.concatenate(token_list, axis=0)
    value_term = jnp.einsum(
        "td,tk->dk", all_tokens, value_grads.reshape(samples_here * image_len, -1),
        preferred_element_type=jnp.float32,
    ).astype(jnp.bfloat16)
    value_term, weights = lax.optimization_barrier((value_term, weights))
    value_sum = lax.psum_scatter(value_term, "dp", scatter_dimension=0, tiled=True)
    query_grads, key_grads = jax.vmap(attend_back)(
        query_local, keys_both, values_both, cotan_local, text_lengths, weights
    )
    key_term = jnp.einsum(
        "td,tk->dk", all_tokens, key_grads.reshape(samples_here * image_len, -1),
        preferred_element_type=jnp.float32,
    ).astype(jnp.bfloat16)
    key_sum = lax.psum_scatter(key_term, "dp", scatter_dimension=0, tiled=True)
    query_out = query_grads[None]
    kv_grads = jnp.concatenate([key_grads, value_grads], axis=-1)
    by_slot = kv_grads.reshape(samples_here, n_section, chunk, -1).transpose(1, 0, 2, 3)
    received = image_exchange(
        by_slot.reshape(n_section * samples_here * chunk, -1), w_key, w_value, n_section
    )
    image_out = (
        jnp.sum(received.astype(jnp.float32), axis=0)
        .reshape(samples_here, chunk, model_width)
        .astype(jnp.bfloat16)
    )
    return (
        query_out,
        image_out,
        key_sum[None],
        value_sum[None],
    )


def solution(mesh):
    placed = (
        P("section", "dp", None, None),
        P("dp", "section", None),
        P("section", None, None),
        P("section", None, None),
        P("section", "dp", None, None),
        P("dp"),
        P("dp"),
    )
    return jax.shard_map(
        shards,
        mesh=mesh,
        in_specs=placed,
        out_specs=(
            P("section", "dp", None, None),
            P("dp", "section", None),
            P("section", "dp", None),
            P("section", "dp", None),
        ),
        check_vma=False,
    )
```

```python
import functools
import math

import jax
import jax.numpy as jnp
from jax import lax
from jax.experimental import pallas as pl
from jax.experimental.pallas import tpu as pltpu
from jax.sharding import PartitionSpec as P

QUERY_HEADS = 32
KEY_VALUE_HEADS = 4
HEAD_SIZE = 128
MAX_TILES = 4
MESH_ID = pl.DeviceIdType.MESH


def attend_one(queries, key_rows, value_rows, cotangent, key_limit, row_limit):
    total_rows = queries.shape[0]
    total_keys = key_rows.shape[0]
    group_width = QUERY_HEADS // KEY_VALUE_HEADS
    heads_of_queries = queries.reshape(total_rows, KEY_VALUE_HEADS, group_width, HEAD_SIZE)
    heads_of_keys = key_rows.reshape(total_keys, KEY_VALUE_HEADS, HEAD_SIZE)
    heads_of_values = value_rows.reshape(total_keys, KEY_VALUE_HEADS, HEAD_SIZE)
    row_live = (jnp.arange(total_rows) < row_limit)[:, None]
    active_cotangent = jnp.where(row_live, cotangent, jnp.zeros_like(cotangent))
    head_gradient = active_cotangent.reshape(total_rows, KEY_VALUE_HEADS, group_width, HEAD_SIZE)
    scaling = 1.0 / math.sqrt(HEAD_SIZE)
    scores = (
        jnp.einsum(
            "lhgd,nhd->hgln", heads_of_queries, heads_of_keys, preferred_element_type=jnp.float32
        )
        * scaling
    )
    key_live = jnp.arange(total_keys) < key_limit
    scores = jnp.where(key_live, scores, -jnp.inf)
    row_max = jnp.max(scores, axis=-1, keepdims=True)
    raised = jnp.exp(scores - row_max)
    weights = raised / jnp.sum(raised, axis=-1, keepdims=True)
    weights_low = weights.astype(jnp.bfloat16)
    value_gradient = jnp.einsum(
        "hgln,lhgd->nhd", weights_low, head_gradient, preferred_element_type=jnp.float32
    ).astype(jnp.bfloat16)
    prob_grad = jnp.einsum(
        "lhgd,nhd->hgln", head_gradient, heads_of_values, preferred_element_type=jnp.float32
    )
    row_dot = jnp.sum(weights * prob_grad, axis=-1, keepdims=True)
    score_grad = (weights * (prob_grad - row_dot) * scaling).astype(jnp.bfloat16)
    query_gradient = jnp.einsum(
        "hgln,nhd->lhgd", score_grad, heads_of_keys, preferred_element_type=jnp.float32
    ).astype(jnp.bfloat16)
    key_gradient = jnp.einsum(
        "hgln,lhgd->nhd", score_grad, heads_of_queries, preferred_element_type=jnp.float32
    ).astype(jnp.bfloat16)
    return (
        query_gradient.reshape(total_rows, QUERY_HEADS * HEAD_SIZE),
        key_gradient.reshape(total_keys, KEY_VALUE_HEADS * HEAD_SIZE),
        value_gradient.reshape(total_keys, KEY_VALUE_HEADS * HEAD_SIZE),
    )


def attend_front(queries, key_rows, cotangent, key_limit, row_limit):
    total_rows = queries.shape[0]
    total_keys = key_rows.shape[0]
    group_width = QUERY_HEADS // KEY_VALUE_HEADS
    heads_of_queries = queries.reshape(total_rows, KEY_VALUE_HEADS, group_width, HEAD_SIZE)
    heads_of_keys = key_rows.reshape(total_keys, KEY_VALUE_HEADS, HEAD_SIZE)
    row_live = (jnp.arange(total_rows) < row_limit)[:, None]
    active_cotangent = jnp.where(row_live, cotangent, jnp.zeros_like(cotangent))
    head_gradient = active_cotangent.reshape(total_rows, KEY_VALUE_HEADS, group_width, HEAD_SIZE)
    scaling = 1.0 / math.sqrt(HEAD_SIZE)
    scores = (
        jnp.einsum(
            "lhgd,nhd->hgln", heads_of_queries, heads_of_keys, preferred_element_type=jnp.float32
        )
        * scaling
    )
    key_live = jnp.arange(total_keys) < key_limit
    scores = jnp.where(key_live, scores, -jnp.inf)
    row_max = jnp.max(scores, axis=-1, keepdims=True)
    raised = jnp.exp(scores - row_max)
    weights = raised / jnp.sum(raised, axis=-1, keepdims=True)
    weights_low = weights.astype(jnp.bfloat16)
    value_gradient = jnp.einsum(
        "hgln,lhgd->nhd", weights_low, head_gradient, preferred_element_type=jnp.float32
    ).astype(jnp.bfloat16)
    return weights, value_gradient.reshape(total_keys, KEY_VALUE_HEADS * HEAD_SIZE)


def attend_back(queries, key_rows, value_rows, cotangent, row_limit, weights):
    total_rows = queries.shape[0]
    total_keys = key_rows.shape[0]
    group_width = QUERY_HEADS // KEY_VALUE_HEADS
    heads_of_queries = queries.reshape(total_rows, KEY_VALUE_HEADS, group_width, HEAD_SIZE)
    heads_of_keys = key_rows.reshape(total_keys, KEY_VALUE_HEADS, HEAD_SIZE)
    heads_of_values = value_rows.reshape(total_keys, KEY_VALUE_HEADS, HEAD_SIZE)
    row_live = (jnp.arange(total_rows) < row_limit)[:, None]
    active_cotangent = jnp.where(row_live, cotangent, jnp.zeros_like(cotangent))
    head_gradient = active_cotangent.reshape(total_rows, KEY_VALUE_HEADS, group_width, HEAD_SIZE)
    scaling = 1.0 / math.sqrt(HEAD_SIZE)
    prob_grad = jnp.einsum(
        "lhgd,nhd->hgln", head_gradient, heads_of_values, preferred_element_type=jnp.float32
    )
    row_dot = jnp.sum(weights * prob_grad, axis=-1, keepdims=True)
    score_grad = (weights * (prob_grad - row_dot) * scaling).astype(jnp.bfloat16)
    query_gradient = jnp.einsum(
        "hgln,nhd->lhgd", score_grad, heads_of_keys, preferred_element_type=jnp.float32
    ).astype(jnp.bfloat16)
    key_gradient = jnp.einsum(
        "hgln,lhgd->nhd", score_grad, heads_of_queries, preferred_element_type=jnp.float32
    ).astype(jnp.bfloat16)
    return (
        query_gradient.reshape(total_rows, QUERY_HEADS * HEAD_SIZE),
        key_gradient.reshape(total_keys, KEY_VALUE_HEADS * HEAD_SIZE),
    )


def exchange_kernel(n, scatter, x_ref, o_ref, send_sems, recv_sems, local_sem):
    me = lax.axis_index("section")
    row = lax.axis_index("dp")
    barrier = pltpu.get_barrier_semaphore()
    for k in range(1, n):
        pl.semaphore_signal(
            barrier, inc=1, device_id=(lax.rem(me + k, n), row), device_id_type=MESH_ID
        )
    pl.semaphore_wait(barrier, n - 1)
    own = x_ref.at[:, me] if scatter else x_ref
    local = pltpu.make_async_copy(own, o_ref.at[:, me], local_sem)
    local.start()
    copies = []
    for k in range(1, n):
        peer = lax.rem(me + k, n)
        src = x_ref.at[:, peer] if scatter else x_ref
        copy = pltpu.make_async_remote_copy(
            src_ref=src,
            dst_ref=o_ref.at[:, me],
            send_sem=send_sems.at[k],
            recv_sem=recv_sems.at[k],
            device_id=(peer, row),
            device_id_type=MESH_ID,
        )
        copy.start()
        copies.append(copy)
    for copy in copies:
        copy.wait()
    local.wait()


def relay_gather_kernel(x_ref, o_ref, stage, local_sem, direct_send, direct_recv,
                        hop_send, hop_recv, fwd_send, fwd_recv):
    s = lax.axis_index("section")
    r = lax.axis_index("dp")
    y = lax.rem(s, 4)
    z = (s // 4) * 2 + r // 8
    xc = lax.rem(r, 8)
    half = x_ref.shape[-1] // 2

    def sec(zz, yy):
        return (lax.rem(zz, 4) // 2) * 4 + yy

    def dpi(zz):
        return lax.rem(zz, 2) * 8 + xc

    up, down = z + 1, z + 3
    peers = [(sec(z, lax.rem(y + j, 4)), r) for j in range(1, 4)]
    for yy in range(4):
        peers.append((sec(up, yy), dpi(up)))
        peers.append((sec(down, yy), dpi(down)))
    barrier = pltpu.get_barrier_semaphore()
    for peer in peers:
        pl.semaphore_signal(barrier, inc=1, device_id=peer, device_id_type=MESH_ID)
    pl.semaphore_wait(barrier, len(peers))

    local = pltpu.make_async_copy(x_ref, o_ref.at[:, s], local_sem)
    local.start()
    sends = []
    for j in range(1, 4):
        copy = pltpu.make_async_remote_copy(
            src_ref=x_ref,
            dst_ref=o_ref.at[:, s],
            send_sem=direct_send.at[j],
            recv_sem=direct_recv.at[j],
            device_id=peers[j - 1],
            device_id_type=MESH_ID,
        )
        copy.start()
        sends.append(copy)
    hops = []
    for side, (target, lanes) in enumerate(((up, pl.ds(0, half)), (down, pl.ds(half, half)))):
        copy = pltpu.make_async_remote_copy(
            src_ref=x_ref.at[:, :, lanes],
            dst_ref=stage.at[side],
            send_sem=hop_send.at[side],
            recv_sem=hop_recv.at[side],
            device_id=(sec(target, y), dpi(target)),
            device_id_type=MESH_ID,
        )
        copy.start()
        hops.append(copy)
    forwards = []
    for side, (origin, target, lanes) in enumerate(
        ((down, up, pl.ds(0, half)), (up, down, pl.ds(half, half)))
    ):
        hops[side].wait_recv()
        for yy in range(4):
            copy = pltpu.make_async_remote_copy(
                src_ref=stage.at[side],
                dst_ref=o_ref.at[:, sec(origin, y), :, lanes],
                send_sem=fwd_send.at[side, yy],
                recv_sem=fwd_recv.at[side, y],
                device_id=(sec(target, yy), dpi(target)),
                device_id_type=MESH_ID,
            )
            copy.start()
            forwards.append(copy)
    for copy in sends:
        copy.wait()
    for copy in hops:
        copy.wait_send()
    for copy in forwards:
        copy.wait_send()
    for side, (origin, target, lanes) in enumerate(
        ((down, up, pl.ds(0, half)), (up, down, pl.ds(half, half)))
    ):
        for yy in range(4):
            pltpu.make_async_remote_copy(
                src_ref=stage.at[side],
                dst_ref=o_ref.at[:, sec(origin, y), :, lanes],
                send_sem=fwd_send.at[side, yy],
                recv_sem=fwd_recv.at[side, yy],
                device_id=(sec(target, yy), dpi(target)),
                device_id_type=MESH_ID,
            ).wait_recv()
    local.wait()


def relay_gather(x, n):
    samples, chunk, width = x.shape
    return pl.pallas_call(
        relay_gather_kernel,
        out_shape=jax.ShapeDtypeStruct((samples, n, chunk, width), x.dtype),
        in_specs=[pl.BlockSpec(memory_space=pl.ANY)],
        out_specs=pl.BlockSpec(memory_space=pl.ANY),
        scratch_shapes=[
            pltpu.VMEM((2, samples, chunk, width // 2), x.dtype),
            pltpu.SemaphoreType.DMA(()),
            pltpu.SemaphoreType.DMA((4,)),
            pltpu.SemaphoreType.DMA((4,)),
            pltpu.SemaphoreType.DMA((2,)),
            pltpu.SemaphoreType.DMA((2,)),
            pltpu.SemaphoreType.DMA((2, 4)),
            pltpu.SemaphoreType.DMA((2, 4)),
        ],
        compiler_params=pltpu.CompilerParams(collective_id=2, has_side_effects=True),
    )(x)


def exchange(x, n, scatter, collective_id):
    if scatter:
        out_shape = x.shape
    else:
        out_shape = (x.shape[0], n) + x.shape[1:]
    return pl.pallas_call(
        functools.partial(exchange_kernel, n, scatter),
        out_shape=jax.ShapeDtypeStruct(out_shape, x.dtype),
        in_specs=[pl.BlockSpec(memory_space=pl.ANY)],
        out_specs=pl.BlockSpec(memory_space=pl.ANY),
        scratch_shapes=[
            pltpu.SemaphoreType.DMA((n,)),
            pltpu.SemaphoreType.DMA((n,)),
            pltpu.SemaphoreType.DMA(()),
        ],
        compiler_params=pltpu.CompilerParams(collective_id=collective_id, has_side_effects=True),
    )(x)


def image_kernel(n, tiles, g_ref, wk_hbm, wv_hbm, o_ref, buf, wk_ref, wv_ref, weight_sems,
                 send_sems, recv_sems, local_sem):
    me = lax.axis_index("section")
    row = lax.axis_index("dp")
    rows = g_ref.shape[0] // n
    half = g_ref.shape[1] // 2
    tile_w = wk_ref.shape[0] // tiles

    def weight_copies(t):
        part = pl.ds(pl.multiple_of(t * tile_w, tile_w), tile_w)
        return [
            pltpu.make_async_copy(src.at[part], dst.at[part], weight_sems.at[i, t])
            for i, (src, dst) in enumerate(((wk_hbm, wk_ref), (wv_hbm, wv_ref)))
        ]

    for t in range(tiles):
        for copy in weight_copies(t):
            copy.start()
    barrier = pltpu.get_barrier_semaphore()
    for k in range(1, n):
        pl.semaphore_signal(
            barrier, inc=1, device_id=(lax.rem(me + k, n), row), device_id_type=MESH_ID
        )
    pl.semaphore_wait(barrier, n - 1)

    def compute(t):
        for copy in weight_copies(t):
            copy.wait()
        cols = pl.ds(pl.multiple_of(t * tile_w, tile_w), tile_w)
        dims = (((1,), (1,)), ((), ()))
        acc = lax.dot_general(
            g_ref[:, pl.ds(0, half)], wk_ref[cols, :], dims, preferred_element_type=jnp.float32
        )
        acc = acc + lax.dot_general(
            g_ref[:, pl.ds(half, half)], wv_ref[cols, :], dims, preferred_element_type=jnp.float32
        )
        buf[:, cols] = acc.astype(buf.dtype)

    def send(t):
        cols = pl.ds(pl.multiple_of(t * tile_w, tile_w), tile_w)
        for k in range(1, n):
            peer = lax.rem(me + k, n)
            pltpu.make_async_remote_copy(
                src_ref=buf.at[pl.ds(pl.multiple_of(peer * rows, 16), rows), cols],
                dst_ref=o_ref.at[me, :, cols],
                send_sem=send_sems.at[k],
                recv_sem=recv_sems.at[k],
                device_id=(peer, row),
                device_id_type=MESH_ID,
            ).start()

    compute(0)

    def body(t, carry):
        compute(t)
        send(t - 1)
        return carry

    lax.fori_loop(1, tiles, body, 0)
    send(tiles - 1)
    own = pl.ds(pl.multiple_of(me * rows, 16), rows)
    local = pltpu.make_async_copy(buf.at[own, :], o_ref.at[me], local_sem)
    local.start()
    for k in range(1, n):
        peer = lax.rem(me + k, n)
        whole = pltpu.make_async_remote_copy(
            src_ref=buf.at[pl.ds(pl.multiple_of(peer * rows, 16), rows), :],
            dst_ref=o_ref.at[me],
            send_sem=send_sems.at[k],
            recv_sem=recv_sems.at[k],
            device_id=(peer, row),
            device_id_type=MESH_ID,
        )
        whole.wait_send()
        whole.wait_recv()
    local.wait()


def image_exchange(g, w_key, w_value, n):
    total_rows, kv = g.shape
    width = w_key.shape[0]
    tiles = 8
    return pl.pallas_call(
        functools.partial(image_kernel, n, tiles),
        out_shape=jax.ShapeDtypeStruct((n, total_rows // n, width), jnp.bfloat16),
        in_specs=[
            pl.BlockSpec(memory_space=pltpu.VMEM),
            pl.BlockSpec(memory_space=pl.ANY),
            pl.BlockSpec(memory_space=pl.ANY),
        ],
        out_specs=pl.BlockSpec(memory_space=pl.ANY),
        scratch_shapes=[
            pltpu.VMEM((total_rows, width), jnp.bfloat16),
            pltpu.VMEM(w_key.shape, w_key.dtype),
            pltpu.VMEM(w_value.shape, w_value.dtype),
            pltpu.SemaphoreType.DMA((2, tiles)),
            pltpu.SemaphoreType.DMA((n,)),
            pltpu.SemaphoreType.DMA((n,)),
            pltpu.SemaphoreType.DMA(()),
        ],
        compiler_params=pltpu.CompilerParams(
            collective_id=3, has_side_effects=True, vmem_limit_bytes=60 * 1024 * 1024
        ),
        cost_estimate=pl.CostEstimate(
            flops=2 * total_rows * kv * width, bytes_accessed=2 * (kv + total_rows) * width,
            transcendentals=0,
        ),
    )(g, w_key, w_value)


def shards(queries, image_tokens, key_weight, value_weight, cotangent, tile_counts, text_lengths):
    n_section = lax.axis_size("section")
    samples_here, chunk, model_width = image_tokens.shape
    image_len = n_section * chunk
    tile_len = image_len // MAX_TILES
    w_key = key_weight[0]
    w_value = value_weight[0]
    query_local = queries[0]
    cotan_local = cotangent[0]
    late = [
        lax.all_gather(image_tokens[i], "section", axis=0, tiled=True)
        for i in range(1, samples_here)
    ]
    if n_section == 8 and lax.axis_size("dp") == 16:
        first = relay_gather(image_tokens[:1], n_section)
    else:
        first = exchange(image_tokens[:1], n_section, False, 0)
    token_list = [first.reshape(image_len, model_width)] + late
    keys_list = []
    values_list = []
    for sample_index in range(samples_here):
        tokens = token_list[sample_index]
        keys_list.append(
            jnp.dot(tokens, w_key, preferred_element_type=jnp.float32).astype(jnp.bfloat16)
        )
        values_list.append(
            jnp.dot(tokens, w_value, preferred_element_type=jnp.float32).astype(jnp.bfloat16)
        )
    keys_both = jnp.stack(keys_list)
    values_both = jnp.stack(values_list)
    key_limits = tile_counts * tile_len
    weights, value_grads = jax.vmap(attend_front)(
        query_local, keys_both, cotan_local, key_limits, text_lengths
    )
    all_tokens = jnp.concatenate(token_list, axis=0)
    value_term = jnp.einsum(
        "td,tk->dk", all_tokens, value_grads.reshape(samples_here * image_len, -1),
        preferred_element_type=jnp.float32,
    ).astype(jnp.bfloat16)
    value_term, weights = lax.optimization_barrier((value_term, weights))
    value_sum = lax.psum_scatter(value_term, "dp", scatter_dimension=0, tiled=True)
    query_grads, key_grads = jax.vmap(attend_back)(
        query_local, keys_both, values_both, cotan_local, text_lengths, weights
    )
    key_term = jnp.einsum(
        "td,tk->dk", all_tokens, key_grads.reshape(samples_here * image_len, -1),
        preferred_element_type=jnp.float32,
    ).astype(jnp.bfloat16)
    key_sum = lax.psum_scatter(key_term, "dp", scatter_dimension=0, tiled=True)
    query_out = query_grads[None]
    kv_grads = jnp.concatenate([key_grads, value_grads], axis=-1)
    by_slot = kv_grads.reshape(samples_here, n_section, chunk, -1).transpose(1, 0, 2, 3)
    received = image_exchange(
        by_slot.reshape(n_section * samples_here * chunk, -1), w_key, w_value, n_section
    )
    image_out = (
        jnp.sum(received.astype(jnp.float32), axis=0)
        .reshape(samples_here, chunk, model_width)
        .astype(jnp.bfloat16)
    )
    return (
        query_out,
        image_out,
        key_sum[None],
        value_sum[None],
    )


def solution(mesh):
    placed = (
        P("section", "dp", None, None),
        P("dp", "section", None),
        P("section", None, None),
        P("section", None, None),
        P("section", "dp", None, None),
        P("dp"),
        P("dp"),
    )
    return jax.shard_map(
        shards,
        mesh=mesh,
        in_specs=placed,
        out_specs=(
            P("section", "dp", None, None),
            P("dp", "section", None),
            P("section", "dp", None),
            P("section", "dp", None),
        ),
        check_vma=False,
    )
```

```python
import functools
import math

import jax
import jax.numpy as jnp
from jax import lax
from jax.experimental import pallas as pl
from jax.experimental.pallas import tpu as pltpu
from jax.sharding import PartitionSpec as P

QUERY_HEADS = 32
KEY_VALUE_HEADS = 4
HEAD_SIZE = 128
MAX_TILES = 4
MESH_ID = pl.DeviceIdType.MESH


def attend_one(queries, key_rows, value_rows, cotangent, key_limit, row_limit):
    total_rows = queries.shape[0]
    total_keys = key_rows.shape[0]
    group_width = QUERY_HEADS // KEY_VALUE_HEADS
    heads_of_queries = queries.reshape(total_rows, KEY_VALUE_HEADS, group_width, HEAD_SIZE)
    heads_of_keys = key_rows.reshape(total_keys, KEY_VALUE_HEADS, HEAD_SIZE)
    heads_of_values = value_rows.reshape(total_keys, KEY_VALUE_HEADS, HEAD_SIZE)
    row_live = (jnp.arange(total_rows) < row_limit)[:, None]
    active_cotangent = jnp.where(row_live, cotangent, jnp.zeros_like(cotangent))
    head_gradient = active_cotangent.reshape(total_rows, KEY_VALUE_HEADS, group_width, HEAD_SIZE)
    scaling = 1.0 / math.sqrt(HEAD_SIZE)
    scores = (
        jnp.einsum(
            "lhgd,nhd->hgln", heads_of_queries, heads_of_keys, preferred_element_type=jnp.float32
        )
        * scaling
    )
    key_live = jnp.arange(total_keys) < key_limit
    scores = jnp.where(key_live, scores, -jnp.inf)
    row_max = jnp.max(scores, axis=-1, keepdims=True)
    raised = jnp.exp(scores - row_max)
    weights = raised / jnp.sum(raised, axis=-1, keepdims=True)
    weights_low = weights.astype(jnp.bfloat16)
    value_gradient = jnp.einsum(
        "hgln,lhgd->nhd", weights_low, head_gradient, preferred_element_type=jnp.float32
    ).astype(jnp.bfloat16)
    prob_grad = jnp.einsum(
        "lhgd,nhd->hgln", head_gradient, heads_of_values, preferred_element_type=jnp.float32
    )
    row_dot = jnp.sum(weights * prob_grad, axis=-1, keepdims=True)
    score_grad = (weights * (prob_grad - row_dot) * scaling).astype(jnp.bfloat16)
    query_gradient = jnp.einsum(
        "hgln,nhd->lhgd", score_grad, heads_of_keys, preferred_element_type=jnp.float32
    ).astype(jnp.bfloat16)
    key_gradient = jnp.einsum(
        "hgln,lhgd->nhd", score_grad, heads_of_queries, preferred_element_type=jnp.float32
    ).astype(jnp.bfloat16)
    return (
        query_gradient.reshape(total_rows, QUERY_HEADS * HEAD_SIZE),
        key_gradient.reshape(total_keys, KEY_VALUE_HEADS * HEAD_SIZE),
        value_gradient.reshape(total_keys, KEY_VALUE_HEADS * HEAD_SIZE),
    )


def attend_front(queries, key_rows, cotangent, key_limit, row_limit):
    total_rows = queries.shape[0]
    total_keys = key_rows.shape[0]
    group_width = QUERY_HEADS // KEY_VALUE_HEADS
    heads_of_queries = queries.reshape(total_rows, KEY_VALUE_HEADS, group_width, HEAD_SIZE)
    heads_of_keys = key_rows.reshape(total_keys, KEY_VALUE_HEADS, HEAD_SIZE)
    row_live = (jnp.arange(total_rows) < row_limit)[:, None]
    active_cotangent = jnp.where(row_live, cotangent, jnp.zeros_like(cotangent))
    head_gradient = active_cotangent.reshape(total_rows, KEY_VALUE_HEADS, group_width, HEAD_SIZE)
    scaling = 1.0 / math.sqrt(HEAD_SIZE)
    scores = (
        jnp.einsum(
            "lhgd,nhd->hgln", heads_of_queries, heads_of_keys, preferred_element_type=jnp.float32
        )
        * scaling
    )
    key_live = jnp.arange(total_keys) < key_limit
    scores = jnp.where(key_live, scores, -jnp.inf)
    row_max = jnp.max(scores, axis=-1, keepdims=True)
    raised = jnp.exp(scores - row_max)
    weights = raised / jnp.sum(raised, axis=-1, keepdims=True)
    weights_low = weights.astype(jnp.bfloat16)
    value_gradient = jnp.einsum(
        "hgln,lhgd->nhd", weights_low, head_gradient, preferred_element_type=jnp.float32
    ).astype(jnp.bfloat16)
    return weights, value_gradient.reshape(total_keys, KEY_VALUE_HEADS * HEAD_SIZE)


def attend_back(queries, key_rows, value_rows, cotangent, row_limit, weights):
    total_rows = queries.shape[0]
    total_keys = key_rows.shape[0]
    group_width = QUERY_HEADS // KEY_VALUE_HEADS
    heads_of_queries = queries.reshape(total_rows, KEY_VALUE_HEADS, group_width, HEAD_SIZE)
    heads_of_keys = key_rows.reshape(total_keys, KEY_VALUE_HEADS, HEAD_SIZE)
    heads_of_values = value_rows.reshape(total_keys, KEY_VALUE_HEADS, HEAD_SIZE)
    row_live = (jnp.arange(total_rows) < row_limit)[:, None]
    active_cotangent = jnp.where(row_live, cotangent, jnp.zeros_like(cotangent))
    head_gradient = active_cotangent.reshape(total_rows, KEY_VALUE_HEADS, group_width, HEAD_SIZE)
    scaling = 1.0 / math.sqrt(HEAD_SIZE)
    prob_grad = jnp.einsum(
        "lhgd,nhd->hgln", head_gradient, heads_of_values, preferred_element_type=jnp.float32
    )
    row_dot = jnp.sum(weights * prob_grad, axis=-1, keepdims=True)
    score_grad = (weights * (prob_grad - row_dot) * scaling).astype(jnp.bfloat16)
    query_gradient = jnp.einsum(
        "hgln,nhd->lhgd", score_grad, heads_of_keys, preferred_element_type=jnp.float32
    ).astype(jnp.bfloat16)
    key_gradient = jnp.einsum(
        "hgln,lhgd->nhd", score_grad, heads_of_queries, preferred_element_type=jnp.float32
    ).astype(jnp.bfloat16)
    return (
        query_gradient.reshape(total_rows, QUERY_HEADS * HEAD_SIZE),
        key_gradient.reshape(total_keys, KEY_VALUE_HEADS * HEAD_SIZE),
    )


def exchange_kernel(n, scatter, x_ref, o_ref, send_sems, recv_sems, local_sem):
    me = lax.axis_index("section")
    row = lax.axis_index("dp")
    barrier = pltpu.get_barrier_semaphore()
    for k in range(1, n):
        pl.semaphore_signal(
            barrier, inc=1, device_id=(lax.rem(me + k, n), row), device_id_type=MESH_ID
        )
    pl.semaphore_wait(barrier, n - 1)
    own = x_ref.at[:, me] if scatter else x_ref
    local = pltpu.make_async_copy(own, o_ref.at[:, me], local_sem)
    local.start()
    copies = []
    for k in range(1, n):
        peer = lax.rem(me + k, n)
        src = x_ref.at[:, peer] if scatter else x_ref
        copy = pltpu.make_async_remote_copy(
            src_ref=src,
            dst_ref=o_ref.at[:, me],
            send_sem=send_sems.at[k],
            recv_sem=recv_sems.at[k],
            device_id=(peer, row),
            device_id_type=MESH_ID,
        )
        copy.start()
        copies.append(copy)
    for copy in copies:
        copy.wait()
    local.wait()


def relay_gather_kernel(x_ref, o_ref, stage, local_sem, direct_send, direct_recv,
                        hop_send, hop_recv, fwd_send, fwd_recv):
    s = lax.axis_index("section")
    r = lax.axis_index("dp")
    y = lax.rem(s, 4)
    z = (s // 4) * 2 + r // 8
    xc = lax.rem(r, 8)
    half = x_ref.shape[-1] // 2

    def sec(zz, yy):
        return (lax.rem(zz, 4) // 2) * 4 + yy

    def dpi(zz):
        return lax.rem(zz, 2) * 8 + xc

    up, down = z + 1, z + 3
    peers = [(sec(z, lax.rem(y + j, 4)), r) for j in range(1, 4)]
    for yy in range(4):
        peers.append((sec(up, yy), dpi(up)))
        peers.append((sec(down, yy), dpi(down)))
    barrier = pltpu.get_barrier_semaphore()
    for peer in peers:
        pl.semaphore_signal(barrier, inc=1, device_id=peer, device_id_type=MESH_ID)
    pl.semaphore_wait(barrier, len(peers))

    local = pltpu.make_async_copy(x_ref, o_ref.at[:, s], local_sem)
    local.start()
    sends = []
    for j in range(1, 4):
        copy = pltpu.make_async_remote_copy(
            src_ref=x_ref,
            dst_ref=o_ref.at[:, s],
            send_sem=direct_send.at[j],
            recv_sem=direct_recv.at[j],
            device_id=peers[j - 1],
            device_id_type=MESH_ID,
        )
        copy.start()
        sends.append(copy)
    hops = []
    for side, (target, lanes) in enumerate(((up, pl.ds(0, half)), (down, pl.ds(half, half)))):
        copy = pltpu.make_async_remote_copy(
            src_ref=x_ref.at[:, :, lanes],
            dst_ref=stage.at[side],
            send_sem=hop_send.at[side],
            recv_sem=hop_recv.at[side],
            device_id=(sec(target, y), dpi(target)),
            device_id_type=MESH_ID,
        )
        copy.start()
        hops.append(copy)
    forwards = []
    for side, (origin, target, lanes) in enumerate(
        ((down, up, pl.ds(0, half)), (up, down, pl.ds(half, half)))
    ):
        hops[side].wait_recv()
        for yy in range(4):
            copy = pltpu.make_async_remote_copy(
                src_ref=stage.at[side],
                dst_ref=o_ref.at[:, sec(origin, y), :, lanes],
                send_sem=fwd_send.at[side, yy],
                recv_sem=fwd_recv.at[side, y],
                device_id=(sec(target, yy), dpi(target)),
                device_id_type=MESH_ID,
            )
            copy.start()
            forwards.append(copy)
    for copy in sends:
        copy.wait()
    for copy in hops:
        copy.wait_send()
    for copy in forwards:
        copy.wait_send()
    for side, (origin, target, lanes) in enumerate(
        ((down, up, pl.ds(0, half)), (up, down, pl.ds(half, half)))
    ):
        for yy in range(4):
            pltpu.make_async_remote_copy(
                src_ref=stage.at[side],
                dst_ref=o_ref.at[:, sec(origin, y), :, lanes],
                send_sem=fwd_send.at[side, yy],
                recv_sem=fwd_recv.at[side, yy],
                device_id=(sec(target, yy), dpi(target)),
                device_id_type=MESH_ID,
            ).wait_recv()
    local.wait()


def relay_gather(x, n):
    samples, chunk, width = x.shape
    return pl.pallas_call(
        relay_gather_kernel,
        out_shape=jax.ShapeDtypeStruct((samples, n, chunk, width), x.dtype),
        in_specs=[pl.BlockSpec(memory_space=pl.ANY)],
        out_specs=pl.BlockSpec(memory_space=pl.ANY),
        scratch_shapes=[
            pltpu.VMEM((2, samples, chunk, width // 2), x.dtype),
            pltpu.SemaphoreType.DMA(()),
            pltpu.SemaphoreType.DMA((4,)),
            pltpu.SemaphoreType.DMA((4,)),
            pltpu.SemaphoreType.DMA((2,)),
            pltpu.SemaphoreType.DMA((2,)),
            pltpu.SemaphoreType.DMA((2, 4)),
            pltpu.SemaphoreType.DMA((2, 4)),
        ],
        compiler_params=pltpu.CompilerParams(collective_id=2, has_side_effects=True),
    )(x)


def exchange(x, n, scatter, collective_id):
    if scatter:
        out_shape = x.shape
    else:
        out_shape = (x.shape[0], n) + x.shape[1:]
    return pl.pallas_call(
        functools.partial(exchange_kernel, n, scatter),
        out_shape=jax.ShapeDtypeStruct(out_shape, x.dtype),
        in_specs=[pl.BlockSpec(memory_space=pl.ANY)],
        out_specs=pl.BlockSpec(memory_space=pl.ANY),
        scratch_shapes=[
            pltpu.SemaphoreType.DMA((n,)),
            pltpu.SemaphoreType.DMA((n,)),
            pltpu.SemaphoreType.DMA(()),
        ],
        compiler_params=pltpu.CompilerParams(collective_id=collective_id, has_side_effects=True),
    )(x)


def image_kernel(n, tiles, g_ref, wk_hbm, wv_hbm, o_ref, buf, recv, acc, wk_ref, wv_ref,
                 weight_sems, send_sems, recv_sems):
    me = lax.axis_index("section")
    row = lax.axis_index("dp")
    rows = g_ref.shape[0] // n
    half = g_ref.shape[1] // 2
    tile_w = wk_ref.shape[0] // tiles

    def weight_copies(t):
        part = pl.ds(pl.multiple_of(t * tile_w, tile_w), tile_w)
        return [
            pltpu.make_async_copy(src.at[part], dst.at[part], weight_sems.at[i, t])
            for i, (src, dst) in enumerate(((wk_hbm, wk_ref), (wv_hbm, wv_ref)))
        ]

    for t in range(tiles):
        for copy in weight_copies(t):
            copy.start()
    barrier = pltpu.get_barrier_semaphore()
    for k in range(1, n):
        pl.semaphore_signal(
            barrier, inc=1, device_id=(lax.rem(me + k, n), row), device_id_type=MESH_ID
        )
    pl.semaphore_wait(barrier, n - 1)

    def compute(t):
        for copy in weight_copies(t):
            copy.wait()
        cols = pl.ds(pl.multiple_of(t * tile_w, tile_w), tile_w)
        dims = (((1,), (1,)), ((), ()))
        acc = lax.dot_general(
            g_ref[:, pl.ds(0, half)], wk_ref[cols, :], dims, preferred_element_type=jnp.float32
        )
        acc = acc + lax.dot_general(
            g_ref[:, pl.ds(half, half)], wv_ref[cols, :], dims, preferred_element_type=jnp.float32
        )
        buf[:, cols] = acc.astype(buf.dtype)

    def send(t):
        cols = pl.ds(pl.multiple_of(t * tile_w, tile_w), tile_w)
        for k in range(1, n):
            peer = lax.rem(me + k, n)
            pltpu.make_async_remote_copy(
                src_ref=buf.at[pl.ds(pl.multiple_of(peer * rows, 16), rows), cols],
                dst_ref=recv.at[me, :, cols],
                send_sem=send_sems.at[k],
                recv_sem=recv_sems.at[k],
                device_id=(peer, row),
                device_id_type=MESH_ID,
            ).start()

    compute(0)

    def body(t, carry):
        compute(t)
        send(t - 1)
        return carry

    lax.fori_loop(1, tiles, body, 0)
    send(tiles - 1)
    own = pl.ds(pl.multiple_of(me * rows, 16), rows)
    acc[...] = buf[own, :].astype(jnp.float32)
    for k in range(1, n):
        peer = lax.rem(me + k, n)
        whole = pltpu.make_async_remote_copy(
            src_ref=buf.at[pl.ds(pl.multiple_of(peer * rows, 16), rows), :],
            dst_ref=recv.at[me],
            send_sem=send_sems.at[k],
            recv_sem=recv_sems.at[k],
            device_id=(peer, row),
            device_id_type=MESH_ID,
        )
        whole.wait_recv()
        acc[...] += recv[lax.rem(me + n - k, n)].astype(jnp.float32)
        whole.wait_send()
    o_ref[...] = acc[...].astype(o_ref.dtype)


def image_exchange(g, w_key, w_value, n):
    total_rows, kv = g.shape
    width = w_key.shape[0]
    tiles = 8
    return pl.pallas_call(
        functools.partial(image_kernel, n, tiles),
        out_shape=jax.ShapeDtypeStruct((total_rows // n, width), jnp.bfloat16),
        in_specs=[
            pl.BlockSpec(memory_space=pltpu.VMEM),
            pl.BlockSpec(memory_space=pl.ANY),
            pl.BlockSpec(memory_space=pl.ANY),
        ],
        out_specs=pl.BlockSpec(memory_space=pltpu.VMEM),
        scratch_shapes=[
            pltpu.VMEM((total_rows, width), jnp.bfloat16),
            pltpu.VMEM((n, total_rows // n, width), jnp.bfloat16),
            pltpu.VMEM((total_rows // n, width), jnp.float32),
            pltpu.VMEM(w_key.shape, w_key.dtype),
            pltpu.VMEM(w_value.shape, w_value.dtype),
            pltpu.SemaphoreType.DMA((2, tiles)),
            pltpu.SemaphoreType.DMA((n,)),
            pltpu.SemaphoreType.DMA((n,)),
        ],
        compiler_params=pltpu.CompilerParams(
            collective_id=3, has_side_effects=True, vmem_limit_bytes=60 * 1024 * 1024
        ),
        cost_estimate=pl.CostEstimate(
            flops=2 * total_rows * kv * width, bytes_accessed=2 * (kv + total_rows) * width,
            transcendentals=0,
        ),
    )(g, w_key, w_value)


def shards(queries, image_tokens, key_weight, value_weight, cotangent, tile_counts, text_lengths):
    n_section = lax.axis_size("section")
    samples_here, chunk, model_width = image_tokens.shape
    image_len = n_section * chunk
    tile_len = image_len // MAX_TILES
    w_key = key_weight[0]
    w_value = value_weight[0]
    query_local = queries[0]
    cotan_local = cotangent[0]
    late = [
        lax.all_gather(image_tokens[i], "section", axis=0, tiled=True)
        for i in range(1, samples_here)
    ]
    if n_section == 8 and lax.axis_size("dp") == 16:
        first = relay_gather(image_tokens[:1], n_section)
    else:
        first = exchange(image_tokens[:1], n_section, False, 0)
    token_list = [first.reshape(image_len, model_width)] + late
    keys_list = []
    values_list = []
    for sample_index in range(samples_here):
        tokens = token_list[sample_index]
        keys_list.append(
            jnp.dot(tokens, w_key, preferred_element_type=jnp.float32).astype(jnp.bfloat16)
        )
        values_list.append(
            jnp.dot(tokens, w_value, preferred_element_type=jnp.float32).astype(jnp.bfloat16)
        )
    keys_both = jnp.stack(keys_list)
    values_both = jnp.stack(values_list)
    key_limits = tile_counts * tile_len
    weights, value_grads = jax.vmap(attend_front)(
        query_local, keys_both, cotan_local, key_limits, text_lengths
    )
    all_tokens = jnp.concatenate(token_list, axis=0)
    value_term = jnp.einsum(
        "td,tk->dk", all_tokens, value_grads.reshape(samples_here * image_len, -1),
        preferred_element_type=jnp.float32,
    ).astype(jnp.bfloat16)
    value_term, weights = lax.optimization_barrier((value_term, weights))
    value_sum = lax.psum_scatter(value_term, "dp", scatter_dimension=0, tiled=True)
    query_grads, key_grads = jax.vmap(attend_back)(
        query_local, keys_both, values_both, cotan_local, text_lengths, weights
    )
    key_term = jnp.einsum(
        "td,tk->dk", all_tokens, key_grads.reshape(samples_here * image_len, -1),
        preferred_element_type=jnp.float32,
    ).astype(jnp.bfloat16)
    key_sum = lax.psum_scatter(key_term, "dp", scatter_dimension=0, tiled=True)
    query_out = query_grads[None]
    kv_grads = jnp.concatenate([key_grads, value_grads], axis=-1)
    by_slot = kv_grads.reshape(samples_here, n_section, chunk, -1).transpose(1, 0, 2, 3)
    received = image_exchange(
        by_slot.reshape(n_section * samples_here * chunk, -1), w_key, w_value, n_section
    )
    image_out = received.reshape(samples_here, chunk, model_width)
    return (
        query_out,
        image_out,
        key_sum[None],
        value_sum[None],
    )


def solution(mesh):
    placed = (
        P("section", "dp", None, None),
        P("dp", "section", None),
        P("section", None, None),
        P("section", None, None),
        P("section", "dp", None, None),
        P("dp"),
        P("dp"),
    )
    return jax.shard_map(
        shards,
        mesh=mesh,
        in_specs=placed,
        out_specs=(
            P("section", "dp", None, None),
            P("dp", "section", None),
            P("section", "dp", None),
            P("section", "dp", None),
        ),
        check_vma=False,
    )
```

```python
import functools
import math

import jax
import jax.numpy as jnp
from jax import lax
from jax.experimental import pallas as pl
from jax.experimental.pallas import tpu as pltpu
from jax.sharding import PartitionSpec as P

QUERY_HEADS = 32
KEY_VALUE_HEADS = 4
HEAD_SIZE = 128
MAX_TILES = 4
MESH_ID = pl.DeviceIdType.MESH


def attend_one(queries, key_rows, value_rows, cotangent, key_limit, row_limit):
    total_rows = queries.shape[0]
    total_keys = key_rows.shape[0]
    group_width = QUERY_HEADS // KEY_VALUE_HEADS
    heads_of_queries = queries.reshape(total_rows, KEY_VALUE_HEADS, group_width, HEAD_SIZE)
    heads_of_keys = key_rows.reshape(total_keys, KEY_VALUE_HEADS, HEAD_SIZE)
    heads_of_values = value_rows.reshape(total_keys, KEY_VALUE_HEADS, HEAD_SIZE)
    row_live = (jnp.arange(total_rows) < row_limit)[:, None]
    active_cotangent = jnp.where(row_live, cotangent, jnp.zeros_like(cotangent))
    head_gradient = active_cotangent.reshape(total_rows, KEY_VALUE_HEADS, group_width, HEAD_SIZE)
    scaling = 1.0 / math.sqrt(HEAD_SIZE)
    scores = (
        jnp.einsum(
            "lhgd,nhd->hgln", heads_of_queries, heads_of_keys, preferred_element_type=jnp.float32
        )
        * scaling
    )
    key_live = jnp.arange(total_keys) < key_limit
    scores = jnp.where(key_live, scores, -jnp.inf)
    row_max = jnp.max(scores, axis=-1, keepdims=True)
    raised = jnp.exp(scores - row_max)
    weights = raised / jnp.sum(raised, axis=-1, keepdims=True)
    weights_low = weights.astype(jnp.bfloat16)
    value_gradient = jnp.einsum(
        "hgln,lhgd->nhd", weights_low, head_gradient, preferred_element_type=jnp.float32
    ).astype(jnp.bfloat16)
    prob_grad = jnp.einsum(
        "lhgd,nhd->hgln", head_gradient, heads_of_values, preferred_element_type=jnp.float32
    )
    row_dot = jnp.sum(weights * prob_grad, axis=-1, keepdims=True)
    score_grad = (weights * (prob_grad - row_dot) * scaling).astype(jnp.bfloat16)
    query_gradient = jnp.einsum(
        "hgln,nhd->lhgd", score_grad, heads_of_keys, preferred_element_type=jnp.float32
    ).astype(jnp.bfloat16)
    key_gradient = jnp.einsum(
        "hgln,lhgd->nhd", score_grad, heads_of_queries, preferred_element_type=jnp.float32
    ).astype(jnp.bfloat16)
    return (
        query_gradient.reshape(total_rows, QUERY_HEADS * HEAD_SIZE),
        key_gradient.reshape(total_keys, KEY_VALUE_HEADS * HEAD_SIZE),
        value_gradient.reshape(total_keys, KEY_VALUE_HEADS * HEAD_SIZE),
    )


def attend_front(queries, key_rows, cotangent, key_limit, row_limit):
    total_rows = queries.shape[0]
    total_keys = key_rows.shape[0]
    group_width = QUERY_HEADS // KEY_VALUE_HEADS
    heads_of_queries = queries.reshape(total_rows, KEY_VALUE_HEADS, group_width, HEAD_SIZE)
    heads_of_keys = key_rows.reshape(total_keys, KEY_VALUE_HEADS, HEAD_SIZE)
    row_live = (jnp.arange(total_rows) < row_limit)[:, None]
    active_cotangent = jnp.where(row_live, cotangent, jnp.zeros_like(cotangent))
    head_gradient = active_cotangent.reshape(total_rows, KEY_VALUE_HEADS, group_width, HEAD_SIZE)
    scaling = 1.0 / math.sqrt(HEAD_SIZE)
    scores = (
        jnp.einsum(
            "lhgd,nhd->hgln", heads_of_queries, heads_of_keys, preferred_element_type=jnp.float32
        )
        * scaling
    )
    key_live = jnp.arange(total_keys) < key_limit
    scores = jnp.where(key_live, scores, -jnp.inf)
    row_max = jnp.max(scores, axis=-1, keepdims=True)
    raised = jnp.exp(scores - row_max)
    weights = raised / jnp.sum(raised, axis=-1, keepdims=True)
    weights_low = weights.astype(jnp.bfloat16)
    value_gradient = jnp.einsum(
        "hgln,lhgd->nhd", weights_low, head_gradient, preferred_element_type=jnp.float32
    ).astype(jnp.bfloat16)
    return weights, value_gradient.reshape(total_keys, KEY_VALUE_HEADS * HEAD_SIZE)


def attend_back(queries, key_rows, value_rows, cotangent, row_limit, weights):
    total_rows = queries.shape[0]
    total_keys = key_rows.shape[0]
    group_width = QUERY_HEADS // KEY_VALUE_HEADS
    heads_of_queries = queries.reshape(total_rows, KEY_VALUE_HEADS, group_width, HEAD_SIZE)
    heads_of_keys = key_rows.reshape(total_keys, KEY_VALUE_HEADS, HEAD_SIZE)
    heads_of_values = value_rows.reshape(total_keys, KEY_VALUE_HEADS, HEAD_SIZE)
    row_live = (jnp.arange(total_rows) < row_limit)[:, None]
    active_cotangent = jnp.where(row_live, cotangent, jnp.zeros_like(cotangent))
    head_gradient = active_cotangent.reshape(total_rows, KEY_VALUE_HEADS, group_width, HEAD_SIZE)
    scaling = 1.0 / math.sqrt(HEAD_SIZE)
    prob_grad = jnp.einsum(
        "lhgd,nhd->hgln", head_gradient, heads_of_values, preferred_element_type=jnp.float32
    )
    row_dot = jnp.sum(weights * prob_grad, axis=-1, keepdims=True)
    score_grad = (weights * (prob_grad - row_dot) * scaling).astype(jnp.bfloat16)
    query_gradient = jnp.einsum(
        "hgln,nhd->lhgd", score_grad, heads_of_keys, preferred_element_type=jnp.float32
    ).astype(jnp.bfloat16)
    key_gradient = jnp.einsum(
        "hgln,lhgd->nhd", score_grad, heads_of_queries, preferred_element_type=jnp.float32
    ).astype(jnp.bfloat16)
    return (
        query_gradient.reshape(total_rows, QUERY_HEADS * HEAD_SIZE),
        key_gradient.reshape(total_keys, KEY_VALUE_HEADS * HEAD_SIZE),
    )


def exchange_kernel(n, scatter, x_ref, o_ref, send_sems, recv_sems, local_sem):
    me = lax.axis_index("section")
    row = lax.axis_index("dp")
    barrier = pltpu.get_barrier_semaphore()
    for k in range(1, n):
        pl.semaphore_signal(
            barrier, inc=1, device_id=(lax.rem(me + k, n), row), device_id_type=MESH_ID
        )
    pl.semaphore_wait(barrier, n - 1)
    own = x_ref.at[:, me] if scatter else x_ref
    local = pltpu.make_async_copy(own, o_ref.at[:, me], local_sem)
    local.start()
    copies = []
    for k in range(1, n):
        peer = lax.rem(me + k, n)
        src = x_ref.at[:, peer] if scatter else x_ref
        copy = pltpu.make_async_remote_copy(
            src_ref=src,
            dst_ref=o_ref.at[:, me],
            send_sem=send_sems.at[k],
            recv_sem=recv_sems.at[k],
            device_id=(peer, row),
            device_id_type=MESH_ID,
        )
        copy.start()
        copies.append(copy)
    for copy in copies:
        copy.wait()
    local.wait()


def relay_gather_kernel(x_ref, o_ref, stage, local_sem, direct_send, direct_recv,
                        hop_send, hop_recv, fwd_send, fwd_recv):
    s = lax.axis_index("section")
    r = lax.axis_index("dp")
    y = lax.rem(s, 4)
    z = (s // 4) * 2 + r // 8
    xc = lax.rem(r, 8)
    half = x_ref.shape[-1] // 2

    def sec(zz, yy):
        return (lax.rem(zz, 4) // 2) * 4 + yy

    def dpi(zz):
        return lax.rem(zz, 2) * 8 + xc

    up, down = z + 1, z + 3
    peers = [(sec(z, lax.rem(y + j, 4)), r) for j in range(1, 4)]
    for yy in range(4):
        peers.append((sec(up, yy), dpi(up)))
        peers.append((sec(down, yy), dpi(down)))
    barrier = pltpu.get_barrier_semaphore()
    for peer in peers:
        pl.semaphore_signal(barrier, inc=1, device_id=peer, device_id_type=MESH_ID)
    pl.semaphore_wait(barrier, len(peers))

    local = pltpu.make_async_copy(x_ref, o_ref.at[:, s], local_sem)
    local.start()
    sends = []
    for j in range(1, 4):
        copy = pltpu.make_async_remote_copy(
            src_ref=x_ref,
            dst_ref=o_ref.at[:, s],
            send_sem=direct_send.at[j],
            recv_sem=direct_recv.at[j],
            device_id=peers[j - 1],
            device_id_type=MESH_ID,
        )
        copy.start()
        sends.append(copy)
    hops = []
    for side, (target, lanes) in enumerate(((up, pl.ds(0, half)), (down, pl.ds(half, half)))):
        copy = pltpu.make_async_remote_copy(
            src_ref=x_ref.at[:, :, lanes],
            dst_ref=stage.at[side],
            send_sem=hop_send.at[side],
            recv_sem=hop_recv.at[side],
            device_id=(sec(target, y), dpi(target)),
            device_id_type=MESH_ID,
        )
        copy.start()
        hops.append(copy)
    forwards = []
    for side, (origin, target, lanes) in enumerate(
        ((down, up, pl.ds(0, half)), (up, down, pl.ds(half, half)))
    ):
        hops[side].wait_recv()
        for yy in range(4):
            copy = pltpu.make_async_remote_copy(
                src_ref=stage.at[side],
                dst_ref=o_ref.at[:, sec(origin, y), :, lanes],
                send_sem=fwd_send.at[side, yy],
                recv_sem=fwd_recv.at[side, y],
                device_id=(sec(target, yy), dpi(target)),
                device_id_type=MESH_ID,
            )
            copy.start()
            forwards.append(copy)
    for copy in sends:
        copy.wait()
    for copy in hops:
        copy.wait_send()
    for copy in forwards:
        copy.wait_send()
    for side, (origin, target, lanes) in enumerate(
        ((down, up, pl.ds(0, half)), (up, down, pl.ds(half, half)))
    ):
        for yy in range(4):
            pltpu.make_async_remote_copy(
                src_ref=stage.at[side],
                dst_ref=o_ref.at[:, sec(origin, y), :, lanes],
                send_sem=fwd_send.at[side, yy],
                recv_sem=fwd_recv.at[side, yy],
                device_id=(sec(target, yy), dpi(target)),
                device_id_type=MESH_ID,
            ).wait_recv()
    local.wait()


def relay_gather(x, n):
    samples, chunk, width = x.shape
    return pl.pallas_call(
        relay_gather_kernel,
        out_shape=jax.ShapeDtypeStruct((samples, n, chunk, width), x.dtype),
        in_specs=[pl.BlockSpec(memory_space=pl.ANY)],
        out_specs=pl.BlockSpec(memory_space=pl.ANY),
        scratch_shapes=[
            pltpu.VMEM((2, samples, chunk, width // 2), x.dtype),
            pltpu.SemaphoreType.DMA(()),
            pltpu.SemaphoreType.DMA((4,)),
            pltpu.SemaphoreType.DMA((4,)),
            pltpu.SemaphoreType.DMA((2,)),
            pltpu.SemaphoreType.DMA((2,)),
            pltpu.SemaphoreType.DMA((2, 4)),
            pltpu.SemaphoreType.DMA((2, 4)),
        ],
        compiler_params=pltpu.CompilerParams(collective_id=2, has_side_effects=True),
    )(x)


def exchange(x, n, scatter, collective_id):
    if scatter:
        out_shape = x.shape
    else:
        out_shape = (x.shape[0], n) + x.shape[1:]
    return pl.pallas_call(
        functools.partial(exchange_kernel, n, scatter),
        out_shape=jax.ShapeDtypeStruct(out_shape, x.dtype),
        in_specs=[pl.BlockSpec(memory_space=pl.ANY)],
        out_specs=pl.BlockSpec(memory_space=pl.ANY),
        scratch_shapes=[
            pltpu.SemaphoreType.DMA((n,)),
            pltpu.SemaphoreType.DMA((n,)),
            pltpu.SemaphoreType.DMA(()),
        ],
        compiler_params=pltpu.CompilerParams(collective_id=collective_id, has_side_effects=True),
    )(x)


def image_kernel(n, tiles, g_ref, wk_hbm, wv_hbm, o_ref, buf, recv, acc, wk_ref, wv_ref,
                 weight_sems, send_sems, recv_sems):
    me = lax.axis_index("section")
    row = lax.axis_index("dp")
    rows = g_ref.shape[0] // n
    half = g_ref.shape[1] // 2
    tile_w = wk_ref.shape[0] // tiles

    def weight_copies(t):
        part = pl.ds(pl.multiple_of(t * tile_w, tile_w), tile_w)
        return [
            pltpu.make_async_copy(src.at[part], dst.at[part], weight_sems.at[i, t])
            for i, (src, dst) in enumerate(((wk_hbm, wk_ref), (wv_hbm, wv_ref)))
        ]

    for t in range(tiles):
        for copy in weight_copies(t):
            copy.start()
    barrier = pltpu.get_barrier_semaphore()
    for k in range(1, n):
        pl.semaphore_signal(
            barrier, inc=1, device_id=(lax.rem(me + k, n), row), device_id_type=MESH_ID
        )
    pl.semaphore_wait(barrier, n - 1)

    def compute(t):
        for copy in weight_copies(t):
            copy.wait()
        cols = pl.ds(pl.multiple_of(t * tile_w, tile_w), tile_w)
        dims = (((1,), (1,)), ((), ()))
        acc = lax.dot_general(
            g_ref[:, pl.ds(0, half)], wk_ref[cols, :], dims, preferred_element_type=jnp.float32
        )
        acc = acc + lax.dot_general(
            g_ref[:, pl.ds(half, half)], wv_ref[cols, :], dims, preferred_element_type=jnp.float32
        )
        buf[:, cols] = acc.astype(buf.dtype)

    def send(t):
        cols = pl.ds(pl.multiple_of(t * tile_w, tile_w), tile_w)
        for k in range(1, n):
            peer = lax.rem(me + k, n)
            pltpu.make_async_remote_copy(
                src_ref=buf.at[pl.ds(pl.multiple_of(peer * rows, 16), rows), cols],
                dst_ref=recv.at[me, :, cols],
                send_sem=send_sems.at[k],
                recv_sem=recv_sems.at[k],
                device_id=(peer, row),
                device_id_type=MESH_ID,
            ).start()

    compute(0)

    def body(t, carry):
        compute(t)
        send(t - 1)
        return carry

    lax.fori_loop(1, tiles, body, 0)
    send(tiles - 1)
    own = pl.ds(pl.multiple_of(me * rows, 16), rows)
    acc[...] = buf[own, :].astype(jnp.float32)
    for k in range(1, n):
        peer = lax.rem(me + k, n)
        whole = pltpu.make_async_remote_copy(
            src_ref=buf.at[pl.ds(pl.multiple_of(peer * rows, 16), rows), :],
            dst_ref=recv.at[me],
            send_sem=send_sems.at[k],
            recv_sem=recv_sems.at[k],
            device_id=(peer, row),
            device_id_type=MESH_ID,
        )
        whole.wait_recv()
        acc[...] += recv[lax.rem(me + n - k, n)].astype(jnp.float32)
        whole.wait_send()
    o_ref[...] = acc[...].astype(o_ref.dtype)


def image_exchange(g, w_key, w_value, n):
    total_rows, kv = g.shape
    width = w_key.shape[0]
    tiles = 8
    return pl.pallas_call(
        functools.partial(image_kernel, n, tiles),
        out_shape=jax.ShapeDtypeStruct((total_rows // n, width), jnp.bfloat16),
        in_specs=[
            pl.BlockSpec(memory_space=pltpu.VMEM),
            pl.BlockSpec(memory_space=pl.ANY),
            pl.BlockSpec(memory_space=pl.ANY),
        ],
        out_specs=pl.BlockSpec(memory_space=pltpu.VMEM),
        scratch_shapes=[
            pltpu.VMEM((total_rows, width), jnp.bfloat16),
            pltpu.VMEM((n, total_rows // n, width), jnp.bfloat16),
            pltpu.VMEM((total_rows // n, width), jnp.float32),
            pltpu.VMEM(w_key.shape, w_key.dtype),
            pltpu.VMEM(w_value.shape, w_value.dtype),
            pltpu.SemaphoreType.DMA((2, tiles)),
            pltpu.SemaphoreType.DMA((n,)),
            pltpu.SemaphoreType.DMA((n,)),
        ],
        compiler_params=pltpu.CompilerParams(
            collective_id=3, has_side_effects=True, vmem_limit_bytes=60 * 1024 * 1024
        ),
        cost_estimate=pl.CostEstimate(
            flops=2 * total_rows * kv * width, bytes_accessed=2 * (kv + total_rows) * width,
            transcendentals=0,
        ),
    )(g, w_key, w_value)


def shards(queries, image_tokens, key_weight, value_weight, cotangent, tile_counts, text_lengths):
    n_section = lax.axis_size("section")
    samples_here, chunk, model_width = image_tokens.shape
    image_len = n_section * chunk
    tile_len = image_len // MAX_TILES
    w_key = key_weight[0]
    w_value = value_weight[0]
    query_local = queries[0]
    cotan_local = cotangent[0]
    late = [
        lax.all_gather(image_tokens[i], "section", axis=0, tiled=True)
        for i in range(1, samples_here)
    ]
    if n_section == 8 and lax.axis_size("dp") == 16:
        first = relay_gather(image_tokens[:1], n_section)
    else:
        first = exchange(image_tokens[:1], n_section, False, 0)
    first, query_local, cotan_local = lax.optimization_barrier((first, query_local, cotan_local))
    token_list = [first.reshape(image_len, model_width)] + late
    keys_list = []
    values_list = []
    for sample_index in range(samples_here):
        tokens = token_list[sample_index]
        keys_list.append(
            jnp.dot(tokens, w_key, preferred_element_type=jnp.float32).astype(jnp.bfloat16)
        )
        values_list.append(
            jnp.dot(tokens, w_value, preferred_element_type=jnp.float32).astype(jnp.bfloat16)
        )
    keys_both = jnp.stack(keys_list)
    values_both = jnp.stack(values_list)
    key_limits = tile_counts * tile_len
    weights, value_grads = jax.vmap(attend_front)(
        query_local, keys_both, cotan_local, key_limits, text_lengths
    )
    all_tokens = jnp.concatenate(token_list, axis=0)
    value_term = jnp.einsum(
        "td,tk->dk", all_tokens, value_grads.reshape(samples_here * image_len, -1),
        preferred_element_type=jnp.float32,
    ).astype(jnp.bfloat16)
    value_term, weights = lax.optimization_barrier((value_term, weights))
    value_sum = lax.psum_scatter(value_term, "dp", scatter_dimension=0, tiled=True)
    query_grads, key_grads = jax.vmap(attend_back)(
        query_local, keys_both, values_both, cotan_local, text_lengths, weights
    )
    key_term = jnp.einsum(
        "td,tk->dk", all_tokens, key_grads.reshape(samples_here * image_len, -1),
        preferred_element_type=jnp.float32,
    ).astype(jnp.bfloat16)
    key_sum = lax.psum_scatter(key_term, "dp", scatter_dimension=0, tiled=True)
    query_out = query_grads[None]
    kv_grads = jnp.concatenate([key_grads, value_grads], axis=-1)
    by_slot = kv_grads.reshape(samples_here, n_section, chunk, -1).transpose(1, 0, 2, 3)
    received = image_exchange(
        by_slot.reshape(n_section * samples_here * chunk, -1), w_key, w_value, n_section
    )
    image_out = received.reshape(samples_here, chunk, model_width)
    return (
        query_out,
        image_out,
        key_sum[None],
        value_sum[None],
    )


def solution(mesh):
    placed = (
        P("section", "dp", None, None),
        P("dp", "section", None),
        P("section", None, None),
        P("section", None, None),
        P("section", "dp", None, None),
        P("dp"),
        P("dp"),
    )
    return jax.shard_map(
        shards,
        mesh=mesh,
        in_specs=placed,
        out_specs=(
            P("section", "dp", None, None),
            P("dp", "section", None),
            P("section", "dp", None),
            P("section", "dp", None),
        ),
        check_vma=False,
    )
```

```python
import functools
import math

import jax
import jax.numpy as jnp
from jax import lax
from jax.experimental import pallas as pl
from jax.experimental.pallas import tpu as pltpu
from jax.sharding import PartitionSpec as P

QUERY_HEADS = 32
KEY_VALUE_HEADS = 4
HEAD_SIZE = 128
MAX_TILES = 4
MESH_ID = pl.DeviceIdType.MESH


def attend_one(queries, key_rows, value_rows, cotangent, key_limit, row_limit):
    total_rows = queries.shape[0]
    total_keys = key_rows.shape[0]
    group_width = QUERY_HEADS // KEY_VALUE_HEADS
    heads_of_queries = queries.reshape(total_rows, KEY_VALUE_HEADS, group_width, HEAD_SIZE)
    heads_of_keys = key_rows.reshape(total_keys, KEY_VALUE_HEADS, HEAD_SIZE)
    heads_of_values = value_rows.reshape(total_keys, KEY_VALUE_HEADS, HEAD_SIZE)
    row_live = (jnp.arange(total_rows) < row_limit)[:, None]
    active_cotangent = jnp.where(row_live, cotangent, jnp.zeros_like(cotangent))
    head_gradient = active_cotangent.reshape(total_rows, KEY_VALUE_HEADS, group_width, HEAD_SIZE)
    scaling = 1.0 / math.sqrt(HEAD_SIZE)
    scores = (
        jnp.einsum(
            "lhgd,nhd->hgln", heads_of_queries, heads_of_keys, preferred_element_type=jnp.float32
        )
        * scaling
    )
    key_live = jnp.arange(total_keys) < key_limit
    scores = jnp.where(key_live, scores, -jnp.inf)
    row_max = jnp.max(scores, axis=-1, keepdims=True)
    raised = jnp.exp(scores - row_max)
    weights = raised / jnp.sum(raised, axis=-1, keepdims=True)
    weights_low = weights.astype(jnp.bfloat16)
    value_gradient = jnp.einsum(
        "hgln,lhgd->nhd", weights_low, head_gradient, preferred_element_type=jnp.float32
    ).astype(jnp.bfloat16)
    prob_grad = jnp.einsum(
        "lhgd,nhd->hgln", head_gradient, heads_of_values, preferred_element_type=jnp.float32
    )
    row_dot = jnp.sum(weights * prob_grad, axis=-1, keepdims=True)
    score_grad = (weights * (prob_grad - row_dot) * scaling).astype(jnp.bfloat16)
    query_gradient = jnp.einsum(
        "hgln,nhd->lhgd", score_grad, heads_of_keys, preferred_element_type=jnp.float32
    ).astype(jnp.bfloat16)
    key_gradient = jnp.einsum(
        "hgln,lhgd->nhd", score_grad, heads_of_queries, preferred_element_type=jnp.float32
    ).astype(jnp.bfloat16)
    return (
        query_gradient.reshape(total_rows, QUERY_HEADS * HEAD_SIZE),
        key_gradient.reshape(total_keys, KEY_VALUE_HEADS * HEAD_SIZE),
        value_gradient.reshape(total_keys, KEY_VALUE_HEADS * HEAD_SIZE),
    )


def attend_front(queries, key_rows, cotangent, key_limit, row_limit):
    total_rows = queries.shape[0]
    total_keys = key_rows.shape[0]
    group_width = QUERY_HEADS // KEY_VALUE_HEADS
    heads_of_queries = queries.reshape(total_rows, KEY_VALUE_HEADS, group_width, HEAD_SIZE)
    heads_of_keys = key_rows.reshape(total_keys, KEY_VALUE_HEADS, HEAD_SIZE)
    row_live = (jnp.arange(total_rows) < row_limit)[:, None]
    active_cotangent = jnp.where(row_live, cotangent, jnp.zeros_like(cotangent))
    head_gradient = active_cotangent.reshape(total_rows, KEY_VALUE_HEADS, group_width, HEAD_SIZE)
    scaling = 1.0 / math.sqrt(HEAD_SIZE)
    scores = (
        jnp.einsum(
            "lhgd,nhd->hgln", heads_of_queries, heads_of_keys, preferred_element_type=jnp.float32
        )
        * scaling
    )
    key_live = jnp.arange(total_keys) < key_limit
    scores = jnp.where(key_live, scores, -jnp.inf)
    row_max = jnp.max(scores, axis=-1, keepdims=True)
    raised = jnp.exp(scores - row_max)
    weights = raised / jnp.sum(raised, axis=-1, keepdims=True)
    weights_low = weights.astype(jnp.bfloat16)
    value_gradient = jnp.einsum(
        "hgln,lhgd->nhd", weights_low, head_gradient, preferred_element_type=jnp.float32
    ).astype(jnp.bfloat16)
    return weights, value_gradient.reshape(total_keys, KEY_VALUE_HEADS * HEAD_SIZE)


def attend_back(queries, key_rows, value_rows, cotangent, row_limit, weights):
    total_rows = queries.shape[0]
    total_keys = key_rows.shape[0]
    group_width = QUERY_HEADS // KEY_VALUE_HEADS
    heads_of_queries = queries.reshape(total_rows, KEY_VALUE_HEADS, group_width, HEAD_SIZE)
    heads_of_keys = key_rows.reshape(total_keys, KEY_VALUE_HEADS, HEAD_SIZE)
    heads_of_values = value_rows.reshape(total_keys, KEY_VALUE_HEADS, HEAD_SIZE)
    row_live = (jnp.arange(total_rows) < row_limit)[:, None]
    active_cotangent = jnp.where(row_live, cotangent, jnp.zeros_like(cotangent))
    head_gradient = active_cotangent.reshape(total_rows, KEY_VALUE_HEADS, group_width, HEAD_SIZE)
    scaling = 1.0 / math.sqrt(HEAD_SIZE)
    prob_grad = jnp.einsum(
        "lhgd,nhd->hgln", head_gradient, heads_of_values, preferred_element_type=jnp.float32
    )
    row_dot = jnp.sum(weights * prob_grad, axis=-1, keepdims=True)
    score_grad = (weights * (prob_grad - row_dot) * scaling).astype(jnp.bfloat16)
    query_gradient = jnp.einsum(
        "hgln,nhd->lhgd", score_grad, heads_of_keys, preferred_element_type=jnp.float32
    ).astype(jnp.bfloat16)
    key_gradient = jnp.einsum(
        "hgln,lhgd->nhd", score_grad, heads_of_queries, preferred_element_type=jnp.float32
    ).astype(jnp.bfloat16)
    return (
        query_gradient.reshape(total_rows, QUERY_HEADS * HEAD_SIZE),
        key_gradient.reshape(total_keys, KEY_VALUE_HEADS * HEAD_SIZE),
    )


def exchange_kernel(n, scatter, x_ref, o_ref, send_sems, recv_sems, local_sem):
    me = lax.axis_index("section")
    row = lax.axis_index("dp")
    barrier = pltpu.get_barrier_semaphore()
    for k in range(1, n):
        pl.semaphore_signal(
            barrier, inc=1, device_id=(lax.rem(me + k, n), row), device_id_type=MESH_ID
        )
    pl.semaphore_wait(barrier, n - 1)
    own = x_ref.at[:, me] if scatter else x_ref
    local = pltpu.make_async_copy(own, o_ref.at[:, me], local_sem)
    local.start()
    copies = []
    for k in range(1, n):
        peer = lax.rem(me + k, n)
        src = x_ref.at[:, peer] if scatter else x_ref
        copy = pltpu.make_async_remote_copy(
            src_ref=src,
            dst_ref=o_ref.at[:, me],
            send_sem=send_sems.at[k],
            recv_sem=recv_sems.at[k],
            device_id=(peer, row),
            device_id_type=MESH_ID,
        )
        copy.start()
        copies.append(copy)
    for copy in copies:
        copy.wait()
    local.wait()


def relay_gather_kernel(x_ref, o_ref, stage, local_sem, direct_send, direct_recv,
                        hop_send, hop_recv, fwd_send, fwd_recv):
    s = lax.axis_index("section")
    r = lax.axis_index("dp")
    y = lax.rem(s, 4)
    z = (s // 4) * 2 + r // 8
    xc = lax.rem(r, 8)
    half = x_ref.shape[-1] // 2

    def sec(zz, yy):
        return (lax.rem(zz, 4) // 2) * 4 + yy

    def dpi(zz):
        return lax.rem(zz, 2) * 8 + xc

    up, down = z + 1, z + 3
    peers = [(sec(z, lax.rem(y + j, 4)), r) for j in range(1, 4)]
    for yy in range(4):
        peers.append((sec(up, yy), dpi(up)))
        peers.append((sec(down, yy), dpi(down)))
    barrier = pltpu.get_barrier_semaphore()
    for peer in peers:
        pl.semaphore_signal(barrier, inc=1, device_id=peer, device_id_type=MESH_ID)
    pl.semaphore_wait(barrier, len(peers))

    local = pltpu.make_async_copy(x_ref, o_ref.at[:, s], local_sem)
    local.start()
    sends = []
    for j in range(1, 4):
        copy = pltpu.make_async_remote_copy(
            src_ref=x_ref,
            dst_ref=o_ref.at[:, s],
            send_sem=direct_send.at[j],
            recv_sem=direct_recv.at[j],
            device_id=peers[j - 1],
            device_id_type=MESH_ID,
        )
        copy.start()
        sends.append(copy)
    hops = []
    for side, (target, lanes) in enumerate(((up, pl.ds(0, half)), (down, pl.ds(half, half)))):
        copy = pltpu.make_async_remote_copy(
            src_ref=x_ref.at[:, :, lanes],
            dst_ref=stage.at[side],
            send_sem=hop_send.at[side],
            recv_sem=hop_recv.at[side],
            device_id=(sec(target, y), dpi(target)),
            device_id_type=MESH_ID,
        )
        copy.start()
        hops.append(copy)
    forwards = []
    for side, (origin, target, lanes) in enumerate(
        ((down, up, pl.ds(0, half)), (up, down, pl.ds(half, half)))
    ):
        hops[side].wait_recv()
        for yy in range(4):
            copy = pltpu.make_async_remote_copy(
                src_ref=stage.at[side],
                dst_ref=o_ref.at[:, sec(origin, y), :, lanes],
                send_sem=fwd_send.at[side, yy],
                recv_sem=fwd_recv.at[side, y],
                device_id=(sec(target, yy), dpi(target)),
                device_id_type=MESH_ID,
            )
            copy.start()
            forwards.append(copy)
    for copy in sends:
        copy.wait()
    for copy in hops:
        copy.wait_send()
    for copy in forwards:
        copy.wait_send()
    for side, (origin, target, lanes) in enumerate(
        ((down, up, pl.ds(0, half)), (up, down, pl.ds(half, half)))
    ):
        for yy in range(4):
            pltpu.make_async_remote_copy(
                src_ref=stage.at[side],
                dst_ref=o_ref.at[:, sec(origin, y), :, lanes],
                send_sem=fwd_send.at[side, yy],
                recv_sem=fwd_recv.at[side, yy],
                device_id=(sec(target, yy), dpi(target)),
                device_id_type=MESH_ID,
            ).wait_recv()
    local.wait()


def relay_gather(x, n):
    samples, chunk, width = x.shape
    return pl.pallas_call(
        relay_gather_kernel,
        out_shape=jax.ShapeDtypeStruct((samples, n, chunk, width), x.dtype),
        in_specs=[pl.BlockSpec(memory_space=pl.ANY)],
        out_specs=pl.BlockSpec(memory_space=pl.ANY),
        scratch_shapes=[
            pltpu.VMEM((2, samples, chunk, width // 2), x.dtype),
            pltpu.SemaphoreType.DMA(()),
            pltpu.SemaphoreType.DMA((4,)),
            pltpu.SemaphoreType.DMA((4,)),
            pltpu.SemaphoreType.DMA((2,)),
            pltpu.SemaphoreType.DMA((2,)),
            pltpu.SemaphoreType.DMA((2, 4)),
            pltpu.SemaphoreType.DMA((2, 4)),
        ],
        compiler_params=pltpu.CompilerParams(collective_id=2, has_side_effects=True),
    )(x)


def exchange(x, n, scatter, collective_id):
    if scatter:
        out_shape = x.shape
    else:
        out_shape = (x.shape[0], n) + x.shape[1:]
    return pl.pallas_call(
        functools.partial(exchange_kernel, n, scatter),
        out_shape=jax.ShapeDtypeStruct(out_shape, x.dtype),
        in_specs=[pl.BlockSpec(memory_space=pl.ANY)],
        out_specs=pl.BlockSpec(memory_space=pl.ANY),
        scratch_shapes=[
            pltpu.SemaphoreType.DMA((n,)),
            pltpu.SemaphoreType.DMA((n,)),
            pltpu.SemaphoreType.DMA(()),
        ],
        compiler_params=pltpu.CompilerParams(collective_id=collective_id, has_side_effects=True),
    )(x)


def image_kernel(n, tiles, g_ref, wk_hbm, wv_hbm, o_ref, buf, recv, acc, wk_ref, wv_ref,
                 weight_sems, send_sems, recv_sems):
    me = lax.axis_index("section")
    row = lax.axis_index("dp")
    rows = g_ref.shape[0] // n
    half = g_ref.shape[1] // 2
    tile_w = wk_ref.shape[0] // tiles

    def weight_copies(t):
        part = pl.ds(pl.multiple_of(t * tile_w, tile_w), tile_w)
        return [
            pltpu.make_async_copy(src.at[part], dst.at[part], weight_sems.at[i, t])
            for i, (src, dst) in enumerate(((wk_hbm, wk_ref), (wv_hbm, wv_ref)))
        ]

    for t in range(tiles):
        for copy in weight_copies(t):
            copy.start()
    barrier = pltpu.get_barrier_semaphore()
    for k in range(1, n):
        pl.semaphore_signal(
            barrier, inc=1, device_id=(lax.rem(me + k, n), row), device_id_type=MESH_ID
        )
    pl.semaphore_wait(barrier, n - 1)

    def compute(t):
        for copy in weight_copies(t):
            copy.wait()
        cols = pl.ds(pl.multiple_of(t * tile_w, tile_w), tile_w)
        dims = (((1,), (1,)), ((), ()))
        acc = lax.dot_general(
            g_ref[:, pl.ds(0, half)], wk_ref[cols, :], dims, preferred_element_type=jnp.float32
        )
        acc = acc + lax.dot_general(
            g_ref[:, pl.ds(half, half)], wv_ref[cols, :], dims, preferred_element_type=jnp.float32
        )
        buf[:, cols] = acc.astype(buf.dtype)

    def send(t):
        cols = pl.ds(pl.multiple_of(t * tile_w, tile_w), tile_w)
        for k in range(1, n):
            peer = lax.rem(me + k, n)
            pltpu.make_async_remote_copy(
                src_ref=buf.at[pl.ds(pl.multiple_of(peer * rows, 16), rows), cols],
                dst_ref=recv.at[me, :, cols],
                send_sem=send_sems.at[k],
                recv_sem=recv_sems.at[k],
                device_id=(peer, row),
                device_id_type=MESH_ID,
            ).start()

    compute(0)

    def body(t, carry):
        compute(t)
        send(t - 1)
        return carry

    lax.fori_loop(1, tiles, body, 0)
    send(tiles - 1)
    own = pl.ds(pl.multiple_of(me * rows, 16), rows)
    acc[...] = buf[own, :].astype(jnp.float32)
    for k in range(1, n):
        peer = lax.rem(me + k, n)
        whole = pltpu.make_async_remote_copy(
            src_ref=buf.at[pl.ds(pl.multiple_of(peer * rows, 16), rows), :],
            dst_ref=recv.at[me],
            send_sem=send_sems.at[k],
            recv_sem=recv_sems.at[k],
            device_id=(peer, row),
            device_id_type=MESH_ID,
        )
        whole.wait_recv()
        acc[...] += recv[lax.rem(me + n - k, n)].astype(jnp.float32)
        whole.wait_send()
    o_ref[...] = acc[...].astype(o_ref.dtype)


def image_exchange(g, w_key, w_value, n):
    total_rows, kv = g.shape
    width = w_key.shape[0]
    tiles = 8
    return pl.pallas_call(
        functools.partial(image_kernel, n, tiles),
        out_shape=jax.ShapeDtypeStruct((total_rows // n, width), jnp.bfloat16),
        in_specs=[
            pl.BlockSpec(memory_space=pltpu.VMEM),
            pl.BlockSpec(memory_space=pl.ANY),
            pl.BlockSpec(memory_space=pl.ANY),
        ],
        out_specs=pl.BlockSpec(memory_space=pltpu.VMEM),
        scratch_shapes=[
            pltpu.VMEM((total_rows, width), jnp.bfloat16),
            pltpu.VMEM((n, total_rows // n, width), jnp.bfloat16),
            pltpu.VMEM((total_rows // n, width), jnp.float32),
            pltpu.VMEM(w_key.shape, w_key.dtype),
            pltpu.VMEM(w_value.shape, w_value.dtype),
            pltpu.SemaphoreType.DMA((2, tiles)),
            pltpu.SemaphoreType.DMA((n,)),
            pltpu.SemaphoreType.DMA((n,)),
        ],
        compiler_params=pltpu.CompilerParams(
            collective_id=3, has_side_effects=True, vmem_limit_bytes=60 * 1024 * 1024
        ),
        cost_estimate=pl.CostEstimate(
            flops=2 * total_rows * kv * width, bytes_accessed=2 * (kv + total_rows) * width,
            transcendentals=0,
        ),
    )(g, w_key, w_value)


def shards(queries, image_tokens, key_weight, value_weight, cotangent, tile_counts, text_lengths):
    n_section = lax.axis_size("section")
    samples_here, chunk, model_width = image_tokens.shape
    image_len = n_section * chunk
    tile_len = image_len // MAX_TILES
    w_key = key_weight[0]
    w_value = value_weight[0]
    query_local = queries[0]
    cotan_local = cotangent[0]
    late = [
        lax.all_gather(image_tokens[i], "section", axis=0, tiled=True)
        for i in range(1, samples_here)
    ]
    if n_section == 8 and lax.axis_size("dp") == 16:
        first = relay_gather(image_tokens[:1], n_section)
    else:
        first = exchange(image_tokens[:1], n_section, False, 0)
    token_list = [first.reshape(image_len, model_width)] + late
    keys_list = []
    values_list = []
    for sample_index in range(samples_here):
        tokens = token_list[sample_index]
        keys_list.append(
            jnp.dot(tokens, w_key, preferred_element_type=jnp.float32).astype(jnp.bfloat16)
        )
        values_list.append(
            jnp.dot(tokens, w_value, preferred_element_type=jnp.float32).astype(jnp.bfloat16)
        )
        if sample_index + 1 < samples_here:
            values_list[-1], token_list[sample_index + 1] = lax.optimization_barrier(
                (values_list[-1], token_list[sample_index + 1])
            )
    keys_both = jnp.stack(keys_list)
    values_both = jnp.stack(values_list)
    key_limits = tile_counts * tile_len
    weights, value_grads = jax.vmap(attend_front)(
        query_local, keys_both, cotan_local, key_limits, text_lengths
    )
    all_tokens = jnp.concatenate(token_list, axis=0)
    value_term = jnp.einsum(
        "td,tk->dk", all_tokens, value_grads.reshape(samples_here * image_len, -1),
        preferred_element_type=jnp.float32,
    ).astype(jnp.bfloat16)
    value_term, weights = lax.optimization_barrier((value_term, weights))
    value_sum = lax.psum_scatter(value_term, "dp", scatter_dimension=0, tiled=True)
    query_grads, key_grads = jax.vmap(attend_back)(
        query_local, keys_both, values_both, cotan_local, text_lengths, weights
    )
    key_term = jnp.einsum(
        "td,tk->dk", all_tokens, key_grads.reshape(samples_here * image_len, -1),
        preferred_element_type=jnp.float32,
    ).astype(jnp.bfloat16)
    key_sum = lax.psum_scatter(key_term, "dp", scatter_dimension=0, tiled=True)
    query_out = query_grads[None]
    kv_grads = jnp.concatenate([key_grads, value_grads], axis=-1)
    by_slot = kv_grads.reshape(samples_here, n_section, chunk, -1).transpose(1, 0, 2, 3)
    received = image_exchange(
        by_slot.reshape(n_section * samples_here * chunk, -1), w_key, w_value, n_section
    )
    image_out = received.reshape(samples_here, chunk, model_width)
    return (
        query_out,
        image_out,
        key_sum[None],
        value_sum[None],
    )


def solution(mesh):
    placed = (
        P("section", "dp", None, None),
        P("dp", "section", None),
        P("section", None, None),
        P("section", None, None),
        P("section", "dp", None, None),
        P("dp"),
        P("dp"),
    )
    return jax.shard_map(
        shards,
        mesh=mesh,
        in_specs=placed,
        out_specs=(
            P("section", "dp", None, None),
            P("dp", "section", None),
            P("section", "dp", None),
            P("section", "dp", None),
        ),
        check_vma=False,
    )
```

```python
import functools
import math

import jax
import jax.numpy as jnp
from jax import lax
from jax.experimental import pallas as pl
from jax.experimental.pallas import tpu as pltpu
from jax.sharding import PartitionSpec as P

QUERY_HEADS = 32
KEY_VALUE_HEADS = 4
HEAD_SIZE = 128
MAX_TILES = 4
MESH_ID = pl.DeviceIdType.MESH


def attend_one(queries, key_rows, value_rows, cotangent, key_limit, row_limit):
    total_rows = queries.shape[0]
    total_keys = key_rows.shape[0]
    group_width = QUERY_HEADS // KEY_VALUE_HEADS
    heads_of_queries = queries.reshape(total_rows, KEY_VALUE_HEADS, group_width, HEAD_SIZE)
    heads_of_keys = key_rows.reshape(total_keys, KEY_VALUE_HEADS, HEAD_SIZE)
    heads_of_values = value_rows.reshape(total_keys, KEY_VALUE_HEADS, HEAD_SIZE)
    row_live = (jnp.arange(total_rows) < row_limit)[:, None]
    active_cotangent = jnp.where(row_live, cotangent, jnp.zeros_like(cotangent))
    head_gradient = active_cotangent.reshape(total_rows, KEY_VALUE_HEADS, group_width, HEAD_SIZE)
    scaling = 1.0 / math.sqrt(HEAD_SIZE)
    scores = (
        jnp.einsum(
            "lhgd,nhd->hgln", heads_of_queries, heads_of_keys, preferred_element_type=jnp.float32
        )
        * scaling
    )
    key_live = jnp.arange(total_keys) < key_limit
    scores = jnp.where(key_live, scores, -jnp.inf)
    row_max = jnp.max(scores, axis=-1, keepdims=True)
    raised = jnp.exp(scores - row_max)
    weights = raised / jnp.sum(raised, axis=-1, keepdims=True)
    weights_low = weights.astype(jnp.bfloat16)
    value_gradient = jnp.einsum(
        "hgln,lhgd->nhd", weights_low, head_gradient, preferred_element_type=jnp.float32
    ).astype(jnp.bfloat16)
    prob_grad = jnp.einsum(
        "lhgd,nhd->hgln", head_gradient, heads_of_values, preferred_element_type=jnp.float32
    )
    row_dot = jnp.sum(weights * prob_grad, axis=-1, keepdims=True)
    score_grad = (weights * (prob_grad - row_dot) * scaling).astype(jnp.bfloat16)
    query_gradient = jnp.einsum(
        "hgln,nhd->lhgd", score_grad, heads_of_keys, preferred_element_type=jnp.float32
    ).astype(jnp.bfloat16)
    key_gradient = jnp.einsum(
        "hgln,lhgd->nhd", score_grad, heads_of_queries, preferred_element_type=jnp.float32
    ).astype(jnp.bfloat16)
    return (
        query_gradient.reshape(total_rows, QUERY_HEADS * HEAD_SIZE),
        key_gradient.reshape(total_keys, KEY_VALUE_HEADS * HEAD_SIZE),
        value_gradient.reshape(total_keys, KEY_VALUE_HEADS * HEAD_SIZE),
    )


def attend_front(queries, key_rows, cotangent, key_limit, row_limit):
    total_rows = queries.shape[0]
    total_keys = key_rows.shape[0]
    group_width = QUERY_HEADS // KEY_VALUE_HEADS
    heads_of_queries = queries.reshape(total_rows, KEY_VALUE_HEADS, group_width, HEAD_SIZE)
    heads_of_keys = key_rows.reshape(total_keys, KEY_VALUE_HEADS, HEAD_SIZE)
    row_live = (jnp.arange(total_rows) < row_limit)[:, None]
    active_cotangent = jnp.where(row_live, cotangent, jnp.zeros_like(cotangent))
    head_gradient = active_cotangent.reshape(total_rows, KEY_VALUE_HEADS, group_width, HEAD_SIZE)
    scaling = 1.0 / math.sqrt(HEAD_SIZE)
    scores = (
        jnp.einsum(
            "lhgd,nhd->hgln", heads_of_queries, heads_of_keys, preferred_element_type=jnp.float32
        )
        * scaling
    )
    key_live = jnp.arange(total_keys) < key_limit
    scores = jnp.where(key_live, scores, -jnp.inf)
    row_max = jnp.max(scores, axis=-1, keepdims=True)
    raised = jnp.exp(scores - row_max)
    weights = raised / jnp.sum(raised, axis=-1, keepdims=True)
    weights_low = weights.astype(jnp.bfloat16)
    value_gradient = jnp.einsum(
        "hgln,lhgd->nhd", weights_low, head_gradient, preferred_element_type=jnp.float32
    ).astype(jnp.bfloat16)
    return weights, value_gradient.reshape(total_keys, KEY_VALUE_HEADS * HEAD_SIZE)


def attend_back(queries, key_rows, value_rows, cotangent, row_limit, weights):
    total_rows = queries.shape[0]
    total_keys = key_rows.shape[0]
    group_width = QUERY_HEADS // KEY_VALUE_HEADS
    heads_of_queries = queries.reshape(total_rows, KEY_VALUE_HEADS, group_width, HEAD_SIZE)
    heads_of_keys = key_rows.reshape(total_keys, KEY_VALUE_HEADS, HEAD_SIZE)
    heads_of_values = value_rows.reshape(total_keys, KEY_VALUE_HEADS, HEAD_SIZE)
    row_live = (jnp.arange(total_rows) < row_limit)[:, None]
    active_cotangent = jnp.where(row_live, cotangent, jnp.zeros_like(cotangent))
    head_gradient = active_cotangent.reshape(total_rows, KEY_VALUE_HEADS, group_width, HEAD_SIZE)
    scaling = 1.0 / math.sqrt(HEAD_SIZE)
    prob_grad = jnp.einsum(
        "lhgd,nhd->hgln", head_gradient, heads_of_values, preferred_element_type=jnp.float32
    )
    row_dot = jnp.sum(weights * prob_grad, axis=-1, keepdims=True)
    score_grad = (weights * (prob_grad - row_dot) * scaling).astype(jnp.bfloat16)
    query_gradient = jnp.einsum(
        "hgln,nhd->lhgd", score_grad, heads_of_keys, preferred_element_type=jnp.float32
    ).astype(jnp.bfloat16)
    key_gradient = jnp.einsum(
        "hgln,lhgd->nhd", score_grad, heads_of_queries, preferred_element_type=jnp.float32
    ).astype(jnp.bfloat16)
    return (
        query_gradient.reshape(total_rows, QUERY_HEADS * HEAD_SIZE),
        key_gradient.reshape(total_keys, KEY_VALUE_HEADS * HEAD_SIZE),
    )


def exchange_kernel(n, scatter, x_ref, o_ref, send_sems, recv_sems, local_sem):
    me = lax.axis_index("section")
    row = lax.axis_index("dp")
    barrier = pltpu.get_barrier_semaphore()
    for k in range(1, n):
        pl.semaphore_signal(
            barrier, inc=1, device_id=(lax.rem(me + k, n), row), device_id_type=MESH_ID
        )
    pl.semaphore_wait(barrier, n - 1)
    own = x_ref.at[:, me] if scatter else x_ref
    local = pltpu.make_async_copy(own, o_ref.at[:, me], local_sem)
    local.start()
    copies = []
    for k in range(1, n):
        peer = lax.rem(me + k, n)
        src = x_ref.at[:, peer] if scatter else x_ref
        copy = pltpu.make_async_remote_copy(
            src_ref=src,
            dst_ref=o_ref.at[:, me],
            send_sem=send_sems.at[k],
            recv_sem=recv_sems.at[k],
            device_id=(peer, row),
            device_id_type=MESH_ID,
        )
        copy.start()
        copies.append(copy)
    for copy in copies:
        copy.wait()
    local.wait()


def relay_gather_kernel(x_ref, o_ref, stage, local_sem, direct_send, direct_recv,
                        hop_send, hop_recv, fwd_send, fwd_recv):
    s = lax.axis_index("section")
    r = lax.axis_index("dp")
    y = lax.rem(s, 4)
    z = (s // 4) * 2 + r // 8
    xc = lax.rem(r, 8)
    half = x_ref.shape[-1] // 2

    def sec(zz, yy):
        return (lax.rem(zz, 4) // 2) * 4 + yy

    def dpi(zz):
        return lax.rem(zz, 2) * 8 + xc

    up, down = z + 1, z + 3
    peers = [(sec(z, lax.rem(y + j, 4)), r) for j in range(1, 4)]
    for yy in range(4):
        peers.append((sec(up, yy), dpi(up)))
        peers.append((sec(down, yy), dpi(down)))
    barrier = pltpu.get_barrier_semaphore()
    for peer in peers:
        pl.semaphore_signal(barrier, inc=1, device_id=peer, device_id_type=MESH_ID)
    pl.semaphore_wait(barrier, len(peers))

    local = pltpu.make_async_copy(x_ref, o_ref.at[:, s], local_sem)
    local.start()
    sends = []
    for j in range(1, 4):
        copy = pltpu.make_async_remote_copy(
            src_ref=x_ref,
            dst_ref=o_ref.at[:, s],
            send_sem=direct_send.at[j],
            recv_sem=direct_recv.at[j],
            device_id=peers[j - 1],
            device_id_type=MESH_ID,
        )
        copy.start()
        sends.append(copy)
    hops = []
    for side, (target, lanes) in enumerate(((up, pl.ds(0, half)), (down, pl.ds(half, half)))):
        copy = pltpu.make_async_remote_copy(
            src_ref=x_ref.at[:, :, lanes],
            dst_ref=stage.at[side],
            send_sem=hop_send.at[side],
            recv_sem=hop_recv.at[side],
            device_id=(sec(target, y), dpi(target)),
            device_id_type=MESH_ID,
        )
        copy.start()
        hops.append(copy)
    forwards = []
    for side, (origin, target, lanes) in enumerate(
        ((down, up, pl.ds(0, half)), (up, down, pl.ds(half, half)))
    ):
        hops[side].wait_recv()
        for yy in range(4):
            copy = pltpu.make_async_remote_copy(
                src_ref=stage.at[side],
                dst_ref=o_ref.at[:, sec(origin, y), :, lanes],
                send_sem=fwd_send.at[side, yy],
                recv_sem=fwd_recv.at[side, y],
                device_id=(sec(target, yy), dpi(target)),
                device_id_type=MESH_ID,
            )
            copy.start()
            forwards.append(copy)
    for copy in sends:
        copy.wait()
    for copy in hops:
        copy.wait_send()
    for copy in forwards:
        copy.wait_send()
    for side, (origin, target, lanes) in enumerate(
        ((down, up, pl.ds(0, half)), (up, down, pl.ds(half, half)))
    ):
        for yy in range(4):
            pltpu.make_async_remote_copy(
                src_ref=stage.at[side],
                dst_ref=o_ref.at[:, sec(origin, y), :, lanes],
                send_sem=fwd_send.at[side, yy],
                recv_sem=fwd_recv.at[side, yy],
                device_id=(sec(target, yy), dpi(target)),
                device_id_type=MESH_ID,
            ).wait_recv()
    local.wait()


def relay_gather(x, n):
    samples, chunk, width = x.shape
    return pl.pallas_call(
        relay_gather_kernel,
        out_shape=jax.ShapeDtypeStruct((samples, n, chunk, width), x.dtype),
        in_specs=[pl.BlockSpec(memory_space=pl.ANY)],
        out_specs=pl.BlockSpec(memory_space=pl.ANY),
        scratch_shapes=[
            pltpu.VMEM((2, samples, chunk, width // 2), x.dtype),
            pltpu.SemaphoreType.DMA(()),
            pltpu.SemaphoreType.DMA((4,)),
            pltpu.SemaphoreType.DMA((4,)),
            pltpu.SemaphoreType.DMA((2,)),
            pltpu.SemaphoreType.DMA((2,)),
            pltpu.SemaphoreType.DMA((2, 4)),
            pltpu.SemaphoreType.DMA((2, 4)),
        ],
        compiler_params=pltpu.CompilerParams(collective_id=2, has_side_effects=True),
    )(x)


def exchange(x, n, scatter, collective_id):
    if scatter:
        out_shape = x.shape
    else:
        out_shape = (x.shape[0], n) + x.shape[1:]
    return pl.pallas_call(
        functools.partial(exchange_kernel, n, scatter),
        out_shape=jax.ShapeDtypeStruct(out_shape, x.dtype),
        in_specs=[pl.BlockSpec(memory_space=pl.ANY)],
        out_specs=pl.BlockSpec(memory_space=pl.ANY),
        scratch_shapes=[
            pltpu.SemaphoreType.DMA((n,)),
            pltpu.SemaphoreType.DMA((n,)),
            pltpu.SemaphoreType.DMA(()),
        ],
        compiler_params=pltpu.CompilerParams(collective_id=collective_id, has_side_effects=True),
    )(x)


def image_kernel(n, tiles, g_ref, wk_hbm, wv_hbm, o_ref, buf, recv, acc, wk_ref, wv_ref,
                 weight_sems, send_sems, recv_sems):
    me = lax.axis_index("section")
    row = lax.axis_index("dp")
    rows = g_ref.shape[0] // n
    half = g_ref.shape[1] // 2
    tile_w = wk_ref.shape[0] // tiles

    def weight_copies(t):
        part = pl.ds(pl.multiple_of(t * tile_w, tile_w), tile_w)
        return [
            pltpu.make_async_copy(src.at[part], dst.at[part], weight_sems.at[i, t])
            for i, (src, dst) in enumerate(((wk_hbm, wk_ref), (wv_hbm, wv_ref)))
        ]

    for t in range(tiles):
        for copy in weight_copies(t):
            copy.start()
    barrier = pltpu.get_barrier_semaphore()
    for k in range(1, n):
        pl.semaphore_signal(
            barrier, inc=1, device_id=(lax.rem(me + k, n), row), device_id_type=MESH_ID
        )
    pl.semaphore_wait(barrier, n - 1)

    def compute(t):
        for copy in weight_copies(t):
            copy.wait()
        cols = pl.ds(pl.multiple_of(t * tile_w, tile_w), tile_w)
        dims = (((1,), (1,)), ((), ()))
        acc = lax.dot_general(
            g_ref[:, pl.ds(0, half)], wk_ref[cols, :], dims, preferred_element_type=jnp.float32
        )
        acc = acc + lax.dot_general(
            g_ref[:, pl.ds(half, half)], wv_ref[cols, :], dims, preferred_element_type=jnp.float32
        )
        buf[:, cols] = acc.astype(buf.dtype)

    def send(t):
        cols = pl.ds(pl.multiple_of(t * tile_w, tile_w), tile_w)
        for k in range(1, n):
            peer = lax.rem(me + k, n)
            pltpu.make_async_remote_copy(
                src_ref=buf.at[pl.ds(pl.multiple_of(peer * rows, 16), rows), cols],
                dst_ref=recv.at[me, :, cols],
                send_sem=send_sems.at[k],
                recv_sem=recv_sems.at[k],
                device_id=(peer, row),
                device_id_type=MESH_ID,
            ).start()

    compute(0)

    def body(t, carry):
        compute(t)
        send(t - 1)
        return carry

    lax.fori_loop(1, tiles, body, 0)
    send(tiles - 1)
    own = pl.ds(pl.multiple_of(me * rows, 16), rows)
    acc[...] = buf[own, :].astype(jnp.float32)
    for k in range(1, n):
        peer = lax.rem(me + k, n)
        whole = pltpu.make_async_remote_copy(
            src_ref=buf.at[pl.ds(pl.multiple_of(peer * rows, 16), rows), :],
            dst_ref=recv.at[me],
            send_sem=send_sems.at[k],
            recv_sem=recv_sems.at[k],
            device_id=(peer, row),
            device_id_type=MESH_ID,
        )
        whole.wait_recv()
        acc[...] += recv[lax.rem(me + n - k, n)].astype(jnp.float32)
        whole.wait_send()
    o_ref[...] = acc[...].astype(o_ref.dtype)


def image_exchange(g, w_key, w_value, n):
    total_rows, kv = g.shape
    width = w_key.shape[0]
    tiles = 8
    return pl.pallas_call(
        functools.partial(image_kernel, n, tiles),
        out_shape=jax.ShapeDtypeStruct((total_rows // n, width), jnp.bfloat16),
        in_specs=[
            pl.BlockSpec(memory_space=pltpu.VMEM),
            pl.BlockSpec(memory_space=pl.ANY),
            pl.BlockSpec(memory_space=pl.ANY),
        ],
        out_specs=pl.BlockSpec(memory_space=pltpu.VMEM),
        scratch_shapes=[
            pltpu.VMEM((total_rows, width), jnp.bfloat16),
            pltpu.VMEM((n, total_rows // n, width), jnp.bfloat16),
            pltpu.VMEM((total_rows // n, width), jnp.float32),
            pltpu.VMEM(w_key.shape, w_key.dtype),
            pltpu.VMEM(w_value.shape, w_value.dtype),
            pltpu.SemaphoreType.DMA((2, tiles)),
            pltpu.SemaphoreType.DMA((n,)),
            pltpu.SemaphoreType.DMA((n,)),
        ],
        compiler_params=pltpu.CompilerParams(
            collective_id=3, has_side_effects=True, vmem_limit_bytes=60 * 1024 * 1024
        ),
        cost_estimate=pl.CostEstimate(
            flops=2 * total_rows * kv * width, bytes_accessed=2 * (kv + total_rows) * width,
            transcendentals=0,
        ),
    )(g, w_key, w_value)


def shards(queries, image_tokens, key_weight, value_weight, cotangent, tile_counts, text_lengths):
    n_section = lax.axis_size("section")
    samples_here, chunk, model_width = image_tokens.shape
    image_len = n_section * chunk
    tile_len = image_len // MAX_TILES
    w_key = key_weight[0]
    w_value = value_weight[0]
    query_local = queries[0]
    cotan_local = cotangent[0]
    late = [
        lax.all_gather(image_tokens[i], "section", axis=0, tiled=True)
        for i in range(1, samples_here)
    ]
    if n_section == 8 and lax.axis_size("dp") == 16:
        first = relay_gather(image_tokens[:1], n_section)
    else:
        first = exchange(image_tokens[:1], n_section, False, 0)
    token_list = [first.reshape(image_len, model_width)] + late
    keys_list = []
    values_list = []
    weight_list = []
    value_grad_list = []
    key_limits = tile_counts * tile_len
    for sample_index in range(samples_here):
        tokens = token_list[sample_index]
        keys_list.append(
            jnp.dot(tokens, w_key, preferred_element_type=jnp.float32).astype(jnp.bfloat16)
        )
        values_list.append(
            jnp.dot(tokens, w_value, preferred_element_type=jnp.float32).astype(jnp.bfloat16)
        )
        weights_here, value_grad_here = attend_front(
            query_local[sample_index],
            keys_list[-1],
            cotan_local[sample_index],
            key_limits[sample_index],
            text_lengths[sample_index],
        )
        if sample_index + 1 < samples_here:
            values_list[-1], weights_here, value_grad_here, token_list[sample_index + 1] = (
                lax.optimization_barrier(
                    (values_list[-1], weights_here, value_grad_here, token_list[sample_index + 1])
                )
            )
        weight_list.append(weights_here)
        value_grad_list.append(value_grad_here)
    keys_both = jnp.stack(keys_list)
    values_both = jnp.stack(values_list)
    weights = jnp.stack(weight_list)
    value_grads = jnp.stack(value_grad_list)
    all_tokens = jnp.concatenate(token_list, axis=0)
    value_term = jnp.einsum(
        "td,tk->dk", all_tokens, value_grads.reshape(samples_here * image_len, -1),
        preferred_element_type=jnp.float32,
    ).astype(jnp.bfloat16)
    value_term, weights = lax.optimization_barrier((value_term, weights))
    value_sum = lax.psum_scatter(value_term, "dp", scatter_dimension=0, tiled=True)
    query_grads, key_grads = jax.vmap(attend_back)(
        query_local, keys_both, values_both, cotan_local, text_lengths, weights
    )
    key_term = jnp.einsum(
        "td,tk->dk", all_tokens, key_grads.reshape(samples_here * image_len, -1),
        preferred_element_type=jnp.float32,
    ).astype(jnp.bfloat16)
    key_sum = lax.psum_scatter(key_term, "dp", scatter_dimension=0, tiled=True)
    query_out = query_grads[None]
    kv_grads = jnp.concatenate([key_grads, value_grads], axis=-1)
    by_slot = kv_grads.reshape(samples_here, n_section, chunk, -1).transpose(1, 0, 2, 3)
    received = image_exchange(
        by_slot.reshape(n_section * samples_here * chunk, -1), w_key, w_value, n_section
    )
    image_out = received.reshape(samples_here, chunk, model_width)
    return (
        query_out,
        image_out,
        key_sum[None],
        value_sum[None],
    )


def solution(mesh):
    placed = (
        P("section", "dp", None, None),
        P("dp", "section", None),
        P("section", None, None),
        P("section", None, None),
        P("section", "dp", None, None),
        P("dp"),
        P("dp"),
    )
    return jax.shard_map(
        shards,
        mesh=mesh,
        in_specs=placed,
        out_specs=(
            P("section", "dp", None, None),
            P("dp", "section", None),
            P("section", "dp", None),
            P("section", "dp", None),
        ),
        check_vma=False,
    )
```
